128 devices in a mesh: row: 8 (over x, core), col: 16 (over y, z).
Axes of the slice: x: 4, y: 4, z: 4, core: 2. Of those that a mesh axis runs over, the one named last changes fastest.
Arguments:
- pair: float32 [1024, 1024, 128], P('row', 'col'), may hold values from -6 to 6
- logit_cotangent: bfloat16 [1024, 1024, 64], P('row', 'col'), may hold values from -6 to 6
- tiles: bfloat16 [2048, 1024, 64], P(('row', 'col')), may hold values from -6 to 6
- tile_target: int32 [2048, 1], P(('row', 'col')), may hold values from 0 to 15; in each aligned block of 16 rows (0 to 15, 16 to 31, ...) at most 2 rows name the same one
- tile_square: int32 [2048], P(('row', 'col')), may hold values from 0 to 7
- tile_count: int32 [2048], P(('row', 'col')), may hold values from 1 to 4
- w_template: bfloat16 [64, 128], replicated, may hold values from -0.75 to 0.75
- transition_norm_gain: float32 [128], replicated, may hold values from 0.1 to 1.9
- transition_norm_bias: float32 [128], replicated, may hold values from -3 to 3
- w_gate: bfloat16 [128, 512], replicated, may hold values from -0.5 to 0.5
- w_up: bfloat16 [128, 512], replicated, may hold values from -0.5 to 0.5
- w_out: bfloat16 [512, 128], replicated, may hold values from -0.25 to 0.25
- w_dist: bfloat16 [128, 64], replicated, may hold values from -0.5 to 0.5
Outputs:
- logits: bfloat16 [1024, 1024, 64], P('row', 'col')
- grad_pair: float32 [1024, 1024, 128], P('row', 'col')
- grad_tiles: bfloat16 [2048, 1024, 64], P(('row', 'col'))
- grad_template: float32 [64, 128], replicated
- grad_gain: float32 [128], replicated
- grad_bias: float32 [128], replicated
- grad_gate: float32 [128, 512], replicated
- grad_up: float32 [128, 512], replicated
- grad_out: float32 [512, 128], replicated
- grad_dist: float32 [128, 64], replicated
The draws below stay inside these ranges and needn't reach their ends.
Inputs may be any that keep to these rules, and one draw needn't show every extreme that they name: `tile_target`: among the 16 tiles of one device no column device is named more than 2 times; some device names one exactly 2 times.
All inputs are finite; a program needn't handle non-finite values.
Results may differ from the reference program's by a relative error of at most 0.0079.
Values may be sent and summed in bfloat16 or wider, within the bound.
A program may use at most 128 MiB of HBM per device.

```python
import math
import jax
import jax.numpy as jnp
import numpy as np
from jax import lax

C = 128
TW = 64
HID = 512
BINS = 64
SQ = 32
SLOTS = 16
CAP = 2
ROW_DEV = 128
CROP = 1024
COL_DEV = 64
SQ_DEV = 8
TILES = 2048
N_ROW = 8
N_COL = 16


def set_ends(result, key, least, largest):
    longest = result.shape.index(max(result.shape))
    spots = []
    for shift in (0, 1):
        where = [jax.random.randint(jax.random.fold_in(key, axis), (), 0, length) for axis, length in enumerate(result.shape)]
        where[longest] = (where[longest] + shift) % result.shape[longest]
        spots.append(tuple(where))
    return result.at[spots[0]].set(least).at[spots[1]].set(largest)


def steps_of(own_key, shape, shards, smallest, top_value):
    factor_of, own = 1.0, jax.random.fold_in(own_key, 6)
    for position, parts in shards:
        steps = jnp.exp(jax.random.uniform(jax.random.fold_in(own, position), (parts,), jnp.float32, smallest / len(shards), top_value / len(shards)))
        factor_of = factor_of * jnp.repeat(steps, shape[position] // parts).reshape([-1 if axis == position else 1 for axis in range(len(shape))])
    return factor_of


def deal_out(key, own, number, rows, amount, top, most, lean):
    order = jax.random.permutation(key, amount)
    packed, ordinary = shares(amount, rows * top, most, lean, True), shares(amount, rows * top, most, lean, False)
    places = jnp.arange(amount)

    def named(lengths, turn):
        used = int((lengths > 0).sum())
        fixed = max(1, used // 4)
        passed = fixed + (places - fixed + turn * (used - fixed)) % max(1, amount - fixed)
        return jnp.zeros((amount,), jnp.int32).at[order[jnp.where(places < fixed, places, passed)]].set(jnp.asarray(lengths, jnp.int32))

    lengths = jnp.where(number % 4 == 0, named(packed, number // 4), named(ordinary, number - number // 4 - 1))
    mixed = jax.random.permutation(jax.random.fold_in(own, 3), amount)
    giver, receiver = mixed[0:amount // 2 * 2:2], mixed[1:amount // 2 * 2:2]
    margin = jnp.minimum(lengths[giver] - 1, most - lengths[receiver]) // 2
    margin = jnp.where((giver == order[0]) | (receiver == order[0]) | (lengths[receiver] == 0), 0, jnp.maximum(margin, 0))
    passed = jax.random.randint(jax.random.fold_in(own, 4), (amount // 2,), 0, 1 << 20) % (margin + 1)
    lengths = lengths.at[giver].add(-passed).at[receiver].add(passed)
    members = jnp.searchsorted(jnp.cumsum(lengths), jnp.arange(rows * top), side="right").astype(jnp.int32)
    table = members.reshape(top, rows).T
    table = table[jax.random.permutation(jax.random.fold_in(own, 1), rows)]
    turn = jax.random.randint(jax.random.fold_in(own, 2), (rows, 1), 0, top)
    return jnp.take_along_axis(table, (jnp.arange(top)[None, :] + turn) % top, axis=1)


def shares(amount, total, most, lean, full):
    weights = [(1 << 20) // math.isqrt(standing ** lean) + 1 for standing in range(1, amount + 1)]
    largest = most if full else min(most, max(-(-total // amount), total * weights[0] // sum(weights)))
    least = 1 if total - largest >= amount - 1 else 0
    holding, surplus = [largest] + [least] * (amount - 1), total - largest - least * (amount - 1)
    while surplus > 0:
        free = [i for i in range(1, amount) if holding[i] < largest] or [i for i in range(1, amount) if holding[i] < most]
        mass, left = sum([weights[i] for i in free]), surplus
        for i in free:
            addition = min(most - holding[i], max(1, left * weights[i] // mass), surplus)
            holding[i] = holding[i] + addition
            surplus = surplus - addition
    return np.array(holding)


def normal_values(rng, dims, deviation, bound, split=(), kind=jnp.bfloat16):
    level = steps_of(rng, dims, split, -0.22, 0.18) if split else 1.0
    entries = jax.random.normal(rng, dims, jnp.float32) * deviation * level
    return jnp.minimum(jnp.maximum(entries, -bound), bound).astype(kind)


def setup_inputs(seed: int = 0) -> dict:
    splits = jax.random.split(jax.random.key(seed), 14)
    pair = normal_values(splits[0], (CROP, CROP, C), 1.0, 6.0, ((0, 8), (1, 16)), jnp.float32)
    logit_cotangent = normal_values(splits[1], (CROP, CROP, BINS), 1.0, 6.0, ((0, 8), (1, 16)))
    tiles = normal_values(splits[2], (TILES, SQ * SQ, TW), 1.0, 6.0, ((0, 128),))
    tile_target_keys = jax.random.split(jax.random.fold_in(splits[3], 1), TILES // SLOTS)
    tile_target_turns = jax.random.permutation(jax.random.fold_in(splits[3], 3), TILES // SLOTS)
    tile_target = jax.vmap(lambda own, number: deal_out(jax.random.fold_in(splits[3], 2), own, number, SLOTS, N_COL, 1, CAP, 2))(tile_target_keys, tile_target_turns).reshape((TILES, 1))
    tile_square = set_ends(jax.random.randint(splits[4], (TILES,), 0, SQ_DEV), jax.random.fold_in(splits[4], 1), 0, SQ_DEV - 1).astype(jnp.int32)
    tile_count = set_ends(jax.random.randint(splits[5], (TILES,), 1, 5), jax.random.fold_in(splits[5], 1), 1, 4).astype(jnp.int32)
    w_template = normal_values(splits[6], (TW, C), TW ** -0.5, 0.75)
    transition_norm_gain = jnp.clip(1.0 + 0.18 * jax.random.normal(splits[7], (C,), jnp.float32), 0.1, 1.9)
    transition_norm_bias = normal_values(splits[8], (C,), 0.5, 3.0, (), jnp.float32)
    w_gate = normal_values(splits[9], (C, HID), C ** -0.5, 0.5)
    w_up = normal_values(splits[10], (C, HID), C ** -0.5, 0.5)
    w_out = normal_values(splits[11], (HID, C), HID ** -0.5, 0.25)
    w_dist = normal_values(splits[12], (C, BINS), C ** -0.5, 0.5)
    return {"pair": pair, "logit_cotangent": logit_cotangent, "tiles": tiles, "tile_target": tile_target, "tile_square": tile_square, "tile_count": tile_count, "w_template": w_template, "transition_norm_gain": transition_norm_gain, "transition_norm_bias": transition_norm_bias, "w_gate": w_gate, "w_up": w_up, "w_out": w_out, "w_dist": w_dist}


def squares_to_grid(values, across, downward):
    return values.reshape(across, downward, SQ, SQ, -1).transpose(0, 2, 1, 3, 4).reshape(across * SQ, downward * SQ, -1)

def grid_to_squares(values, across, downward):
    return values.reshape(across, SQ, downward, SQ, -1).transpose(0, 2, 1, 3, 4).reshape(across * downward, SQ * SQ, -1)

def norm_intermediates(pair_entries, transition_norm_gain, transition_norm_bias):
    centered_entries = pair_entries - lax.optimization_barrier(jnp.mean(pair_entries, axis=-1, keepdims=True))
    inverse_deviation = lax.rsqrt(lax.optimization_barrier(jnp.mean(centered_entries * centered_entries, axis=-1, keepdims=True)) + 1e-05)
    standardized_entries = centered_entries * inverse_deviation
    return (standardized_entries, inverse_deviation, (standardized_entries * transition_norm_gain + transition_norm_bias).astype(jnp.bfloat16))

def transition_forward(pair_entries, transition_norm_gain, transition_norm_bias, w_gate, w_up, w_out):
    standardized_entries, inverse_deviation, normalized_entries = norm_intermediates(pair_entries, transition_norm_gain, transition_norm_bias)
    gate = jnp.dot(normalized_entries, w_gate, preferred_element_type=jnp.float32)
    upper = jnp.dot(normalized_entries, w_up, preferred_element_type=jnp.float32)
    hidden = (jax.nn.silu(gate) * upper).astype(jnp.bfloat16)
    return pair_entries + jnp.dot(hidden, w_out, preferred_element_type=jnp.float32)

def transition_backward(pair_entries, upstream, transition_norm_gain, transition_norm_bias, w_gate, w_up, w_out):
    standardized_entries, inverse_deviation, normalized_entries = norm_intermediates(pair_entries, transition_norm_gain, transition_norm_bias)
    gate = jnp.dot(normalized_entries, w_gate, preferred_element_type=jnp.float32)
    upper = jnp.dot(normalized_entries, w_up, preferred_element_type=jnp.float32)
    sigma = jax.nn.sigmoid(gate)
    swish = gate * sigma
    hidden = (swish * upper).astype(jnp.bfloat16)
    up_low = upstream.astype(jnp.bfloat16)
    g_out = jnp.dot(hidden.T, up_low, preferred_element_type=jnp.float32)
    d_hidden = jnp.dot(up_low, w_out.T, preferred_element_type=jnp.float32)
    d_gate = (d_hidden * upper * sigma * (1.0 + gate * (1.0 - sigma))).astype(jnp.bfloat16)
    d_upper = (d_hidden * swish).astype(jnp.bfloat16)
    g_gate = jnp.dot(normalized_entries.T, d_gate, preferred_element_type=jnp.float32)
    g_up = jnp.dot(normalized_entries.T, d_upper, preferred_element_type=jnp.float32)
    normalized_gradient = jnp.dot(d_gate, w_gate.T, preferred_element_type=jnp.float32) + jnp.dot(d_upper, w_up.T, preferred_element_type=jnp.float32)
    gain_gradient = lax.optimization_barrier(jnp.sum(normalized_gradient * standardized_entries, axis=0))
    g_bias = lax.optimization_barrier(jnp.sum(normalized_gradient, axis=0))
    standardized_gradient = normalized_gradient * transition_norm_gain
    entries_gradient = (standardized_gradient - lax.optimization_barrier(jnp.mean(standardized_gradient, axis=-1, keepdims=True)) - standardized_entries * lax.optimization_barrier(jnp.mean(standardized_gradient * standardized_entries, axis=-1, keepdims=True))) * inverse_deviation
    return (upstream + entries_gradient, (gain_gradient, g_bias, g_gate, g_up, g_out))

def reference(pair, logit_cotangent, tiles, tile_target, tile_square, tile_count, w_template, transition_norm_gain, transition_norm_bias, w_gate, w_up, w_out, w_dist):
    length = ROW_DEV * N_ROW
    side = length // SQ
    per_row = COL_DEV // SQ
    cells_sq = SQ * SQ
    target = tile_target[:, 0].astype(jnp.int32)
    holder = jnp.arange(TILES, dtype=jnp.int32) // SLOTS
    owner_row = holder // N_COL
    square_row = owner_row * (ROW_DEV // SQ) + tile_square // per_row
    square_col = target * per_row + tile_square % per_row
    global_ids = (square_row * side + square_col).astype(jnp.int32)
    counts_f = tile_count.astype(jnp.float32)
    group = SLOTS * 8
    groups = TILES // group
    tiles_g = tiles.reshape(groups, group, cells_sq, TW)
    ids_g = global_ids.reshape(groups, group)
    counts_g = counts_f.reshape(groups, group)

    def add_group(totals, items):
        piece, ident, weight = items
        proj = jnp.dot(piece.reshape(group * cells_sq, TW), w_template, preferred_element_type=jnp.float32)
        proj = (proj.reshape(group, cells_sq, C) / weight[:, None, None]).astype(jnp.bfloat16).astype(jnp.float32)
        return (totals.at[ident].add(proj), None)
    totals, unused = lax.scan(add_group, jnp.zeros((side * side, cells_sq, C), jnp.float32), (tiles_g, ids_g, counts_g))
    z_one = pair + squares_to_grid(totals, side, side)
    band = 8
    bands = length // band
    z_blocks = z_one.reshape(bands, band * length, C)
    z_two = lax.map(lambda piece: transition_forward(piece, transition_norm_gain, transition_norm_bias, w_gate, w_up, w_out), z_blocks)
    z_low = z_two.reshape(length * length, C).astype(jnp.bfloat16)
    heads = jnp.dot(z_low, w_dist, preferred_element_type=jnp.float32).astype(jnp.bfloat16).reshape(length, length, BINS)
    logits = (heads.astype(jnp.float32) + jnp.swapaxes(heads, 0, 1).astype(jnp.float32)).astype(jnp.bfloat16)
    d_heads = (logit_cotangent.astype(jnp.float32) + jnp.swapaxes(logit_cotangent, 0, 1).astype(jnp.float32)).astype(jnp.bfloat16)
    d_heads = d_heads.reshape(length * length, BINS)
    dz_two = jnp.dot(d_heads, w_dist.T, preferred_element_type=jnp.float32)
    g_dist = jnp.dot(z_low.T, d_heads, preferred_element_type=jnp.float32)

    def back_band(carry, items):
        piece, upstream = items
        d_piece, grads = transition_backward(piece, upstream, transition_norm_gain, transition_norm_bias, w_gate, w_up, w_out)
        return (tuple((total + term for total, term in zip(carry, grads))), d_piece)
    start = (jnp.zeros((C,), jnp.float32), jnp.zeros((C,), jnp.float32), jnp.zeros((C, HID), jnp.float32), jnp.zeros((C, HID), jnp.float32), jnp.zeros((HID, C), jnp.float32))
    sums, dz_one = lax.scan(back_band, start, (z_blocks, dz_two.reshape(bands, band * length, C)))
    grad_pair = dz_one.reshape(length, length, C)
    d_squares = grid_to_squares(grad_pair, side, side)

    def tile_back(carry, items):
        piece, ident, weight = items
        d_proj = d_squares[ident].astype(jnp.bfloat16)
        g_tile = jnp.dot(d_proj.reshape(group * cells_sq, C), w_template.T, preferred_element_type=jnp.float32)
        g_tile = (g_tile.reshape(group, cells_sq, TW) / weight[:, None, None]).astype(jnp.bfloat16)
        per_slot = jnp.einsum('spt,spc->stc', piece.astype(jnp.float32), d_proj.astype(jnp.float32))
        return (carry + lax.optimization_barrier(jnp.sum(per_slot / weight[:, None, None], axis=0)), g_tile)
    g_template, grad_tiles = lax.scan(tile_back, jnp.zeros((TW, C), jnp.float32), (tiles_g, ids_g, counts_g))
    grad_tiles = grad_tiles.reshape(TILES, cells_sq, TW)
    scale = jnp.float32(length)
    return (logits, grad_pair, grad_tiles, g_template / scale, sums[0] / scale, sums[1] / scale, sums[2] / scale, sums[3] / scale, sums[4] / scale, g_dist / scale)
```

```python
import functools

import jax
import jax.numpy as jnp
from jax import lax
from jax.experimental import pallas as pl
from jax.experimental.pallas import tpu as pltpu
from jax.sharding import PartitionSpec as P

SQ = 32
CAP = 2
MESH = pl.DeviceIdType.MESH
F32 = jnp.float32
BF16 = jnp.bfloat16
ROWS_SUM = 2048
VMEM_LIMIT = 60 * 1024 * 1024


def vmem():
    return pl.BlockSpec(memory_space=pltpu.VMEM)


def smem():
    return pl.BlockSpec(memory_space=pltpu.SMEM)


def hbm():
    return pl.BlockSpec(memory_space=pl.ANY)


def nn(a, b):
    return lax.dot_general(a, b, (((1,), (0,)), ((), ())), preferred_element_type=F32)


def nt(a, b):
    return lax.dot_general(a, b, (((1,), (1,)), ((), ())), preferred_element_type=F32)


def tn(a, b):
    return lax.dot_general(a, b, (((0,), (0,)), ((), ())), preferred_element_type=F32)


def displacements(col_devs):
    if col_devs != 16:
        return (1, col_devs), [(0, k) for k in range(1, col_devs)]
    order = [(0, 1), (1, 0), (0, 3), (3, 0), (1, 1), (3, 3), (1, 3), (3, 1),
             (0, 2), (2, 0), (1, 2), (2, 1), (3, 2), (2, 3), (2, 2)]
    return (4, 4), order


def moved(col, shape, step, sign):
    ys, zs = shape
    y = lax.rem(col // zs + sign * step[0] + ys, ys)
    z = lax.rem(lax.rem(col, zs) + sign * step[1] + zs, zs)
    return y * zs + z


def mirror_copies(row, col, src, dst, send_sem, recv_sem):
    out = []
    for h in (0, 1):
        to_row, to_col = col // 2, 2 * row + h
        here = jnp.logical_and(to_row == row, to_col == col)
        slot = lax.rem(col, 2)
        remote = pltpu.make_async_remote_copy(
            src_ref=src[h], dst_ref=dst.at[slot], send_sem=send_sem.at[h],
            recv_sem=recv_sem.at[slot], device_id=(to_row, to_col), device_id_type=MESH)
        local = pltpu.make_async_copy(src[h], dst.at[slot], recv_sem.at[slot])
        out.append((here, remote, local))
    return out


def start_mirror(copies):
    for here, remote, local in copies:
        @pl.when(jnp.logical_not(here))
        def _():
            remote.start()

        @pl.when(here)
        def _():
            local.start()


def wait_mirror(copies, src, dst, recv_sem):
    for h, (here, remote, local) in enumerate(copies):
        @pl.when(jnp.logical_not(here))
        def _():
            remote.wait_send()

        pltpu.make_async_copy(src[h], dst.at[h], recv_sem.at[h]).wait()


def greet(row, col, row_devs, col_devs, rows_too):
    barrier = pltpu.get_barrier_semaphore()
    shape, order = displacements(col_devs)
    for step in order:
        pl.semaphore_signal(barrier, inc=1, device_id=(row, moved(col, shape, step, 1)), device_id_type=MESH)
    count = len(order)
    if rows_too:
        for k in range(1, row_devs):
            pl.semaphore_signal(
                barrier, inc=1, device_id=(lax.rem(row + k, row_devs), col), device_id_type=MESH)
        count += row_devs - 1
    for h in (0, 1):
        to_row, to_col = col // 2, 2 * row + h

        @pl.when(jnp.logical_not(jnp.logical_and(to_row == row, to_col == col)))
        def _():
            pl.semaphore_signal(barrier, inc=1, device_id=(to_row, to_col), device_id_type=MESH)
    return barrier, count


def greeted(row, col, barrier, count):
    here = (col // 2 == row).astype(jnp.int32)
    pl.semaphore_wait(barrier, count + 2 - here)


def exchange_kernel(row_devs, col_devs, idx_ref, inv_ref, ids_ref, tiles_ref, cot_ref,
                    recv_ref, got_ref, mir_ref, sendbuf, pack, dma_send, dma_recv, id_send, id_recv,
                    own_sem, mir_send, mir_recv):
    row, col = lax.axis_index("row"), lax.axis_index("col")
    shape, order = displacements(col_devs)
    barrier, count = greet(row, col, row_devs, col_devs, False)

    bins, lanes = cot_ref.shape[1:]
    low = lax.broadcasted_iota(jnp.int32, (bins, lanes), 1) < lanes // 2

    def pack_pair(k, carry):
        a, b = cot_ref[2 * k].astype(F32), cot_ref[2 * k + 1].astype(F32)
        pack[0, k] = jnp.where(low, a, pltpu.roll(b, lanes // 2, 1)).astype(BF16)
        pack[1, k] = jnp.where(low, pltpu.roll(a, lanes // 2, 1), b).astype(BF16)
        return carry

    lax.fori_loop(0, cot_ref.shape[0] // 2, pack_pair, 0)

    def fill(d, carry):
        for k in range(CAP):
            sendbuf[d, k] = (tiles_ref[idx_ref[d, k]].astype(F32) * inv_ref[d, k]).astype(BF16)
        return carry

    lax.fori_loop(0, col_devs, fill, 0)
    greeted(row, col, barrier, count)

    mirror = mirror_copies(row, col, (pack.at[0], pack.at[1]), mir_ref, mir_send, mir_recv)
    start_mirror(mirror)
    copies = []
    for k, step in enumerate(order):
        to = moved(col, shape, step, 1)
        copies.append(pltpu.make_async_remote_copy(
            src_ref=sendbuf.at[to], dst_ref=recv_ref.at[col], send_sem=dma_send.at[k],
            recv_sem=dma_recv.at[k], device_id=(row, to), device_id_type=MESH))
        copies.append(pltpu.make_async_remote_copy(
            src_ref=ids_ref.at[to], dst_ref=got_ref.at[col], send_sem=id_send.at[k],
            recv_sem=id_recv.at[k], device_id=(row, to), device_id_type=MESH))
    for copy in copies:
        copy.start()
    own = pltpu.make_async_copy(sendbuf.at[col], recv_ref.at[col], own_sem.at[0])
    own_id = pltpu.make_async_copy(ids_ref.at[col], got_ref.at[col], own_sem.at[1])
    own.start()
    own_id.start()
    own.wait()
    own_id.wait()
    for copy in copies:
        copy.wait()
    wait_mirror(mirror, (pack.at[0], pack.at[1]), mir_ref, mir_recv)


def exchange(row_devs, col_devs, idx, inv, ids, tiles_t, cot_t):
    slots, feature, cells = tiles_t.shape
    cols, bins, rows = cot_t.shape
    peers = col_devs - 1
    return pl.pallas_call(
        functools.partial(exchange_kernel, row_devs, col_devs),
        name="exchange",
        out_shape=(
            jax.ShapeDtypeStruct((col_devs, CAP, feature, cells), BF16),
            jax.ShapeDtypeStruct((col_devs, 8, 128), jnp.int32),
            jax.ShapeDtypeStruct((2, cols // 2, bins, rows), BF16),
        ),
        in_specs=[smem(), smem(), vmem(), vmem(), vmem()],
        out_specs=(hbm(), hbm(), hbm()),
        scratch_shapes=[
            pltpu.VMEM((col_devs, CAP, feature, cells), BF16),
            pltpu.VMEM((2, cols // 2, bins, rows), BF16),
            pltpu.SemaphoreType.DMA((peers,)), pltpu.SemaphoreType.DMA((peers,)),
            pltpu.SemaphoreType.DMA((peers,)), pltpu.SemaphoreType.DMA((peers,)),
            pltpu.SemaphoreType.DMA((2,)),
            pltpu.SemaphoreType.DMA((2,)), pltpu.SemaphoreType.DMA((2,)),
        ],
        compiler_params=pltpu.CompilerParams(
            collective_id=0, has_side_effects=True, vmem_limit_bytes=VMEM_LIMIT),
    )(idx, inv, ids, tiles_t, cot_t)


BAND = 8


def compute_kernel(cols, rows, ids_ref, pair_ref, recv_ref, cot_ref, mir_ref, wt_ref, gain_ref, bias_ref,
                   wg_ref, wu_ref, wo_ref, wd_ref,
                   gp_ref, g_ref, hs_ref, hl_ref, acc_ref,
                   s_ref, d_ref, z_ref, ag_ref, au_ref, ao_ref, ad_ref, at_ref, an_ref):
    step = pl.program_id(0)
    col_devs = recv_ref.shape[0]
    width = gain_ref.shape[1]
    hidden = wg_ref.shape[1]
    squares, feature, cells_sq = s_ref.shape
    sq_cols = cols // SQ
    cells = BAND * cols

    @pl.when(step == 0)
    def _():
        for ref in (s_ref, ag_ref, au_ref, ao_ref, ad_ref, at_ref, an_ref):
            ref[...] = jnp.zeros(ref.shape, F32)

        def land(n, carry):
            d, k = n // CAP, lax.rem(n, CAP)
            square = ids_ref[d, 0, k]

            @pl.when(square >= 0)
            def _():
                s_ref[square] += recv_ref[d, k].astype(F32)
            return carry

        lax.fori_loop(0, col_devs * CAP, land, 0)

        def own(j, carry):
            d_ref[pl.ds(j, rows, stride=cols), :] = cot_ref[j].astype(F32).T
            return carry

        lax.fori_loop(0, cols, own, 0)

        def mirrored(n, carry):
            at = pl.multiple_of(n * rows, rows)
            d_ref[pl.ds(at, rows), :] += mir_ref[n // (cols // 2), lax.rem(n, cols // 2)].astype(F32).T
            return carry

        lax.fori_loop(0, cols, mirrored, 0)

    row0 = step * BAND
    first = row0 // SQ * sq_cols
    at = pl.multiple_of(lax.rem(row0, SQ) * SQ, BAND * SQ)
    w_t = wt_ref[...]
    pieces = [s_ref[first + d, :, pl.ds(at, BAND * SQ)].astype(BF16) for d in range(sq_cols)]
    proj = jnp.concatenate(
        [tn(piece, w_t).reshape(BAND, SQ, width) for piece in pieces], axis=1).reshape(cells, width)
    z1 = pair_ref[...].reshape(cells, width) + proj
    gain, bias = gain_ref[...], bias_ref[...]
    mean = jnp.mean(z1, axis=1, keepdims=True)
    centered = z1 - mean
    rdev = lax.rsqrt(jnp.mean(centered * centered, axis=1, keepdims=True) + 1e-5)
    xhat = centered * rdev
    normed = (xhat * gain + bias).astype(BF16)
    base = pl.multiple_of(step * cells, cells)
    dheads = d_ref[pl.ds(base, cells), :].astype(BF16)
    wd = wd_ref[...]
    dz2 = nn(dheads, wd)
    dzl = dz2.astype(BF16)
    normed_t = normed.T
    dzl_t = dzl.T
    z2 = z1
    dnorm = jnp.zeros((cells, width), F32)
    part = 256
    for k in range(hidden // part):
        span = slice(k * part, (k + 1) * part)
        gate = nn(normed, wg_ref[:, span])
        up = nn(normed, wu_ref[:, span])
        dhid = nt(dzl, wo_ref[span, :])
        s = 0.5 * jnp.tanh(0.5 * gate) + 0.5
        swish = gate * s
        hid = (swish * up).astype(BF16)
        dup = (dhid * swish).astype(BF16)
        dgate = (dhid * up * (s + swish * (1.0 - s))).astype(BF16)
        z2 = z2 + nn(hid, wo_ref[span, :])
        dnorm = dnorm + nt(dgate, wg_ref[:, span]) + nt(dup, wu_ref[:, span])
        ao_ref[:, span] += nn(dzl_t, hid)
        ag_ref[:, span] += nn(normed_t, dgate)
        au_ref[:, span] += nn(normed_t, dup)
    z_ref[pl.ds(base, cells), :] = z2
    z2_low = z2.astype(BF16)
    heads_t = nt(wd, z2_low).astype(BF16)
    for k in range(cells // 128):
        hs_ref[k] = heads_t[:, k * 128:(k + 1) * 128]
    ad_ref[...] += tn(dheads, z2_low)
    an_ref[0] += jnp.sum((dnorm * xhat).reshape(cells // 8, 8, width), axis=0)
    an_ref[1] += jnp.sum(dnorm.reshape(cells // 8, 8, width), axis=0)
    dx = dnorm * gain
    grad = dz2 + (dx - jnp.mean(dx, axis=1, keepdims=True)
                  - xhat * jnp.mean(dx * xhat, axis=1, keepdims=True)) * rdev
    grad3 = grad.reshape(BAND, cols, width)
    gp_ref[...] = grad3
    total = jnp.zeros((feature, width), F32)
    for d in range(sq_cols):
        dproj = grad3[:, d * SQ:(d + 1) * SQ, :].reshape(BAND * SQ, width).astype(BF16)
        g_ref[first + d, :, pl.ds(at, BAND * SQ)] = nt(w_t, dproj).astype(BF16)
        total = total + nn(pieces[d], dproj)
    at_ref[...] += total

    @pl.when(step == pl.num_programs(0) - 1)
    def _():
        def local(j, carry):
            zj = z_ref[pl.ds(j, rows, stride=cols), :].astype(BF16)
            hl_ref[j] = nt(wd, zj).astype(BF16)
            return carry

        lax.fori_loop(0, cols, local, 0)
        for k in range(hidden // width):
            span = slice(k * width, (k + 1) * width)
            acc_ref[k * width:(k + 1) * width, :] = ag_ref[:, span]
            acc_ref[hidden + k * width:hidden + (k + 1) * width, :] = au_ref[:, span]
            acc_ref[2 * hidden + k * width:2 * hidden + (k + 1) * width, :] = ao_ref[:, span].T
        base3 = 3 * hidden
        bins = wd.shape[0]
        acc_ref[base3:base3 + bins, :] = ad_ref[...]
        acc_ref[base3 + bins:base3 + bins + feature, :] = at_ref[...]
        tail = base3 + bins + feature
        acc_ref[tail:tail + 8, :] = an_ref[0]
        acc_ref[tail + 8:tail + 16, :] = an_ref[1]
        acc_ref[tail + 16:, :] = jnp.zeros((ROWS_SUM - tail - 16, width), F32)


def compute(ids, pair, recv, cot_t, mir, w_t, gain, bias, w_gate, w_up, w_out, wd_t):
    rows, cols, width = pair.shape
    bins = wd_t.shape[0]
    feature, cells_sq = recv.shape[2:]
    hidden = w_gate.shape[1]
    squares = rows // SQ * (cols // SQ)
    whole = lambda x: pl.BlockSpec(x.shape, lambda i: (0,) * x.ndim, pipeline_mode=pl.Buffered(1))
    ops = (pair, recv, cot_t, mir, w_t, gain, bias, w_gate, w_up, w_out, wd_t)
    hs_step = BAND * cols // 128
    return pl.pallas_call(
        functools.partial(compute_kernel, cols, rows),
        name="pair_block",
        grid=(rows // BAND,),
        out_shape=(
            jax.ShapeDtypeStruct((rows, cols, width), F32),
            jax.ShapeDtypeStruct((squares, feature, cells_sq), BF16),
            jax.ShapeDtypeStruct((rows // 2, bins, 128), BF16),
            jax.ShapeDtypeStruct((cols, bins, rows), BF16),
            jax.ShapeDtypeStruct((ROWS_SUM, width), F32),
        ),
        in_specs=[smem(), pl.BlockSpec((BAND, cols, width), lambda i: (i, 0, 0))] + [whole(x) for x in ops[1:]],
        out_specs=(
            pl.BlockSpec((BAND, cols, width), lambda i: (i, 0, 0)),
            pl.BlockSpec((squares, feature, cells_sq), lambda i: (0, 0, 0)),
            pl.BlockSpec((hs_step, bins, 128), lambda i: (i, 0, 0)),
            pl.BlockSpec((cols, bins, rows), lambda i: (0, 0, 0)),
            pl.BlockSpec((ROWS_SUM, width), lambda i: (0, 0)),
        ),
        scratch_shapes=[
            pltpu.VMEM((squares, feature, cells_sq), F32),
            pltpu.VMEM((rows * cols, bins), F32),
            pltpu.VMEM((rows * cols, width), F32),
            pltpu.VMEM((width, hidden), F32),
            pltpu.VMEM((width, hidden), F32),
            pltpu.VMEM((width, hidden), F32),
            pltpu.VMEM((bins, width), F32),
            pltpu.VMEM((feature, width), F32),
            pltpu.VMEM((2, 8, width), F32),
        ],
        compiler_params=pltpu.CompilerParams(
            dimension_semantics=("arbitrary",), vmem_limit_bytes=VMEM_LIMIT),
    )(ids, *ops)


def return_kernel(row_devs, col_devs, scale, ids_ref, g_ref, hs_ref, acc_ref,
                  back_ref, mir_ref, sum_ref, sendbuf, low, rs_recv, cs_send, cs_recv, piece, chunk,
                  dma_send, dma_recv, own_sem, mir_send, mir_recv, a_send, a_recv, b_send, b_recv,
                  c_send, c_recv, d_send, d_recv):
    row, col = lax.axis_index("row"), lax.axis_index("col")
    shape, order = displacements(col_devs)
    barrier, count = greet(row, col, row_devs, col_devs, True)
    rows_chunk = ROWS_SUM // row_devs
    rows_piece = rows_chunk // col_devs
    low[...] = acc_ref[...].astype(BF16)

    def fill(d, carry):
        for k in range(CAP):
            sendbuf[d, k] = g_ref[jnp.maximum(ids_ref[d, 0, k], 0)]
        return carry

    lax.fori_loop(0, col_devs, fill, 0)
    greeted(row, col, barrier, count)

    def at_row(k):
        return lax.rem(row + k, row_devs)

    def part(r):
        return pl.ds(pl.multiple_of(r * rows_chunk, rows_chunk), rows_chunk)

    first = []
    for k in range(1, row_devs):
        to = at_row(k)
        first.append(pltpu.make_async_remote_copy(
            src_ref=low.at[part(to)], dst_ref=rs_recv.at[k - 1], send_sem=a_send.at[k - 1],
            recv_sem=a_recv.at[k - 1], device_id=(to, col), device_id_type=MESH))
    bulk = []
    for k, step in enumerate(order):
        to = moved(col, shape, step, 1)
        bulk.append(pltpu.make_async_remote_copy(
            src_ref=sendbuf.at[to], dst_ref=back_ref.at[col], send_sem=dma_send.at[k],
            recv_sem=dma_recv.at[k], device_id=(row, to), device_id_type=MESH))
    half = hs_ref.shape[0] // 2
    sources = (hs_ref.at[pl.ds(0, half)], hs_ref.at[pl.ds(half, half)])
    mirror = mirror_copies(row, col, sources, mir_ref, mir_send, mir_recv)
    own = pltpu.make_async_copy(sendbuf.at[col], back_ref.at[col], own_sem.at[0])

    for copy in first:
        copy.start()
    start_mirror(mirror)
    own.start()
    third = (len(bulk) + 2) // 3
    for copy in bulk[:third]:
        copy.start()

    for copy in first:
        copy.wait()
    total = acc_ref[part(row), :]
    for k in range(row_devs - 1):
        total = total + rs_recv[k].astype(F32)
    cs_send[...] = total.astype(BF16).reshape(cs_send.shape)
    second = []
    for k, step in enumerate(order):
        to = moved(col, shape, step, 1)
        second.append(pltpu.make_async_remote_copy(
            src_ref=cs_send.at[to], dst_ref=cs_recv.at[k], send_sem=b_send.at[k],
            recv_sem=b_recv.at[k], device_id=(row, to), device_id_type=MESH))
    for copy in second:
        copy.start()
    for copy in bulk[third:2 * third]:
        copy.start()
    for copy in second:
        copy.wait()
    mine = cs_send[col].astype(F32)
    for k in range(col_devs - 1):
        mine = mine + cs_recv[k].astype(F32)
    piece[...] = (mine * scale).astype(BF16)
    chunk[col] = piece[...]
    third_leg = []
    for k, step in enumerate(order):
        third_leg.append(pltpu.make_async_remote_copy(
            src_ref=piece, dst_ref=chunk.at[col], send_sem=c_send.at[k],
            recv_sem=c_recv.at[k], device_id=(row, moved(col, shape, step, 1)), device_id_type=MESH))
    for copy in third_leg:
        copy.start()
    for copy in bulk[2 * third:]:
        copy.start()
    for copy in third_leg:
        copy.wait()
    last = []
    for k in range(1, row_devs):
        last.append(pltpu.make_async_remote_copy(
            src_ref=chunk, dst_ref=sum_ref.at[row], send_sem=d_send.at[k - 1],
            recv_sem=d_recv.at[k - 1], device_id=(at_row(k), col), device_id_type=MESH))
    for copy in last:
        copy.start()
    own_sum = pltpu.make_async_copy(chunk, sum_ref.at[row], own_sem.at[1])
    own_sum.start()
    own_sum.wait()
    for copy in last:
        copy.wait()
    own.wait()
    wait_mirror(mirror, sources, mir_ref, mir_recv)
    for copy in bulk:
        copy.wait()


def give_back(row_devs, col_devs, scale, ids, g, hs, acc):
    squares, feature, cells = g.shape
    bins = hs.shape[1]
    peers = col_devs - 1
    rows_chunk = ROWS_SUM // row_devs
    rows_piece = rows_chunk // col_devs
    dma = lambda n: pltpu.SemaphoreType.DMA((n,))
    return pl.pallas_call(
        functools.partial(return_kernel, row_devs, col_devs, scale),
        name="give_back",
        out_shape=(
            jax.ShapeDtypeStruct((col_devs, CAP, feature, cells), BF16),
            jax.ShapeDtypeStruct((2, hs.shape[0] // 2, bins, 128), BF16),
            jax.ShapeDtypeStruct((row_devs, col_devs, rows_piece, 128), BF16),
        ),
        in_specs=[smem(), vmem(), vmem(), vmem()],
        out_specs=(hbm(), hbm(), hbm()),
        scratch_shapes=[
            pltpu.VMEM((col_devs, CAP, feature, cells), BF16),
            pltpu.VMEM((ROWS_SUM, 128), BF16),
            pltpu.VMEM((row_devs - 1, rows_chunk, 128), BF16),
            pltpu.VMEM((col_devs, rows_piece, 128), BF16),
            pltpu.VMEM((col_devs - 1, rows_piece, 128), BF16),
            pltpu.VMEM((rows_piece, 128), BF16),
            pltpu.VMEM((col_devs, rows_piece, 128), BF16),
            dma(peers), dma(peers), dma(2), dma(2), dma(2),
            dma(row_devs - 1), dma(row_devs - 1), dma(peers), dma(peers),
            dma(peers), dma(peers), dma(row_devs - 1), dma(row_devs - 1),
        ],
        compiler_params=pltpu.CompilerParams(
            collective_id=1, has_side_effects=True, vmem_limit_bytes=VMEM_LIMIT),
    )(ids, g, hs, acc)


def finish_kernel(hidden, slot_ref, back_ref, inv_ref, mir_ref, hl_ref, sum_ref,
                  tile_ref, log_ref, gt_ref, gg_ref, gu_ref, go_ref, gd_ref, gn_ref):
    step = pl.program_id(0)
    tile_ref[0] = (back_ref[0].astype(F32) * inv_ref[step]).astype(BF16)
    bins, lanes = hl_ref.shape[1:]
    low = lax.broadcasted_iota(jnp.int32, (bins, lanes), 1) < lanes // 2
    for k in range(mir_ref.shape[1]):
        a, b = mir_ref[0, k].astype(F32), mir_ref[1, k].astype(F32)
        even = jnp.where(low, a, pltpu.roll(b, lanes // 2, 1))
        odd = jnp.where(low, pltpu.roll(a, lanes // 2, 1), b)
        log_ref[2 * k] = (hl_ref[2 * k].astype(F32) + even).astype(BF16)
        log_ref[2 * k + 1] = (hl_ref[2 * k + 1].astype(F32) + odd).astype(BF16)

    @pl.when(step == 0)
    def _():
        width = sum_ref.shape[1]
        for k in range(hidden // width):
            span = slice(k * width, (k + 1) * width)
            gg_ref[:, span] = sum_ref[k * width:(k + 1) * width, :].astype(F32)
            gu_ref[:, span] = sum_ref[hidden + k * width:hidden + (k + 1) * width, :].astype(F32)
        go_ref[...] = sum_ref[2 * hidden:3 * hidden, :].astype(F32)
        at = 3 * hidden
        gd_ref[...] = sum_ref[at:at + gd_ref.shape[0], :].astype(F32)
        at += gd_ref.shape[0]
        gt_ref[...] = sum_ref[at:at + gt_ref.shape[0], :].astype(F32)
        at += gt_ref.shape[0]
        norm = sum_ref[at:at + 16, :].astype(F32)
        gn_ref[0:1, :] = jnp.sum(norm[0:8], axis=0, keepdims=True)
        gn_ref[1:2, :] = jnp.sum(norm[8:16], axis=0, keepdims=True)


def finish(hidden, slot_of, inv, back, mir, hl, sums):
    slots = slot_of.shape[0]
    feature, cells = back.shape[1:]
    cols, bins, rows = hl.shape
    width = sums.shape[1]
    per = cols // slots
    const = lambda shape: pl.BlockSpec(shape, lambda i, s: (0,) * len(shape))
    outs = [((slots, feature, cells), BF16), ((cols, bins, rows), BF16), ((feature, width), F32),
            ((width, hidden), F32), ((width, hidden), F32), ((hidden, width), F32), ((bins, width), F32),
            ((2, width), F32)]
    return pl.pallas_call(
        functools.partial(finish_kernel, hidden),
        name="finish",
        grid_spec=pltpu.PrefetchScalarGridSpec(
            num_scalar_prefetch=1,
            grid=(slots,),
            in_specs=[
                pl.BlockSpec((1, feature, cells), lambda i, s: (s[i], 0, 0)),
                pl.BlockSpec(memory_space=pltpu.SMEM),
                pl.BlockSpec((2, per // 2, bins, rows), lambda i, s: (0, i, 0, 0)),
                pl.BlockSpec((per, bins, rows), lambda i, s: (i, 0, 0)),
                const(sums.shape),
            ],
            out_specs=[
                pl.BlockSpec((1, feature, cells), lambda i, s: (i, 0, 0)),
                pl.BlockSpec((per, bins, rows), lambda i, s: (i, 0, 0)),
            ] + [const(shape) for shape, _ in outs[2:]],
        ),
        out_shape=[jax.ShapeDtypeStruct(shape, kind) for shape, kind in outs],
        compiler_params=pltpu.CompilerParams(
            dimension_semantics=("arbitrary",), vmem_limit_bytes=VMEM_LIMIT),
    )(slot_of, back, inv, mir, hl, sums)


def per_device(pair, logit_cotangent, tiles, tile_target, tile_square, tile_count, w_template,
               transition_norm_gain, transition_norm_bias, w_gate, w_up, w_out, w_dist):
    row_devs = lax.axis_size("row")
    col_devs = lax.axis_size("col")
    rows, cols, width = pair.shape
    length = rows * row_devs
    slots, cells_sq, feature = tiles.shape
    hidden = w_gate.shape[1]
    tiles_t = jnp.transpose(tiles, (0, 2, 1))
    cot_t = jnp.transpose(logit_cotangent, (1, 2, 0))
    target = tile_target[:, 0]
    places = jnp.arange(slots, dtype=jnp.int32)
    rank = jnp.sum((target[:, None] == target[None, :]) & (places[None, :] < places[:, None]),
                   axis=1, dtype=jnp.int32)
    slot_of = target * CAP + rank
    inv_count = 1.0 / tile_count.astype(F32)
    chosen = slot_of[None, :] == jnp.arange(col_devs * CAP, dtype=jnp.int32)[:, None]
    picked = chosen.astype(jnp.int32)
    idx = jnp.sum(picked * places[None, :], axis=1).reshape(col_devs, CAP)
    send_inv = jnp.sum(jnp.where(chosen, inv_count[None, :], 0.0), axis=1).reshape(col_devs, CAP)
    send_ids = (jnp.sum(picked * (tile_square + 1)[None, :], axis=1) - 1).reshape(col_devs, CAP)
    ids = jnp.broadcast_to(jnp.pad(send_ids, ((0, 0), (0, 128 - CAP)))[:, None, :], (col_devs, 8, 128))

    recv, got, mir = exchange(row_devs, col_devs, idx, send_inv, ids, tiles_t, cot_t)
    grad_pair, g, hs, hl, acc = compute(
        got, pair, recv, cot_t, mir, w_template, transition_norm_gain[None, :],
        transition_norm_bias[None, :], w_gate, w_up, w_out, w_dist.T)
    back, mir_heads, sums = give_back(row_devs, col_devs, 1.0 / length, got, g, hs, acc)
    grad_tiles_t, logits_t, g_template, g_gate, g_up, g_out, g_dist_t, g_norm = finish(
        hidden, slot_of, inv_count, back.reshape(col_devs * CAP, feature, cells_sq), mir_heads, hl,
        sums.reshape(ROWS_SUM, width))
    return (
        jnp.transpose(logits_t, (2, 0, 1)),
        grad_pair,
        jnp.transpose(grad_tiles_t, (0, 2, 1)),
        g_template,
        g_norm[0],
        g_norm[1],
        g_gate,
        g_up,
        g_out,
        g_dist_t.T,
    )


def solution(mesh):
    return jax.shard_map(
        per_device,
        mesh=mesh,
        in_specs=(
            P("row", "col", None),
            P("row", "col", None),
            P(("row", "col"), None, None),
            P(("row", "col"), None),
            P(("row", "col")),
            P(("row", "col")),
            P(), P(), P(), P(), P(), P(), P(),
        ),
        out_specs=(
            P("row", "col", None),
            P("row", "col", None),
            P(("row", "col"), None, None),
            P(), P(), P(), P(), P(), P(), P(),
        ),
        check_vma=False,
    )
```

```python
import functools

import jax
import jax.numpy as jnp
from jax import lax
from jax.experimental import pallas as pl
from jax.experimental.pallas import tpu as pltpu
from jax.sharding import PartitionSpec as P

SQ = 32
CAP = 2
MESH = pl.DeviceIdType.MESH
F32 = jnp.float32
BF16 = jnp.bfloat16
ROWS_SUM = 2048
VMEM_LIMIT = 60 * 1024 * 1024


def vmem():
    return pl.BlockSpec(memory_space=pltpu.VMEM)


def smem():
    return pl.BlockSpec(memory_space=pltpu.SMEM)


def hbm():
    return pl.BlockSpec(memory_space=pl.ANY)


def nn(a, b):
    return lax.dot_general(a, b, (((1,), (0,)), ((), ())), preferred_element_type=F32)


def nt(a, b):
    return lax.dot_general(a, b, (((1,), (1,)), ((), ())), preferred_element_type=F32)


def tn(a, b):
    return lax.dot_general(a, b, (((0,), (0,)), ((), ())), preferred_element_type=F32)


def displacements(col_devs):
    if col_devs != 16:
        return (1, col_devs), [(0, k) for k in range(1, col_devs)]
    order = [(0, 1), (1, 0), (0, 3), (3, 0), (1, 1), (3, 3), (1, 3), (3, 1),
             (0, 2), (2, 0), (1, 2), (2, 1), (3, 2), (2, 3), (2, 2)]
    return (4, 4), order


def moved(col, shape, step, sign):
    ys, zs = shape
    y = lax.rem(col // zs + sign * step[0] + ys, ys)
    z = lax.rem(lax.rem(col, zs) + sign * step[1] + zs, zs)
    return y * zs + z


class Place:
    def __init__(self, row_devs, col_devs):
        self.row, self.col = lax.axis_index("row"), lax.axis_index("col")
        self.xs, self.zs = row_devs // 2, col_devs // (row_devs // 2)
        self.x, self.k = self.row // 2, lax.rem(self.row, 2)
        self.y, self.z = self.col // self.zs, lax.rem(self.col, self.zs)

    def turn(self, value, by):
        return lax.rem(value + by, self.xs) if self.xs > 1 else value


class Mirror:
    def __init__(self, place, src, first, second, dst, sems):
        self.p, self.src, self.first, self.second, self.dst = place, src, first, second, dst
        self.s1, self.r1, self.s2, self.r2, self.s3, self.r3, self.own = sems

    def along_x(self, source, target, send, recv):
        p = self.p
        copies = []
        for n in range(1, p.xs):
            to = p.turn(p.x, n)
            copies.append(pltpu.make_async_remote_copy(
                src_ref=source(to), dst_ref=target.at[p.x], send_sem=send.at[n - 1], recv_sem=recv.at[n - 1],
                device_id=(2 * to + p.k, p.col), device_id_type=MESH))
        return copies

    def start_1(self):
        p = self.p
        self.copies = self.along_x(lambda to: self.src.at[:, to], self.first, self.s1, self.r1)
        for copy in self.copies:
            copy.start()
        self.local = pltpu.make_async_copy(self.src.at[:, p.x], self.first.at[p.x], self.own.at[0])
        self.local.start()

    def finish(self):
        self.local.wait()
        for copy in self.copies:
            copy.wait()

    def start_2(self):
        p = self.p
        self.plan = []
        for n in range(p.xs):
            to_y = p.turn(p.y, n)
            for h in (0, 1):
                to_z, to_k = 2 * p.k + h, p.z // 2
                source, target = self.first.at[to_y, h], self.second.at[p.y, lax.rem(p.z, 2)]
                slot = 2 * n + lax.rem(p.z, 2)
                remote = pltpu.make_async_remote_copy(
                    src_ref=source, dst_ref=target, send_sem=self.s2.at[2 * n + h], recv_sem=self.r2.at[slot],
                    device_id=(2 * p.x + to_k, to_y * p.zs + to_z), device_id_type=MESH)
                if n == 0:
                    here = jnp.logical_and(to_k == p.k, to_z == p.z)
                    local = pltpu.make_async_copy(source, target, self.r2.at[slot])
                    start_one(here, remote, local)
                    self.plan.append((here, remote))
                else:
                    remote.start()
                    self.plan.append((None, remote))

    def finish_2(self):
        for i, (here, remote) in enumerate(self.plan):
            if here is None:
                remote.wait_send()
            else:
                @pl.when(jnp.logical_not(here))
                def _():
                    remote.wait_send()
            ref = self.second.at[0, 0]
            pltpu.make_async_copy(ref, ref, self.r2.at[i]).wait()

    def start_3(self):
        p = self.p
        self.copies = self.along_x(lambda to: self.second.at[to], self.dst, self.s3, self.r3)
        for copy in self.copies:
            copy.start()
        self.local = pltpu.make_async_copy(self.second.at[p.x], self.dst.at[p.x], self.own.at[1])
        self.local.start()


def start_one(here, remote, local):
    @pl.when(jnp.logical_not(here))
    def _():
        remote.start()

    @pl.when(here)
    def _():
        local.start()


def mirror_sems(row_devs):
    xs = row_devs // 2
    dma = lambda n: pltpu.SemaphoreType.DMA((n,))
    return [dma(max(xs - 1, 1)), dma(max(xs - 1, 1)), dma(2 * xs), dma(2 * xs),
            dma(max(xs - 1, 1)), dma(max(xs - 1, 1)), dma(2)]


def greet(p, row_devs, col_devs):
    barrier = pltpu.get_barrier_semaphore()
    peers = 0
    for n in range(1, col_devs):
        pl.semaphore_signal(barrier, inc=1, device_id=(p.row, lax.rem(p.col + n, col_devs)), device_id_type=MESH)
        peers += 1
    for n in range(1, row_devs):
        pl.semaphore_signal(barrier, inc=1, device_id=(lax.rem(p.row + n, row_devs), p.col), device_id_type=MESH)
        peers += 1
    for n in range(1, col_devs):
        pl.semaphore_signal(
            barrier, inc=1, device_id=(2 * p.x + 1 - p.k, lax.rem(p.col + n, col_devs)), device_id_type=MESH)
        peers += 1
    return lambda: pl.semaphore_wait(barrier, peers)


def exchange_kernel(row_devs, col_devs, idx_ref, inv_ref, ids_ref, tiles_ref, cot_ref,
                    recv_ref, got_ref, mir_ref, sendbuf, pack, first, second, dma_send, dma_recv,
                    id_send, id_recv, own_sem, *mirror_sem):
    p = Place(row_devs, col_devs)
    row, col = p.row, p.col
    shape, order = displacements(col_devs)
    greeted = greet(p, row_devs, col_devs)

    bins, lanes = cot_ref.shape[1:]
    low = lax.broadcasted_iota(jnp.int32, (bins, lanes), 1) < lanes // 2

    def pack_pair(k, carry):
        a, b = cot_ref[2 * k].astype(F32), cot_ref[2 * k + 1].astype(F32)
        m, t = k // pack.shape[2], lax.rem(k, pack.shape[2])
        pack[0, m, t] = jnp.where(low, a, pltpu.roll(b, lanes // 2, 1)).astype(BF16)
        pack[1, m, t] = jnp.where(low, pltpu.roll(a, lanes // 2, 1), b).astype(BF16)
        return carry

    lax.fori_loop(0, cot_ref.shape[0] // 2, pack_pair, 0)

    def fill(d, carry):
        for k in range(CAP):
            sendbuf[d, k] = (tiles_ref[idx_ref[d, k]].astype(F32) * inv_ref[d, k]).astype(BF16)
        return carry

    lax.fori_loop(0, col_devs, fill, 0)
    greeted()

    mirror = Mirror(p, pack, first, second, mir_ref, mirror_sem)
    mirror.start_1()
    names, bulk = [], []
    for k, step in enumerate(order):
        to = moved(col, shape, step, 1)
        names.append(pltpu.make_async_remote_copy(
            src_ref=ids_ref.at[to], dst_ref=got_ref.at[col], send_sem=id_send.at[k],
            recv_sem=id_recv.at[k], device_id=(row, to), device_id_type=MESH))
        bulk.append(pltpu.make_async_remote_copy(
            src_ref=sendbuf.at[to], dst_ref=recv_ref.at[col], send_sem=dma_send.at[k],
            recv_sem=dma_recv.at[k], device_id=(row, to), device_id_type=MESH))
    own = pltpu.make_async_copy(sendbuf.at[col], recv_ref.at[col], own_sem.at[0])
    own_id = pltpu.make_async_copy(ids_ref.at[col], got_ref.at[col], own_sem.at[1])
    own.start()
    own_id.start()
    ahead = len(bulk) * 2 // 5
    for copy in names + bulk[:ahead]:
        copy.start()
    mirror.finish()
    mirror.start_2()
    for copy in bulk[ahead:]:
        copy.start()
    mirror.finish_2()
    mirror.start_3()
    own.wait()
    own_id.wait()
    for copy in names:
        copy.wait()
    mirror.finish()
    for copy in bulk:
        copy.wait()


def exchange(row_devs, col_devs, idx, inv, ids, tiles_t, cot_t):
    slots, feature, cells = tiles_t.shape
    cols, bins, rows = cot_t.shape
    peers, xs = col_devs - 1, row_devs // 2
    return pl.pallas_call(
        functools.partial(exchange_kernel, row_devs, col_devs),
        name="exchange",
        out_shape=(
            jax.ShapeDtypeStruct((col_devs, CAP, feature, cells), BF16),
            jax.ShapeDtypeStruct((col_devs, 8, 128), jnp.int32),
            jax.ShapeDtypeStruct((xs, 2, cols // 2 // xs, bins, rows), BF16),
        ),
        in_specs=[smem(), smem(), vmem(), vmem(), vmem()],
        out_specs=(hbm(), hbm(), hbm()),
        scratch_shapes=[
            pltpu.VMEM((col_devs, CAP, feature, cells), BF16),
            pltpu.VMEM((2, xs, cols // 2 // xs, bins, rows), BF16),
            pltpu.VMEM((xs, 2, cols // 2 // xs, bins, rows), BF16),
            pltpu.VMEM((xs, 2, cols // 2 // xs, bins, rows), BF16),
            pltpu.SemaphoreType.DMA((peers,)), pltpu.SemaphoreType.DMA((peers,)),
            pltpu.SemaphoreType.DMA((peers,)), pltpu.SemaphoreType.DMA((peers,)),
            pltpu.SemaphoreType.DMA((2,)),
        ] + mirror_sems(row_devs),
        compiler_params=pltpu.CompilerParams(
            collective_id=0, has_side_effects=True, vmem_limit_bytes=VMEM_LIMIT),
    )(idx, inv, ids, tiles_t, cot_t)


BAND = 8


def compute_kernel(cols, rows, ids_ref, pair_ref, recv_ref, cot_ref, mir_ref, wt_ref, gain_ref, bias_ref,
                   wg_ref, wu_ref, wo_ref, wd_ref,
                   gp_ref, g_ref, hs_ref, hl_ref, acc_ref,
                   s_ref, d_ref, z_ref, ag_ref, au_ref, ao_ref, ad_ref, at_ref, an_ref):
    step = pl.program_id(0)
    col_devs = recv_ref.shape[0]
    width = gain_ref.shape[1]
    hidden = wg_ref.shape[1]
    squares, feature, cells_sq = s_ref.shape
    sq_cols = cols // SQ
    cells = BAND * cols

    @pl.when(step == 0)
    def _():
        for ref in (s_ref, ag_ref, au_ref, ao_ref, ad_ref, at_ref, an_ref):
            ref[...] = jnp.zeros(ref.shape, F32)

        def land(n, carry):
            d, k = n // CAP, lax.rem(n, CAP)
            square = ids_ref[d, 0, k]

            @pl.when(square >= 0)
            def _():
                s_ref[square] += recv_ref[d, k].astype(F32)
            return carry

        lax.fori_loop(0, col_devs * CAP, land, 0)

        def own(j, carry):
            d_ref[pl.ds(j, rows, stride=cols), :] = cot_ref[j].astype(F32).T
            return carry

        lax.fori_loop(0, cols, own, 0)

        def mirrored(n, carry):
            at = pl.multiple_of(n * rows, rows)
            d_ref[pl.ds(at, rows), :] += mir_ref[
                lax.rem(n, cols // 2) // mir_ref.shape[2], n // (cols // 2), lax.rem(n, mir_ref.shape[2])].astype(F32).T
            return carry

        lax.fori_loop(0, cols, mirrored, 0)

    row0 = step * BAND
    first = row0 // SQ * sq_cols
    at = pl.multiple_of(lax.rem(row0, SQ) * SQ, BAND * SQ)
    w_t = wt_ref[...]
    pieces = [s_ref[first + d, :, pl.ds(at, BAND * SQ)].astype(BF16) for d in range(sq_cols)]
    proj = jnp.concatenate(
        [tn(piece, w_t).reshape(BAND, SQ, width) for piece in pieces], axis=1).reshape(cells, width)
    z1 = pair_ref[...].reshape(cells, width) + proj
    gain, bias = gain_ref[...], bias_ref[...]
    mean = jnp.mean(z1, axis=1, keepdims=True)
    centered = z1 - mean
    rdev = lax.rsqrt(jnp.mean(centered * centered, axis=1, keepdims=True) + 1e-5)
    xhat = centered * rdev
    normed = (xhat * gain + bias).astype(BF16)
    base = pl.multiple_of(step * cells, cells)
    dheads = d_ref[pl.ds(base, cells), :].astype(BF16)
    wd = wd_ref[...]
    dz2 = nn(dheads, wd)
    dzl = dz2.astype(BF16)
    normed_t = normed.T
    dzl_t = dzl.T
    z2 = z1
    dnorm = jnp.zeros((cells, width), F32)
    part = 256
    for k in range(hidden // part):
        span = slice(k * part, (k + 1) * part)
        gate = nn(normed, wg_ref[:, span])
        up = nn(normed, wu_ref[:, span])
        dhid = nt(dzl, wo_ref[span, :])
        s = 0.5 * jnp.tanh(0.5 * gate) + 0.5
        swish = gate * s
        hid = (swish * up).astype(BF16)
        dup = (dhid * swish).astype(BF16)
        dgate = (dhid * up * (s + swish * (1.0 - s))).astype(BF16)
        z2 = z2 + nn(hid, wo_ref[span, :])
        dnorm = dnorm + nt(dgate, wg_ref[:, span]) + nt(dup, wu_ref[:, span])
        ao_ref[:, span] += nn(dzl_t, hid)
        ag_ref[:, span] += nn(normed_t, dgate)
        au_ref[:, span] += nn(normed_t, dup)
    z_ref[pl.ds(base, cells), :] = z2
    z2_low = z2.astype(BF16)
    heads_t = nt(wd, z2_low).astype(BF16)
    for k in range(cells // 128):
        hs_ref[k] = heads_t[:, k * 128:(k + 1) * 128]
    ad_ref[...] += tn(dheads, z2_low)
    an_ref[0] += jnp.sum((dnorm * xhat).reshape(cells // 8, 8, width), axis=0)
    an_ref[1] += jnp.sum(dnorm.reshape(cells // 8, 8, width), axis=0)
    dx = dnorm * gain
    grad = dz2 + (dx - jnp.mean(dx, axis=1, keepdims=True)
                  - xhat * jnp.mean(dx * xhat, axis=1, keepdims=True)) * rdev
    grad3 = grad.reshape(BAND, cols, width)
    gp_ref[...] = grad3
    total = jnp.zeros((feature, width), F32)
    for d in range(sq_cols):
        dproj = grad3[:, d * SQ:(d + 1) * SQ, :].reshape(BAND * SQ, width).astype(BF16)
        g_ref[first + d, :, pl.ds(at, BAND * SQ)] = nt(w_t, dproj).astype(BF16)
        total = total + nn(pieces[d], dproj)
    at_ref[...] += total

    @pl.when(step == pl.num_programs(0) - 1)
    def _():
        def local(j, carry):
            zj = z_ref[pl.ds(j, rows, stride=cols), :].astype(BF16)
            hl_ref[j] = nt(wd, zj).astype(BF16)
            return carry

        lax.fori_loop(0, cols, local, 0)
        for k in range(hidden // width):
            span = slice(k * width, (k + 1) * width)
            acc_ref[k * width:(k + 1) * width, :] = ag_ref[:, span]
            acc_ref[hidden + k * width:hidden + (k + 1) * width, :] = au_ref[:, span]
            acc_ref[2 * hidden + k * width:2 * hidden + (k + 1) * width, :] = ao_ref[:, span].T
        base3 = 3 * hidden
        bins = wd.shape[0]
        acc_ref[base3:base3 + bins, :] = ad_ref[...]
        acc_ref[base3 + bins:base3 + bins + feature, :] = at_ref[...]
        tail = base3 + bins + feature
        acc_ref[tail:tail + 8, :] = an_ref[0]
        acc_ref[tail + 8:tail + 16, :] = an_ref[1]
        acc_ref[tail + 16:, :] = jnp.zeros((ROWS_SUM - tail - 16, width), F32)


def compute(ids, pair, recv, cot_t, mir, w_t, gain, bias, w_gate, w_up, w_out, wd_t):
    rows, cols, width = pair.shape
    bins = wd_t.shape[0]
    feature, cells_sq = recv.shape[2:]
    hidden = w_gate.shape[1]
    squares = rows // SQ * (cols // SQ)
    whole = lambda x: pl.BlockSpec(x.shape, lambda i: (0,) * x.ndim, pipeline_mode=pl.Buffered(1))
    ops = (pair, recv, cot_t, mir, w_t, gain, bias, w_gate, w_up, w_out, wd_t)
    hs_step = BAND * cols // 128
    return pl.pallas_call(
        functools.partial(compute_kernel, cols, rows),
        name="pair_block",
        grid=(rows // BAND,),
        out_shape=(
            jax.ShapeDtypeStruct((rows, cols, width), F32),
            jax.ShapeDtypeStruct((squares, feature, cells_sq), BF16),
            jax.ShapeDtypeStruct((rows // 2, bins, 128), BF16),
            jax.ShapeDtypeStruct((cols, bins, rows), BF16),
            jax.ShapeDtypeStruct((ROWS_SUM, width), F32),
        ),
        in_specs=[smem(), pl.BlockSpec((BAND, cols, width), lambda i: (i, 0, 0))] + [whole(x) for x in ops[1:]],
        out_specs=(
            pl.BlockSpec((BAND, cols, width), lambda i: (i, 0, 0)),
            pl.BlockSpec((squares, feature, cells_sq), lambda i: (0, 0, 0)),
            pl.BlockSpec((hs_step, bins, 128), lambda i: (i, 0, 0)),
            pl.BlockSpec((cols, bins, rows), lambda i: (0, 0, 0)),
            pl.BlockSpec((ROWS_SUM, width), lambda i: (0, 0)),
        ),
        scratch_shapes=[
            pltpu.VMEM((squares, feature, cells_sq), F32),
            pltpu.VMEM((rows * cols, bins), F32),
            pltpu.VMEM((rows * cols, width), F32),
            pltpu.VMEM((width, hidden), F32),
            pltpu.VMEM((width, hidden), F32),
            pltpu.VMEM((width, hidden), F32),
            pltpu.VMEM((bins, width), F32),
            pltpu.VMEM((feature, width), F32),
            pltpu.VMEM((2, 8, width), F32),
        ],
        compiler_params=pltpu.CompilerParams(
            dimension_semantics=("arbitrary",), vmem_limit_bytes=VMEM_LIMIT),
    )(ids, *ops)


def return_kernel(row_devs, col_devs, scale, ids_ref, g_ref, hs_ref, acc_ref,
                  back_ref, mir_ref, sum_ref, sendbuf, low, rs_recv, cs_send, cs_recv, piece, chunk,
                  m_first, m_second, dma_send, dma_recv, own_sem, a_send, a_recv, b_send, b_recv,
                  c_send, c_recv, d_send, d_recv, *mirror_sem):
    p = Place(row_devs, col_devs)
    row, col = p.row, p.col
    shape, order = displacements(col_devs)
    greeted = greet(p, row_devs, col_devs)
    rows_chunk = ROWS_SUM // row_devs
    rows_piece = rows_chunk // col_devs
    low[...] = acc_ref[...].astype(BF16)

    def fill(d, carry):
        for k in range(CAP):
            sendbuf[d, k] = g_ref[jnp.maximum(ids_ref[d, 0, k], 0)]
        return carry

    lax.fori_loop(0, col_devs, fill, 0)
    greeted()

    def at_row(k):
        return lax.rem(row + k, row_devs)

    def part(r):
        return pl.ds(pl.multiple_of(r * rows_chunk, rows_chunk), rows_chunk)

    first = []
    for k in range(1, row_devs):
        to = at_row(k)
        first.append(pltpu.make_async_remote_copy(
            src_ref=low.at[part(to)], dst_ref=rs_recv.at[k - 1], send_sem=a_send.at[k - 1],
            recv_sem=a_recv.at[k - 1], device_id=(to, col), device_id_type=MESH))
    bulk = []
    for k, step in enumerate(order):
        to = moved(col, shape, step, 1)
        bulk.append(pltpu.make_async_remote_copy(
            src_ref=sendbuf.at[to], dst_ref=back_ref.at[col], send_sem=dma_send.at[k],
            recv_sem=dma_recv.at[k], device_id=(row, to), device_id_type=MESH))
    mirror = Mirror(p, hs_ref, m_first, m_second, mir_ref, mirror_sem)
    own = pltpu.make_async_copy(sendbuf.at[col], back_ref.at[col], own_sem.at[0])

    mirror.start_1()
    for copy in first:
        copy.start()
    own.start()
    third = (len(bulk) + 2) // 3
    for copy in bulk[:third]:
        copy.start()

    mirror.finish()
    mirror.start_2()
    for copy in first:
        copy.wait()
    total = acc_ref[part(row), :]
    for k in range(row_devs - 1):
        total = total + rs_recv[k].astype(F32)
    cs_send[...] = total.astype(BF16).reshape(cs_send.shape)
    second = []
    for k, step in enumerate(order):
        to = moved(col, shape, step, 1)
        second.append(pltpu.make_async_remote_copy(
            src_ref=cs_send.at[to], dst_ref=cs_recv.at[k], send_sem=b_send.at[k],
            recv_sem=b_recv.at[k], device_id=(row, to), device_id_type=MESH))
    for copy in second:
        copy.start()
    for copy in bulk[third:2 * third]:
        copy.start()
    mirror.finish_2()
    mirror.start_3()
    for copy in second:
        copy.wait()
    mine = cs_send[col].astype(F32)
    for k in range(col_devs - 1):
        mine = mine + cs_recv[k].astype(F32)
    piece[...] = (mine * scale).astype(BF16)
    chunk[col] = piece[...]
    third_leg = []
    for k, step in enumerate(order):
        third_leg.append(pltpu.make_async_remote_copy(
            src_ref=piece, dst_ref=chunk.at[col], send_sem=c_send.at[k],
            recv_sem=c_recv.at[k], device_id=(row, moved(col, shape, step, 1)), device_id_type=MESH))
    for copy in third_leg:
        copy.start()
    for copy in bulk[2 * third:]:
        copy.start()
    for copy in third_leg:
        copy.wait()
    last = []
    for k in range(1, row_devs):
        last.append(pltpu.make_async_remote_copy(
            src_ref=chunk, dst_ref=sum_ref.at[row], send_sem=d_send.at[k - 1],
            recv_sem=d_recv.at[k - 1], device_id=(at_row(k), col), device_id_type=MESH))
    for copy in last:
        copy.start()
    own_sum = pltpu.make_async_copy(chunk, sum_ref.at[row], own_sem.at[1])
    own_sum.start()
    own_sum.wait()
    for copy in last:
        copy.wait()
    own.wait()
    mirror.finish()
    for copy in bulk:
        copy.wait()


def give_back(row_devs, col_devs, scale, ids, g, hs, acc):
    squares, feature, cells = g.shape
    bins = hs.shape[1]
    peers, xs = col_devs - 1, row_devs // 2
    slices = (xs, 2, hs.shape[0] // 2 // xs, bins, 128)
    hs = hs.reshape(2, xs, slices[2], bins, 128)
    rows_chunk = ROWS_SUM // row_devs
    rows_piece = rows_chunk // col_devs
    dma = lambda n: pltpu.SemaphoreType.DMA((n,))
    return pl.pallas_call(
        functools.partial(return_kernel, row_devs, col_devs, scale),
        name="give_back",
        out_shape=(
            jax.ShapeDtypeStruct((col_devs, CAP, feature, cells), BF16),
            jax.ShapeDtypeStruct(slices, BF16),
            jax.ShapeDtypeStruct((row_devs, col_devs, rows_piece, 128), BF16),
        ),
        in_specs=[smem(), vmem(), vmem(), vmem()],
        out_specs=(hbm(), hbm(), hbm()),
        scratch_shapes=[
            pltpu.VMEM((col_devs, CAP, feature, cells), BF16),
            pltpu.VMEM((ROWS_SUM, 128), BF16),
            pltpu.VMEM((row_devs - 1, rows_chunk, 128), BF16),
            pltpu.VMEM((col_devs, rows_piece, 128), BF16),
            pltpu.VMEM((col_devs - 1, rows_piece, 128), BF16),
            pltpu.VMEM((rows_piece, 128), BF16),
            pltpu.VMEM((col_devs, rows_piece, 128), BF16),
            pltpu.VMEM(slices, BF16),
            pltpu.VMEM(slices, BF16),
            dma(peers), dma(peers), dma(2),
            dma(row_devs - 1), dma(row_devs - 1), dma(peers), dma(peers),
            dma(peers), dma(peers), dma(row_devs - 1), dma(row_devs - 1),
        ] + mirror_sems(row_devs),
        compiler_params=pltpu.CompilerParams(
            collective_id=1, has_side_effects=True, vmem_limit_bytes=VMEM_LIMIT),
    )(ids, g, hs, acc)


def finish_kernel(hidden, slot_ref, back_ref, inv_ref, mir_ref, hl_ref, sum_ref,
                  tile_ref, log_ref, gt_ref, gg_ref, gu_ref, go_ref, gd_ref, gn_ref):
    step = pl.program_id(0)
    tile_ref[0] = (back_ref[0].astype(F32) * inv_ref[step]).astype(BF16)
    bins, lanes = hl_ref.shape[1:]
    low = lax.broadcasted_iota(jnp.int32, (bins, lanes), 1) < lanes // 2
    for k in range(mir_ref.shape[2]):
        a, b = mir_ref[0, 0, k].astype(F32), mir_ref[0, 1, k].astype(F32)
        even = jnp.where(low, a, pltpu.roll(b, lanes // 2, 1))
        odd = jnp.where(low, pltpu.roll(a, lanes // 2, 1), b)
        log_ref[2 * k] = (hl_ref[2 * k].astype(F32) + even).astype(BF16)
        log_ref[2 * k + 1] = (hl_ref[2 * k + 1].astype(F32) + odd).astype(BF16)

    @pl.when(step == 0)
    def _():
        width = sum_ref.shape[1]
        for k in range(hidden // width):
            span = slice(k * width, (k + 1) * width)
            gg_ref[:, span] = sum_ref[k * width:(k + 1) * width, :].astype(F32)
            gu_ref[:, span] = sum_ref[hidden + k * width:hidden + (k + 1) * width, :].astype(F32)
        go_ref[...] = sum_ref[2 * hidden:3 * hidden, :].astype(F32)
        at = 3 * hidden
        gd_ref[...] = sum_ref[at:at + gd_ref.shape[0], :].astype(F32)
        at += gd_ref.shape[0]
        gt_ref[...] = sum_ref[at:at + gt_ref.shape[0], :].astype(F32)
        at += gt_ref.shape[0]
        norm = sum_ref[at:at + 16, :].astype(F32)
        gn_ref[0:1, :] = jnp.sum(norm[0:8], axis=0, keepdims=True)
        gn_ref[1:2, :] = jnp.sum(norm[8:16], axis=0, keepdims=True)


def finish(hidden, slot_of, inv, back, mir, hl, sums):
    slots = slot_of.shape[0]
    feature, cells = back.shape[1:]
    cols, bins, rows = hl.shape
    width = sums.shape[1]
    per = cols // slots
    deep = mir.shape[2] // (per // 2)
    const = lambda shape: pl.BlockSpec(shape, lambda i, s: (0,) * len(shape))
    outs = [((slots, feature, cells), BF16), ((cols, bins, rows), BF16), ((feature, width), F32),
            ((width, hidden), F32), ((width, hidden), F32), ((hidden, width), F32), ((bins, width), F32),
            ((2, width), F32)]
    return pl.pallas_call(
        functools.partial(finish_kernel, hidden),
        name="finish",
        grid_spec=pltpu.PrefetchScalarGridSpec(
            num_scalar_prefetch=1,
            grid=(slots,),
            in_specs=[
                pl.BlockSpec((1, feature, cells), lambda i, s: (s[i], 0, 0)),
                pl.BlockSpec(memory_space=pltpu.SMEM),
                pl.BlockSpec((1, 2, per // 2, bins, rows), lambda i, s: (i // deep, 0, lax.rem(i, deep), 0, 0)),
                pl.BlockSpec((per, bins, rows), lambda i, s: (i, 0, 0)),
                const(sums.shape),
            ],
            out_specs=[
                pl.BlockSpec((1, feature, cells), lambda i, s: (i, 0, 0)),
                pl.BlockSpec((per, bins, rows), lambda i, s: (i, 0, 0)),
            ] + [const(shape) for shape, _ in outs[2:]],
        ),
        out_shape=[jax.ShapeDtypeStruct(shape, kind) for shape, kind in outs],
        compiler_params=pltpu.CompilerParams(
            dimension_semantics=("arbitrary",), vmem_limit_bytes=VMEM_LIMIT),
    )(slot_of, back, inv, mir, hl, sums)


def per_device(pair, logit_cotangent, tiles, tile_target, tile_square, tile_count, w_template,
               transition_norm_gain, transition_norm_bias, w_gate, w_up, w_out, w_dist):
    row_devs = lax.axis_size("row")
    col_devs = lax.axis_size("col")
    rows, cols, width = pair.shape
    length = rows * row_devs
    slots, cells_sq, feature = tiles.shape
    hidden = w_gate.shape[1]
    tiles_t = jnp.transpose(tiles, (0, 2, 1))
    cot_t = jnp.transpose(logit_cotangent, (1, 2, 0))
    target = tile_target[:, 0]
    places = jnp.arange(slots, dtype=jnp.int32)
    rank = jnp.sum((target[:, None] == target[None, :]) & (places[None, :] < places[:, None]),
                   axis=1, dtype=jnp.int32)
    slot_of = target * CAP + rank
    inv_count = 1.0 / tile_count.astype(F32)
    chosen = slot_of[None, :] == jnp.arange(col_devs * CAP, dtype=jnp.int32)[:, None]
    picked = chosen.astype(jnp.int32)
    idx = jnp.sum(picked * places[None, :], axis=1).reshape(col_devs, CAP)
    send_inv = jnp.sum(jnp.where(chosen, inv_count[None, :], 0.0), axis=1).reshape(col_devs, CAP)
    send_ids = (jnp.sum(picked * (tile_square + 1)[None, :], axis=1) - 1).reshape(col_devs, CAP)
    ids = jnp.broadcast_to(jnp.pad(send_ids, ((0, 0), (0, 128 - CAP)))[:, None, :], (col_devs, 8, 128))

    recv, got, mir = exchange(row_devs, col_devs, idx, send_inv, ids, tiles_t, cot_t)
    grad_pair, g, hs, hl, acc = compute(
        got, pair, recv, cot_t, mir, w_template, transition_norm_gain[None, :],
        transition_norm_bias[None, :], w_gate, w_up, w_out, w_dist.T)
    back, mir_heads, sums = give_back(row_devs, col_devs, 1.0 / length, got, g, hs, acc)
    grad_tiles_t, logits_t, g_template, g_gate, g_up, g_out, g_dist_t, g_norm = finish(
        hidden, slot_of, inv_count, back.reshape(col_devs * CAP, feature, cells_sq), mir_heads, hl,
        sums.reshape(ROWS_SUM, width))
    return (
        jnp.transpose(logits_t, (2, 0, 1)),
        grad_pair,
        jnp.transpose(grad_tiles_t, (0, 2, 1)),
        g_template,
        g_norm[0],
        g_norm[1],
        g_gate,
        g_up,
        g_out,
        g_dist_t.T,
    )


def solution(mesh):
    return jax.shard_map(
        per_device,
        mesh=mesh,
        in_specs=(
            P("row", "col", None),
            P("row", "col", None),
            P(("row", "col"), None, None),
            P(("row", "col"), None),
            P(("row", "col")),
            P(("row", "col")),
            P(), P(), P(), P(), P(), P(), P(),
        ),
        out_specs=(
            P("row", "col", None),
            P("row", "col", None),
            P(("row", "col"), None, None),
            P(), P(), P(), P(), P(), P(), P(),
        ),
        check_vma=False,
    )
```

```python
import functools

import jax
import jax.numpy as jnp
from jax import lax
from jax.experimental import pallas as pl
from jax.experimental.pallas import tpu as pltpu
from jax.sharding import PartitionSpec as P

SQ = 32
CAP = 2
MESH = pl.DeviceIdType.MESH
F32 = jnp.float32
BF16 = jnp.bfloat16
ROWS_SUM = 2048
VMEM_LIMIT = 60 * 1024 * 1024


def vmem():
    return pl.BlockSpec(memory_space=pltpu.VMEM)


def smem():
    return pl.BlockSpec(memory_space=pltpu.SMEM)


def hbm():
    return pl.BlockSpec(memory_space=pl.ANY)


def nn(a, b):
    return lax.dot_general(a, b, (((1,), (0,)), ((), ())), preferred_element_type=F32)


def nt(a, b):
    return lax.dot_general(a, b, (((1,), (1,)), ((), ())), preferred_element_type=F32)


def tn(a, b):
    return lax.dot_general(a, b, (((0,), (0,)), ((), ())), preferred_element_type=F32)


def displacements(col_devs):
    if col_devs != 16:
        return (1, col_devs), [(0, k) for k in range(1, col_devs)]
    order = [(0, 1), (1, 0), (0, 3), (3, 0), (1, 1), (3, 3), (1, 3), (3, 1),
             (0, 2), (2, 0), (1, 2), (2, 1), (3, 2), (2, 3), (2, 2)]
    return (4, 4), order


def moved(col, shape, step, sign):
    ys, zs = shape
    y = lax.rem(col // zs + sign * step[0] + ys, ys)
    z = lax.rem(lax.rem(col, zs) + sign * step[1] + zs, zs)
    return y * zs + z


class Place:
    def __init__(self, row_devs, col_devs):
        self.row, self.col = lax.axis_index("row"), lax.axis_index("col")
        self.xs, self.zs = row_devs // 2, col_devs // (row_devs // 2)
        self.x, self.k = self.row // 2, lax.rem(self.row, 2)
        self.y, self.z = self.col // self.zs, lax.rem(self.col, self.zs)

    def turn(self, value, by):
        return lax.rem(value + by, self.xs) if self.xs > 1 else value


class Mirror:
    def __init__(self, place, src, first, second, dst, sems):
        self.p, self.src, self.first, self.second, self.dst = place, src, first, second, dst
        self.s1, self.r1, self.s2, self.r2, self.s3, self.r3, self.own = sems

    def along_x(self, source, target, send, recv):
        p = self.p
        copies = []
        for n in range(1, p.xs):
            to = p.turn(p.x, n)
            copies.append(pltpu.make_async_remote_copy(
                src_ref=source(to), dst_ref=target.at[p.x], send_sem=send.at[n - 1], recv_sem=recv.at[n - 1],
                device_id=(2 * to + p.k, p.col), device_id_type=MESH))
        return copies

    def start_1(self):
        p = self.p
        self.copies = self.along_x(lambda to: self.src.at[:, to], self.first, self.s1, self.r1)
        for copy in self.copies:
            copy.start()
        self.local = pltpu.make_async_copy(self.src.at[:, p.x], self.first.at[p.x], self.own.at[0])
        self.local.start()

    def finish(self):
        self.local.wait()
        for copy in self.copies:
            copy.wait()

    finish_1 = finish_3 = finish

    def start_2(self):
        p = self.p
        self.plan = []
        for n in range(p.xs):
            to_y = p.turn(p.y, n)
            for h in (0, 1):
                to_z, to_k = 2 * p.k + h, p.z // 2
                source, target = self.first.at[to_y, h], self.second.at[p.y, lax.rem(p.z, 2)]
                slot = 2 * n + lax.rem(p.z, 2)
                remote = pltpu.make_async_remote_copy(
                    src_ref=source, dst_ref=target, send_sem=self.s2.at[2 * n + h], recv_sem=self.r2.at[slot],
                    device_id=(2 * p.x + to_k, to_y * p.zs + to_z), device_id_type=MESH)
                if n == 0:
                    here = jnp.logical_and(to_k == p.k, to_z == p.z)
                    local = pltpu.make_async_copy(source, target, self.r2.at[slot])
                    start_one(here, remote, local)
                    self.plan.append((here, remote))
                else:
                    remote.start()
                    self.plan.append((None, remote))

    def finish_2(self):
        for i, (here, remote) in enumerate(self.plan):
            if here is None:
                remote.wait_send()
            else:
                @pl.when(jnp.logical_not(here))
                def _():
                    remote.wait_send()
            ref = self.second.at[0, 0]
            pltpu.make_async_copy(ref, ref, self.r2.at[i]).wait()

    def start_3(self):
        p = self.p
        self.copies = self.along_x(lambda to: self.second.at[to], self.dst, self.s3, self.r3)
        for copy in self.copies:
            copy.start()
        self.local = pltpu.make_async_copy(self.second.at[p.x], self.dst.at[p.x], self.own.at[1])
        self.local.start()


def start_one(here, remote, local):
    @pl.when(jnp.logical_not(here))
    def _():
        remote.start()

    @pl.when(here)
    def _():
        local.start()


def mirror_sems(row_devs):
    xs = row_devs // 2
    dma = lambda n: pltpu.SemaphoreType.DMA((n,))
    return [dma(max(xs - 1, 1)), dma(max(xs - 1, 1)), dma(2 * xs), dma(2 * xs),
            dma(max(xs - 1, 1)), dma(max(xs - 1, 1)), dma(2)]


def greet(p, row_devs, col_devs):
    barrier = pltpu.get_barrier_semaphore()
    peers = 0
    for n in range(1, col_devs):
        pl.semaphore_signal(barrier, inc=1, device_id=(p.row, lax.rem(p.col + n, col_devs)), device_id_type=MESH)
        peers += 1
    for n in range(1, row_devs):
        pl.semaphore_signal(barrier, inc=1, device_id=(lax.rem(p.row + n, row_devs), p.col), device_id_type=MESH)
        peers += 1
    for n in range(1, col_devs):
        pl.semaphore_signal(
            barrier, inc=1, device_id=(2 * p.x + 1 - p.k, lax.rem(p.col + n, col_devs)), device_id_type=MESH)
        peers += 1
    return lambda: pl.semaphore_wait(barrier, peers)


BAND = 8
CHUNKS = SQ // BAND
SPAN = BAND * SQ
PART = 256


def window_kernel(row_devs, col_devs, scale, idx_ref, inv_ref, ids_ref, tiles_ref, cot_ref, pair_ref, wt_ref,
                  gain_ref, bias_ref, wg_ref, wu_ref, wo_ref, wd_ref,
                  back_ref, heads_ref, sum_ref, gp_ref, hl_ref, got_ref,
                  sendbuf, recv, names, onehot, s_ref, g_ref, pair_v, d_ref, z_ref, hs_ref,
                  pack, c_first, c_second, c_dst, h_first, h_second,
                  ag_ref, au_ref, ao_ref, ad_ref, at_ref, an_ref, acc_ref,
                  low, rs_recv, cs_send, cs_recv, piece, chunk,
                  pair_sem, out_sem, id_send, id_recv, t_send, t_recv, g_send, g_recv, own_t, own_g, own_sem,
                  a_send, a_recv, b_send, b_recv, e_send, e_recv, f_send, f_recv, *mirror_sem):
    p = Place(row_devs, col_devs)
    row, col = p.row, p.col
    shape, order = displacements(col_devs)
    rows, cols, width = pair_v.shape
    bins, feature, hidden = wd_ref.shape[0], wt_ref.shape[0], wg_ref.shape[1]
    sq_cols, sq_rows = cols // SQ, rows // SQ
    squares = sq_cols * sq_rows
    cells = BAND * cols
    greeted = greet(p, row_devs, col_devs)
    pair_in = pltpu.make_async_copy(pair_ref, pair_v, pair_sem.at[0])
    pair_in.start()

    lanes = rows
    left = lax.broadcasted_iota(jnp.int32, (bins, lanes), 1) < lanes // 2

    def pack_pair(n, carry):
        u, v = cot_ref[2 * n].astype(F32), cot_ref[2 * n + 1].astype(F32)
        m, t = n // pack.shape[2], lax.rem(n, pack.shape[2])
        pack[0, m, t] = jnp.where(left, u, pltpu.roll(v, lanes // 2, 1)).astype(BF16)
        pack[1, m, t] = jnp.where(left, pltpu.roll(u, lanes // 2, 1), v).astype(BF16)
        return carry

    lax.fori_loop(0, cols // 2, pack_pair, 0)

    def fill(d, carry):
        for k in range(CAP):
            tile = (tiles_ref[idx_ref[d, k]].astype(F32) * inv_ref[d, k]).astype(BF16)
            for q in range(CHUNKS):
                sendbuf[q, d, k] = tile[:, q * SPAN:(q + 1) * SPAN]
        return carry

    lax.fori_loop(0, col_devs, fill, 0)
    greeted()

    mirror = Mirror(p, pack, c_first, c_second, c_dst, mirror_sem[:7])
    mirror.start_1()

    def to_all(source, target, send, recv_sem):
        copies = []
        for n, step in enumerate(order):
            to = moved(col, shape, step, 1)
            copies.append(pltpu.make_async_remote_copy(
                src_ref=source(to), dst_ref=target(n), send_sem=send(n), recv_sem=recv_sem(n),
                device_id=(row, to), device_id_type=MESH))
        return copies

    def local(source, target, sem):
        copy = pltpu.make_async_copy(source, target, sem)
        copy.start()
        return copy

    id_copies = to_all(lambda to: ids_ref.at[to], lambda n: got_ref.at[col],
                       lambda n: id_send.at[n], lambda n: id_recv.at[n])
    for copy in id_copies:
        copy.start()
    own_id = local(ids_ref.at[col], got_ref.at[col], own_sem.at[0])
    tile_copies = []
    for q in range(CHUNKS):
        tile_copies.append(to_all(lambda to: sendbuf.at[q, to], lambda n: recv.at[q, col],
                                  lambda n: t_send.at[q, n], lambda n: t_recv.at[q, n]))
    own_tiles = [local(sendbuf.at[q, col], recv.at[q, col], own_t.at[q]) for q in range(CHUNKS)]
    for copy in tile_copies[0]:
        copy.start()

    for ref in (ag_ref, au_ref, ao_ref, ad_ref, at_ref, an_ref):
        ref[...] = jnp.zeros(ref.shape, F32)
    mirror.finish()
    mirror.start_2()
    for q in range(1, CHUNKS):
        for copy in tile_copies[q]:
            copy.start()

    def own_cot(j, carry):
        d_ref[pl.ds(j, rows, stride=cols), :] = cot_ref[j].astype(F32).T
        return carry

    lax.fori_loop(0, cols, own_cot, 0)
    own_id.wait()
    for copy in id_copies:
        copy.wait()
    to_smem = local(got_ref, names, own_sem.at[1])
    to_smem.wait()
    one_rows = lax.broadcasted_iota(jnp.int32, (squares * feature, CAP * feature), 0)
    one_cols = lax.broadcasted_iota(jnp.int32, (squares * feature, CAP * feature), 1)
    same = lax.rem(one_rows, feature) == lax.rem(one_cols, feature)
    square_of = one_rows // feature
    for d in range(col_devs):
        wanted = jnp.where(one_cols < feature, names[d, 0, 0], names[d, 0, 1])
        onehot[:, d * CAP * feature:(d + 1) * CAP * feature] = jnp.where(
            jnp.logical_and(same, square_of == wanted), 1.0, 0.0).astype(BF16)
    mirror.finish_2()
    mirror.start_3()
    mirror.finish()

    def mirrored(n, carry):
        at = pl.multiple_of(n * rows, rows)
        d_ref[pl.ds(at, rows), :] += c_dst[
            lax.rem(n, cols // 2) // c_dst.shape[2], n // (cols // 2), lax.rem(n, c_dst.shape[2])].astype(F32).T
        return carry

    lax.fori_loop(0, cols, mirrored, 0)
    pair_in.wait()

    def band(q, a, carry):
        row0 = a * SQ + q * BAND
        w_t = wt_ref[...]
        pieces = [s_ref[a * sq_cols + d] for d in range(sq_cols)]
        proj = jnp.concatenate(
            [tn(one, w_t).reshape(BAND, SQ, width) for one in pieces], axis=1).reshape(cells, width)
        z1 = pair_v[pl.ds(row0, BAND)].reshape(cells, width) + proj
        gain, bias = gain_ref[...], bias_ref[...]
        mean = jnp.mean(z1, axis=1, keepdims=True)
        centered = z1 - mean
        rdev = lax.rsqrt(jnp.mean(centered * centered, axis=1, keepdims=True) + 1e-5)
        xhat = centered * rdev
        normed = (xhat * gain + bias).astype(BF16)
        base = pl.multiple_of(row0 * cols, cells)
        dheads = d_ref[pl.ds(base, cells), :].astype(BF16)
        wd = wd_ref[...]
        dz2 = nn(dheads, wd)
        dzl = dz2.astype(BF16)
        normed_t = normed.T
        dzl_t = dzl.T
        z2 = z1
        dnorm = jnp.zeros((cells, width), F32)
        for k in range(hidden // PART):
            span = slice(k * PART, (k + 1) * PART)
            gate = nn(normed, wg_ref[:, span])
            up = nn(normed, wu_ref[:, span])
            dhid = nt(dzl, wo_ref[span, :])
            s = 0.5 * jnp.tanh(0.5 * gate) + 0.5
            swish = gate * s
            hid = (swish * up).astype(BF16)
            dup = (dhid * swish).astype(BF16)
            dgate = (dhid * up * (s + swish * (1.0 - s))).astype(BF16)
            z2 = z2 + nn(hid, wo_ref[span, :])
            dnorm = dnorm + nt(dgate, wg_ref[:, span]) + nt(dup, wu_ref[:, span])
            ao_ref[:, span] += nn(dzl_t, hid)
            ag_ref[:, span] += nn(normed_t, dgate)
            au_ref[:, span] += nn(normed_t, dup)
        z_ref[pl.ds(base, cells), :] = z2
        z2_low = z2.astype(BF16)
        heads_t = nt(wd, z2_low).astype(BF16)
        pairs = BAND // 2
        deep = pairs // p.xs
        for u in range(pairs):
            t = (q % 2 * 2 + lax.rem(a, 2)) * deep + u // p.xs
            hs_ref[q // 2, a // 2, u % p.xs, t] = heads_t[:, u * 128:(u + 1) * 128]
        ad_ref[...] += tn(dheads, z2_low)
        an_ref[0] += jnp.sum((dnorm * xhat).reshape(cells // 8, 8, width), axis=0)
        an_ref[1] += jnp.sum(dnorm.reshape(cells // 8, 8, width), axis=0)
        dx = dnorm * gain
        grad = dz2 + (dx - jnp.mean(dx, axis=1, keepdims=True)
                      - xhat * jnp.mean(dx * xhat, axis=1, keepdims=True)) * rdev
        grad3 = grad.reshape(BAND, cols, width)
        pair_v[pl.ds(row0, BAND)] = grad3
        total = jnp.zeros((feature, width), F32)
        for d in range(sq_cols):
            dproj = grad3[:, d * SQ:(d + 1) * SQ, :].reshape(SPAN, width).astype(BF16)
            g_ref[a * sq_cols + d] = nt(w_t, dproj).astype(BF16)
            total = total + nn(pieces[d], dproj)
        at_ref[...] += total
        return carry

    back_copies, own_back, pair_out = [], [], []
    halves = [Mirror(p, hs_ref.at[n], h_first.at[n], h_second.at[n], heads_ref.at[n],
                     mirror_sem[7 * (n + 1):7 * (n + 2)]) for n in range(2)]
    for q in range(CHUNKS):
        own_tiles[q].wait()
        for copy in tile_copies[q]:
            copy.wait()
        s_ref[...] = nn(onehot[...], recv[q].reshape(col_devs * CAP * feature, SPAN)).astype(BF16).reshape(
            s_ref.shape)
        lax.fori_loop(0, sq_rows, functools.partial(band, q), 0)

        def take(d, carry):
            for k in range(CAP):
                sendbuf[q, d, k] = g_ref[jnp.maximum(names[d, 0, k], 0)]
            return carry

        lax.fori_loop(0, col_devs, take, 0)
        for a in range(sq_rows):
            part_rows = pl.ds(a * SQ + q * BAND, BAND)
            pair_out.append(local(pair_v.at[part_rows], gp_ref.at[part_rows], out_sem.at[q * sq_rows + a]))
        if q == 1:
            halves[0].start_1()
        if q == 2:
            halves[0].finish()
            halves[0].start_2()
        if q == 3:
            halves[0].finish_2()
            halves[0].start_3()
            halves[1].start_1()
        back_copies.append(to_all(lambda to: sendbuf.at[q, to], lambda n: back_ref.at[q, col],
                                  lambda n: g_send.at[q, n], lambda n: g_recv.at[q, n]))
        own_back.append(local(sendbuf.at[q, col], back_ref.at[q, col], own_g.at[q]))
        if q < CHUNKS - 1:
            for copy in back_copies[q]:
                copy.start()

    for k in range(hidden // width):
        span = slice(k * width, (k + 1) * width)
        acc_ref[k * width:(k + 1) * width, :] = ag_ref[:, span]
        acc_ref[hidden + k * width:hidden + (k + 1) * width, :] = au_ref[:, span]
        acc_ref[2 * hidden + k * width:2 * hidden + (k + 1) * width, :] = ao_ref[:, span].T
    tail = 3 * hidden
    acc_ref[tail:tail + bins, :] = ad_ref[...]
    tail += bins
    acc_ref[tail:tail + feature, :] = at_ref[...]
    tail += feature
    acc_ref[tail:tail + 8, :] = an_ref[0]
    acc_ref[tail + 8:tail + 16, :] = an_ref[1]
    acc_ref[tail + 16:, :] = jnp.zeros((ROWS_SUM - tail - 16, width), F32)
    low[...] = acc_ref[...].astype(BF16)
    rows_chunk = ROWS_SUM // row_devs

    def part(r):
        return pl.ds(pl.multiple_of(r * rows_chunk, rows_chunk), rows_chunk)

    first = []
    for k in range(1, row_devs):
        to = lax.rem(row + k, row_devs)
        first.append(pltpu.make_async_remote_copy(
            src_ref=low.at[part(to)], dst_ref=rs_recv.at[k - 1], send_sem=a_send.at[k - 1],
            recv_sem=a_recv.at[k - 1], device_id=(to, col), device_id_type=MESH))
    for copy in first:
        copy.start()
    bulk = back_copies[-1]
    third = (len(bulk) + 2) // 3
    for copy in bulk[:third]:
        copy.start()

    wd = wd_ref[...]

    def local_heads(j, carry):
        zj = z_ref[pl.ds(j, rows, stride=cols), :].astype(BF16)
        hl_ref[j] = nt(wd, zj).astype(BF16)
        return carry

    lax.fori_loop(0, cols, local_heads, 0)
    halves[1].finish_1()
    halves[1].start_2()
    for copy in first:
        copy.wait()
    total = acc_ref[part(row), :]
    for k in range(row_devs - 1):
        total = total + rs_recv[k].astype(F32)
    cs_send[...] = total.astype(BF16).reshape(cs_send.shape)
    second = to_all(lambda to: cs_send.at[to], lambda n: cs_recv.at[n],
                    lambda n: b_send.at[n], lambda n: b_recv.at[n])
    for copy in second:
        copy.start()
    for copy in bulk[third:2 * third]:
        copy.start()
    for copy in second:
        copy.wait()
    mine = cs_send[col].astype(F32)
    for k in range(col_devs - 1):
        mine = mine + cs_recv[k].astype(F32)
    piece[...] = (mine * scale).astype(BF16)
    chunk[col] = piece[...]
    gather = to_all(lambda to: piece, lambda n: chunk.at[col], lambda n: e_send.at[n], lambda n: e_recv.at[n])
    for copy in gather:
        copy.start()
    for copy in bulk[2 * third:]:
        copy.start()
    halves[1].finish_2()
    halves[1].start_3()
    for copy in gather:
        copy.wait()
    last = []
    for k in range(1, row_devs):
        last.append(pltpu.make_async_remote_copy(
            src_ref=chunk, dst_ref=sum_ref.at[row], send_sem=f_send.at[k - 1],
            recv_sem=f_recv.at[k - 1], device_id=(lax.rem(row + k, row_devs), col), device_id_type=MESH))
    for copy in last:
        copy.start()
    local(chunk, sum_ref.at[row], own_sem.at[2]).wait()
    for copy in pair_out:
        copy.wait()
    halves[0].finish_3()
    for copy in last:
        copy.wait()
    halves[1].finish_3()
    for q in range(CHUNKS):
        own_back[q].wait()
        for copy in back_copies[q]:
            copy.wait()


def window(row_devs, col_devs, scale, idx, inv, ids, tiles_t, cot_t, pair, *weights):
    slots, feature, cells_sq = tiles_t.shape
    cols, bins, rows = cot_t.shape
    width = pair.shape[2]
    hidden = weights[3].shape[1]
    squares = rows // SQ * (cols // SQ)
    peers, xs = col_devs - 1, row_devs // 2
    rows_chunk = ROWS_SUM // row_devs
    rows_piece = rows_chunk // col_devs
    dma = lambda *n: pltpu.SemaphoreType.DMA(n)
    slices = (2, xs, cols // 2 // xs, bins, rows)
    cot_slices = (xs, 2) + slices[2:]
    head_deep = cols // 4 // xs
    heads = (2, xs, 2, head_deep, bins, 128)
    return pl.pallas_call(
        functools.partial(window_kernel, row_devs, col_devs, scale),
        name="window",
        out_shape=(
            jax.ShapeDtypeStruct((CHUNKS, col_devs, CAP, feature, SPAN), BF16),
            jax.ShapeDtypeStruct(heads, BF16),
            jax.ShapeDtypeStruct((row_devs, col_devs, rows_piece, 128), BF16),
            jax.ShapeDtypeStruct(pair.shape, F32),
            jax.ShapeDtypeStruct((cols, bins, rows), BF16),
            jax.ShapeDtypeStruct((col_devs, 8, 128), jnp.int32),
        ),
        in_specs=[smem(), smem(), vmem(), vmem(), vmem(), hbm()] + [vmem()] * len(weights),
        out_specs=(hbm(), hbm(), hbm(), hbm(), vmem(), hbm()),
        scratch_shapes=[
            pltpu.VMEM((CHUNKS, col_devs, CAP, feature, SPAN), BF16),
            pltpu.VMEM((CHUNKS, col_devs, CAP, feature, SPAN), BF16),
            pltpu.SMEM((col_devs, 8, 128), jnp.int32),
            pltpu.VMEM((squares * feature, col_devs * CAP * feature), BF16),
            pltpu.VMEM((squares, feature, SPAN), BF16),
            pltpu.VMEM((squares, feature, SPAN), BF16),
            pltpu.VMEM((rows, cols, width), F32),
            pltpu.VMEM((rows * cols, bins), F32),
            pltpu.VMEM((rows * cols, width), F32),
            pltpu.VMEM((2, 2, xs, head_deep, bins, 128), BF16),
            pltpu.VMEM(slices, BF16),
            pltpu.VMEM(cot_slices, BF16),
            pltpu.VMEM(cot_slices, BF16),
            pltpu.VMEM(cot_slices, BF16),
            pltpu.VMEM(heads, BF16),
            pltpu.VMEM(heads, BF16),
            pltpu.VMEM((width, hidden), F32),
            pltpu.VMEM((width, hidden), F32),
            pltpu.VMEM((width, hidden), F32),
            pltpu.VMEM((bins, width), F32),
            pltpu.VMEM((feature, width), F32),
            pltpu.VMEM((2, 8, width), F32),
            pltpu.VMEM((ROWS_SUM, 128), F32),
            pltpu.VMEM((ROWS_SUM, 128), BF16),
            pltpu.VMEM((row_devs - 1, rows_chunk, 128), BF16),
            pltpu.VMEM((col_devs, rows_piece, 128), BF16),
            pltpu.VMEM((col_devs - 1, rows_piece, 128), BF16),
            pltpu.VMEM((rows_piece, 128), BF16),
            pltpu.VMEM((col_devs, rows_piece, 128), BF16),
            dma(1), dma(rows // BAND), dma(peers), dma(peers),
            dma(CHUNKS, peers), dma(CHUNKS, peers), dma(CHUNKS, peers), dma(CHUNKS, peers),
            dma(CHUNKS), dma(CHUNKS), dma(3),
            dma(row_devs - 1), dma(row_devs - 1), dma(peers), dma(peers),
            dma(peers), dma(peers), dma(row_devs - 1), dma(row_devs - 1),
        ] + mirror_sems(row_devs) * 3,
        compiler_params=pltpu.CompilerParams(
            collective_id=0, has_side_effects=True, vmem_limit_bytes=VMEM_LIMIT),
    )(idx, inv, ids, tiles_t, cot_t, pair, *weights)


def finish_kernel(hidden, slot_ref, back_ref, inv_ref, mir_ref, hl_ref, sum_ref,
                  tile_ref, log_ref, gt_ref, gg_ref, gu_ref, go_ref, gd_ref, gn_ref):
    step = pl.program_id(0)
    span = back_ref.shape[3]
    for q in range(back_ref.shape[0]):
        tile_ref[0, :, q * span:(q + 1) * span] = (back_ref[q, 0].astype(F32) * inv_ref[step]).astype(BF16)
    per, bins, lanes = hl_ref.shape
    xs = mir_ref.shape[1]
    pairs = BAND // 2
    low = lax.broadcasted_iota(jnp.int32, (bins, lanes), 1) < lanes // 2
    for k in range(per // 2):
        n = step * (per // 2) + k
        u, q, a = lax.rem(n, pairs), lax.rem(n // pairs, CHUNKS), n // (pairs * CHUNKS)
        m, t = lax.rem(u, xs), (lax.rem(q, 2) * 2 + a) * (pairs // xs) + u // xs
        a, b = mir_ref[q // 2, m, 0, t].astype(F32), mir_ref[q // 2, m, 1, t].astype(F32)
        even = jnp.where(low, a, pltpu.roll(b, lanes // 2, 1))
        odd = jnp.where(low, pltpu.roll(a, lanes // 2, 1), b)
        log_ref[2 * k] = (hl_ref[2 * k].astype(F32) + even).astype(BF16)
        log_ref[2 * k + 1] = (hl_ref[2 * k + 1].astype(F32) + odd).astype(BF16)

    @pl.when(step == 0)
    def _():
        width = sum_ref.shape[1]
        for k in range(hidden // width):
            span = slice(k * width, (k + 1) * width)
            gg_ref[:, span] = sum_ref[k * width:(k + 1) * width, :].astype(F32)
            gu_ref[:, span] = sum_ref[hidden + k * width:hidden + (k + 1) * width, :].astype(F32)
        go_ref[...] = sum_ref[2 * hidden:3 * hidden, :].astype(F32)
        at = 3 * hidden
        gd_ref[...] = sum_ref[at:at + gd_ref.shape[0], :].astype(F32)
        at += gd_ref.shape[0]
        gt_ref[...] = sum_ref[at:at + gt_ref.shape[0], :].astype(F32)
        at += gt_ref.shape[0]
        norm = sum_ref[at:at + 16, :].astype(F32)
        gn_ref[0:1, :] = jnp.sum(norm[0:8], axis=0, keepdims=True)
        gn_ref[1:2, :] = jnp.sum(norm[8:16], axis=0, keepdims=True)


def finish(hidden, slot_of, inv, back, mir, hl, sums):
    slots = slot_of.shape[0]
    feature, cells = back.shape[2], back.shape[0] * back.shape[3]
    cols, bins, rows = hl.shape
    width = sums.shape[1]
    per = cols // slots
    const = lambda shape: pl.BlockSpec(shape, lambda i, s: (0,) * len(shape))
    outs = [((slots, feature, cells), BF16), ((cols, bins, rows), BF16), ((feature, width), F32),
            ((width, hidden), F32), ((width, hidden), F32), ((hidden, width), F32), ((bins, width), F32),
            ((2, width), F32)]
    return pl.pallas_call(
        functools.partial(finish_kernel, hidden),
        name="finish",
        grid_spec=pltpu.PrefetchScalarGridSpec(
            num_scalar_prefetch=1,
            grid=(slots,),
            in_specs=[
                pl.BlockSpec((back.shape[0], 1, feature, back.shape[3]), lambda i, s: (0, s[i], 0, 0)),
                pl.BlockSpec(memory_space=pltpu.SMEM),
                const(mir.shape),
                pl.BlockSpec((per, bins, rows), lambda i, s: (i, 0, 0)),
                const(sums.shape),
            ],
            out_specs=[
                pl.BlockSpec((1, feature, cells), lambda i, s: (i, 0, 0)),
                pl.BlockSpec((per, bins, rows), lambda i, s: (i, 0, 0)),
            ] + [const(shape) for shape, _ in outs[2:]],
        ),
        out_shape=[jax.ShapeDtypeStruct(shape, kind) for shape, kind in outs],
        compiler_params=pltpu.CompilerParams(
            dimension_semantics=("arbitrary",), vmem_limit_bytes=VMEM_LIMIT),
    )(slot_of, back, inv, mir, hl, sums)


def per_device(pair, logit_cotangent, tiles, tile_target, tile_square, tile_count, w_template,
               transition_norm_gain, transition_norm_bias, w_gate, w_up, w_out, w_dist):
    row_devs = lax.axis_size("row")
    col_devs = lax.axis_size("col")
    rows, cols, width = pair.shape
    length = rows * row_devs
    slots, cells_sq, feature = tiles.shape
    hidden = w_gate.shape[1]
    tiles_t = jnp.transpose(tiles, (0, 2, 1))
    cot_t = jnp.transpose(logit_cotangent, (1, 2, 0))
    target = tile_target[:, 0]
    places = jnp.arange(slots, dtype=jnp.int32)
    rank = jnp.sum((target[:, None] == target[None, :]) & (places[None, :] < places[:, None]),
                   axis=1, dtype=jnp.int32)
    slot_of = target * CAP + rank
    inv_count = 1.0 / tile_count.astype(F32)
    chosen = slot_of[None, :] == jnp.arange(col_devs * CAP, dtype=jnp.int32)[:, None]
    picked = chosen.astype(jnp.int32)
    idx = jnp.sum(picked * places[None, :], axis=1).reshape(col_devs, CAP)
    send_inv = jnp.sum(jnp.where(chosen, inv_count[None, :], 0.0), axis=1).reshape(col_devs, CAP)
    send_ids = (jnp.sum(picked * (tile_square + 1)[None, :], axis=1) - 1).reshape(col_devs, CAP)
    ids = jnp.broadcast_to(jnp.pad(send_ids, ((0, 0), (0, 128 - CAP)))[:, None, :], (col_devs, 8, 128))

    back, mir_heads, sums, grad_pair, hl, _ = window(
        row_devs, col_devs, 1.0 / length, idx, send_inv, ids, tiles_t, cot_t, pair, w_template,
        transition_norm_gain[None, :], transition_norm_bias[None, :], w_gate, w_up, w_out, w_dist.T)
    grad_tiles_t, logits_t, g_template, g_gate, g_up, g_out, g_dist_t, g_norm = finish(
        hidden, slot_of, inv_count, back.reshape(CHUNKS, col_devs * CAP, feature, SPAN), mir_heads, hl,
        sums.reshape(ROWS_SUM, width))
    return (
        jnp.transpose(logits_t, (2, 0, 1)),
        grad_pair,
        jnp.transpose(grad_tiles_t, (0, 2, 1)),
        g_template,
        g_norm[0],
        g_norm[1],
        g_gate,
        g_up,
        g_out,
        g_dist_t.T,
    )


def solution(mesh):
    return jax.shard_map(
        per_device,
        mesh=mesh,
        in_specs=(
            P("row", "col", None),
            P("row", "col", None),
            P(("row", "col"), None, None),
            P(("row", "col"), None),
            P(("row", "col")),
            P(("row", "col")),
            P(), P(), P(), P(), P(), P(), P(),
        ),
        out_specs=(
            P("row", "col", None),
            P("row", "col", None),
            P(("row", "col"), None, None),
            P(), P(), P(), P(), P(), P(), P(),
        ),
        check_vma=False,
    )
```

```python
import functools

import jax
import jax.numpy as jnp
from jax import lax
from jax.experimental import pallas as pl
from jax.experimental.pallas import tpu as pltpu
from jax.sharding import PartitionSpec as P

SQ = 32
CAP = 2
MESH = pl.DeviceIdType.MESH
F32 = jnp.float32
BF16 = jnp.bfloat16
ROWS_SUM = 2048
VMEM_LIMIT = 60 * 1024 * 1024


def vmem():
    return pl.BlockSpec(memory_space=pltpu.VMEM)


def smem():
    return pl.BlockSpec(memory_space=pltpu.SMEM)


def hbm():
    return pl.BlockSpec(memory_space=pl.ANY)


def nn(a, b):
    return lax.dot_general(a, b, (((1,), (0,)), ((), ())), preferred_element_type=F32)


def nt(a, b):
    return lax.dot_general(a, b, (((1,), (1,)), ((), ())), preferred_element_type=F32)


def tn(a, b):
    return lax.dot_general(a, b, (((0,), (0,)), ((), ())), preferred_element_type=F32)


def displacements(col_devs):
    if col_devs != 16:
        return (1, col_devs), [(0, k) for k in range(1, col_devs)]
    order = [(0, 1), (1, 0), (0, 3), (3, 0), (1, 1), (3, 3), (1, 3), (3, 1),
             (0, 2), (2, 0), (1, 2), (2, 1), (3, 2), (2, 3), (2, 2)]
    return (4, 4), order


def moved(col, shape, step, sign):
    ys, zs = shape
    y = lax.rem(col // zs + sign * step[0] + ys, ys)
    z = lax.rem(lax.rem(col, zs) + sign * step[1] + zs, zs)
    return y * zs + z


class Place:
    def __init__(self, row_devs, col_devs):
        self.row, self.col = lax.axis_index("row"), lax.axis_index("col")
        self.xs, self.zs = row_devs // 2, col_devs // (row_devs // 2)
        self.x, self.k = self.row // 2, lax.rem(self.row, 2)
        self.y, self.z = self.col // self.zs, lax.rem(self.col, self.zs)

    def turn(self, value, by):
        return lax.rem(value + by, self.xs) if self.xs > 1 else value


class Mirror:
    def __init__(self, place, src, first, second, dst, sems):
        self.p, self.src, self.first, self.second, self.dst = place, src, first, second, dst
        self.s1, self.r1, self.s2, self.r2, self.s3, self.r3, self.own = sems

    def along_x(self, source, target, send, recv):
        p = self.p
        copies = []
        for n in range(1, p.xs):
            to = p.turn(p.x, n)
            copies.append(pltpu.make_async_remote_copy(
                src_ref=source(to), dst_ref=target.at[p.x], send_sem=send.at[n - 1], recv_sem=recv.at[n - 1],
                device_id=(2 * to + p.k, p.col), device_id_type=MESH))
        return copies

    def start_1(self):
        p = self.p
        self.copies = self.along_x(lambda to: self.src.at[:, to], self.first, self.s1, self.r1)
        for copy in self.copies:
            copy.start()
        self.local = pltpu.make_async_copy(self.src.at[:, p.x], self.first.at[p.x], self.own.at[0])
        self.local.start()

    def finish(self):
        self.local.wait()
        for copy in self.copies:
            copy.wait()

    finish_1 = finish_3 = finish

    def start_2(self):
        p = self.p
        self.plan = []
        for n in range(p.xs):
            to_y = p.turn(p.y, n)
            for h in (0, 1):
                to_z, to_k = 2 * p.k + h, p.z // 2
                source, target = self.first.at[to_y, h], self.second.at[p.y, lax.rem(p.z, 2)]
                slot = 2 * n + lax.rem(p.z, 2)
                remote = pltpu.make_async_remote_copy(
                    src_ref=source, dst_ref=target, send_sem=self.s2.at[2 * n + h], recv_sem=self.r2.at[slot],
                    device_id=(2 * p.x + to_k, to_y * p.zs + to_z), device_id_type=MESH)
                if n == 0:
                    here = jnp.logical_and(to_k == p.k, to_z == p.z)
                    local = pltpu.make_async_copy(source, target, self.r2.at[slot])
                    start_one(here, remote, local)
                    self.plan.append((here, remote))
                else:
                    remote.start()
                    self.plan.append((None, remote))

    def finish_2(self):
        for i, (here, remote) in enumerate(self.plan):
            if here is None:
                remote.wait_send()
            else:
                @pl.when(jnp.logical_not(here))
                def _():
                    remote.wait_send()
            ref = self.second.at[0, 0]
            pltpu.make_async_copy(ref, ref, self.r2.at[i]).wait()

    def start_3(self):
        p = self.p
        self.copies = self.along_x(lambda to: self.second.at[to], self.dst, self.s3, self.r3)
        for copy in self.copies:
            copy.start()
        self.local = pltpu.make_async_copy(self.second.at[p.x], self.dst.at[p.x], self.own.at[1])
        self.local.start()


def start_one(here, remote, local):
    @pl.when(jnp.logical_not(here))
    def _():
        remote.start()

    @pl.when(here)
    def _():
        local.start()


def mirror_sems(row_devs):
    xs = row_devs // 2
    dma = lambda n: pltpu.SemaphoreType.DMA((n,))
    return [dma(max(xs - 1, 1)), dma(max(xs - 1, 1)), dma(2 * xs), dma(2 * xs),
            dma(max(xs - 1, 1)), dma(max(xs - 1, 1)), dma(2)]


def greet(p, row_devs, col_devs):
    barrier = pltpu.get_barrier_semaphore()
    peers = 0
    for n in range(1, col_devs):
        pl.semaphore_signal(barrier, inc=1, device_id=(p.row, lax.rem(p.col + n, col_devs)), device_id_type=MESH)
        peers += 1
    for n in range(1, row_devs):
        pl.semaphore_signal(barrier, inc=1, device_id=(lax.rem(p.row + n, row_devs), p.col), device_id_type=MESH)
        peers += 1
    for n in range(1, col_devs):
        pl.semaphore_signal(
            barrier, inc=1, device_id=(2 * p.x + 1 - p.k, lax.rem(p.col + n, col_devs)), device_id_type=MESH)
        peers += 1
    return lambda: pl.semaphore_wait(barrier, peers)


BAND = 8
CHUNKS = SQ // BAND
SPAN = BAND * SQ
PART = 256


def share(count):
    inv = jnp.where(count == 1, 1.0, jnp.where(count == 2, 0.5, jnp.where(count == 3, 1.0 / 3.0, 0.25)))
    return jnp.where(count == 0, 0.0, inv).astype(F32)


def pair_place(n, xs):
    u, q, a = lax.rem(n, BAND // 2), lax.rem(n // (BAND // 2), CHUNKS), n // (BAND // 2 * CHUNKS)
    return q // 2, lax.rem(u, xs), (lax.rem(q, 2) * 2 + a) * (BAND // 2 // xs) + u // xs


def window_kernel(row_devs, col_devs, scale, code_ref, tiles_ref, cot_ref, pair_ref, wt_ref,
                  gain_ref, bias_ref, wg_ref, wu_ref, wo_ref, wd_ref,
                  back_ref, heads_ref, sum_ref, gp_ref, hl_ref, got_ref,
                  ids_ref, sendbuf, recv, names, onehot, s_ref, g_ref, pair_v, d_ref, z_ref, hs_ref,
                  pack, c_first, c_second, c_dst, h_first, h_second,
                  ag_ref, au_ref, ao_ref, ad_ref, at_ref, an_ref, acc_ref,
                  low, rs_recv, cs_send, cs_recv, piece, chunk,
                  pair_sem, out_sem, id_send, id_recv, t_send, t_recv, g_send, g_recv, own_t, own_g, own_sem,
                  a_send, a_recv, b_send, b_recv, e_send, e_recv, f_send, f_recv, *mirror_sem):
    p = Place(row_devs, col_devs)
    row, col = p.row, p.col
    shape, order = displacements(col_devs)
    rows, cols, width = pair_v.shape
    bins, feature, hidden = wd_ref.shape[0], wt_ref.shape[0], wg_ref.shape[1]
    sq_cols, sq_rows = cols // SQ, rows // SQ
    squares = sq_cols * sq_rows
    cells = BAND * cols
    greeted = greet(p, row_devs, col_devs)
    pair_in = pltpu.make_async_copy(pair_ref, pair_v, pair_sem.at[0])
    pair_in.start()

    lanes = rows
    left = lax.broadcasted_iota(jnp.int32, (bins, lanes), 1) < lanes // 2

    def pack_pair(n, carry):
        u, v = cot_ref[2 * n].astype(F32), cot_ref[2 * n + 1].astype(F32)
        half, m, t = pair_place(n, p.xs)
        pack[half, 0, m, t] = jnp.where(left, u, pltpu.roll(v, lanes // 2, 1)).astype(BF16)
        pack[half, 1, m, t] = jnp.where(left, pltpu.roll(u, lanes // 2, 1), v).astype(BF16)
        return carry

    lax.fori_loop(0, cols // 2, pack_pair, 0)

    def fill(parts, d, carry):
        for k in range(CAP):
            code = code_ref[d, k]
            at, inv = jnp.bitwise_and(code, 255), share(code // 65536)
            for q in parts:
                sendbuf[q, d, k] = (
                    tiles_ref[at, :, q * SPAN:(q + 1) * SPAN].astype(F32) * inv).astype(BF16)
        return carry

    lax.fori_loop(0, col_devs, functools.partial(fill, (0,)), 0)
    id_lane = lax.broadcasted_iota(jnp.int32, (8, 128), 1)
    for d in range(col_devs):
        ids_ref[d] = jnp.where(id_lane == 0, code_ref[d, 0], code_ref[d, 1])
    greeted()

    mirrors = [Mirror(p, pack.at[n], c_first.at[n], c_second.at[n], c_dst.at[n], mirror_sem[7 * n:7 * (n + 1)])
               for n in range(2)]
    mirrors[0].start_1()

    def to_all(source, target, send, recv_sem):
        copies = []
        for n, step in enumerate(order):
            to = moved(col, shape, step, 1)
            copies.append(pltpu.make_async_remote_copy(
                src_ref=source(to), dst_ref=target(n), send_sem=send(n), recv_sem=recv_sem(n),
                device_id=(row, to), device_id_type=MESH))
        return copies

    def local(source, target, sem):
        copy = pltpu.make_async_copy(source, target, sem)
        copy.start()
        return copy

    id_copies = to_all(lambda to: ids_ref.at[to], lambda n: got_ref.at[col],
                       lambda n: id_send.at[n], lambda n: id_recv.at[n])
    for copy in id_copies:
        copy.start()
    own_id = local(ids_ref.at[col], got_ref.at[col], own_sem.at[0])
    tile_copies = []
    for q in range(CHUNKS):
        tile_copies.append(to_all(lambda to: sendbuf.at[q, to], lambda n: recv.at[q, col],
                                  lambda n: t_send.at[q, n], lambda n: t_recv.at[q, n]))
    ahead = len(order) // 2
    for copy in tile_copies[0][:ahead]:
        copy.start()
    mirrors[1].start_1()
    lax.fori_loop(0, col_devs, functools.partial(fill, tuple(range(1, CHUNKS))), 0)
    own_tiles = [local(sendbuf.at[q, col], recv.at[q, col], own_t.at[q]) for q in range(CHUNKS)]
    for ref in (ag_ref, au_ref, ao_ref, ad_ref, at_ref, an_ref):
        ref[...] = jnp.zeros(ref.shape, F32)
    mirrors[0].finish_1()
    mirrors[0].start_2()
    for copy in tile_copies[0][ahead:] + tile_copies[1]:
        copy.start()

    def own_cot(j, carry):
        d_ref[pl.ds(j, rows, stride=cols), :] = cot_ref[j].astype(F32).T
        return carry

    lax.fori_loop(0, cols, own_cot, 0)
    own_id.wait()
    for copy in id_copies:
        copy.wait()
    local(got_ref, names, own_sem.at[1]).wait()

    def square(d, k):
        return jnp.bitwise_and(names[d, 0, k] // 256, 255) - 1

    one_rows = lax.broadcasted_iota(jnp.int32, (squares * feature, CAP * feature), 0)
    one_cols = lax.broadcasted_iota(jnp.int32, (squares * feature, CAP * feature), 1)
    same = lax.rem(one_rows, feature) == lax.rem(one_cols, feature)
    square_of = one_rows // feature
    for d in range(col_devs):
        wanted = jnp.where(one_cols < feature, square(d, 0), square(d, 1))
        onehot[:, d * CAP * feature:(d + 1) * CAP * feature] = jnp.where(
            jnp.logical_and(same, square_of == wanted), 1.0, 0.0).astype(BF16)
    mirrors[1].finish_1()
    mirrors[1].start_2()
    for copy in tile_copies[2] + tile_copies[3]:
        copy.start()
    mirrors[0].finish_2()
    mirrors[0].start_3()

    def mirrored(half, r, carry):
        parity, r = r // (cols // 4), lax.rem(r, cols // 4)
        n = r // BAND * (2 * BAND) + half * BAND + lax.rem(r, BAND)
        _, m, t = pair_place(n, p.xs)
        at = pl.multiple_of((parity * (cols // 2) + n) * rows, rows)
        d_ref[pl.ds(at, rows), :] += c_dst[half, m, parity, t].astype(F32).T
        return carry

    mirrors[0].finish_3()
    lax.fori_loop(0, cols // 2, functools.partial(mirrored, 0), 0)
    pair_in.wait()

    def band(q, a, carry):
        row0 = a * SQ + q * BAND
        w_t = wt_ref[...]
        pieces = [s_ref[a * sq_cols + d] for d in range(sq_cols)]
        proj = jnp.concatenate(
            [tn(one, w_t).reshape(BAND, SQ, width) for one in pieces], axis=1).reshape(cells, width)
        z1 = pair_v[pl.ds(row0, BAND)].reshape(cells, width) + proj
        gain, bias = gain_ref[...], bias_ref[...]
        mean = jnp.mean(z1, axis=1, keepdims=True)
        centered = z1 - mean
        rdev = lax.rsqrt(jnp.mean(centered * centered, axis=1, keepdims=True) + 1e-5)
        xhat = centered * rdev
        normed = (xhat * gain + bias).astype(BF16)
        base = pl.multiple_of(row0 * cols, cells)
        dheads = d_ref[pl.ds(base, cells), :].astype(BF16)
        wd = wd_ref[...]
        dz2 = nn(dheads, wd)
        dzl = dz2.astype(BF16)
        normed_t = normed.T
        dzl_t = dzl.T
        z2 = z1
        dnorm = jnp.zeros((cells, width), F32)
        for k in range(hidden // PART):
            span = slice(k * PART, (k + 1) * PART)
            gate = nn(normed, wg_ref[:, span])
            up = nn(normed, wu_ref[:, span])
            dhid = nt(dzl, wo_ref[span, :])
            s = 0.5 * jnp.tanh(0.5 * gate) + 0.5
            swish = gate * s
            hid = (swish * up).astype(BF16)
            dup = (dhid * swish).astype(BF16)
            dgate = (dhid * up * (s + swish * (1.0 - s))).astype(BF16)
            z2 = z2 + nn(hid, wo_ref[span, :])
            dnorm = dnorm + nt(dgate, wg_ref[:, span]) + nt(dup, wu_ref[:, span])
            ao_ref[:, span] += nn(dzl_t, hid)
            ag_ref[:, span] += nn(normed_t, dgate)
            au_ref[:, span] += nn(normed_t, dup)
        z_ref[pl.ds(base, cells), :] = z2
        z2_low = z2.astype(BF16)
        heads_t = nt(wd, z2_low).astype(BF16)
        pairs = BAND // 2
        deep = pairs // p.xs
        for u in range(pairs):
            t = (q % 2 * 2 + lax.rem(a, 2)) * deep + u // p.xs
            hs_ref[q // 2, a // 2, u % p.xs, t] = heads_t[:, u * 128:(u + 1) * 128]
        ad_ref[...] += tn(dheads, z2_low)
        an_ref[0] += jnp.sum((dnorm * xhat).reshape(cells // 8, 8, width), axis=0)
        an_ref[1] += jnp.sum(dnorm.reshape(cells // 8, 8, width), axis=0)
        dx = dnorm * gain
        grad = dz2 + (dx - jnp.mean(dx, axis=1, keepdims=True)
                      - xhat * jnp.mean(dx * xhat, axis=1, keepdims=True)) * rdev
        grad3 = grad.reshape(BAND, cols, width)
        pair_v[pl.ds(row0, BAND)] = grad3
        total = jnp.zeros((feature, width), F32)
        for d in range(sq_cols):
            dproj = grad3[:, d * SQ:(d + 1) * SQ, :].reshape(SPAN, width).astype(BF16)
            g_ref[a * sq_cols + d] = nt(w_t, dproj).astype(BF16)
            total = total + nn(pieces[d], dproj)
        at_ref[...] += total
        return carry

    back_copies, own_back, pair_out = [], [], []
    halves = [Mirror(p, hs_ref.at[n], h_first.at[n], h_second.at[n], heads_ref.at[n],
                     mirror_sem[7 * (n + 2):7 * (n + 3)]) for n in range(2)]
    for q in range(CHUNKS):
        if q == 2:
            mirrors[1].finish_3()
            lax.fori_loop(0, cols // 2, functools.partial(mirrored, 1), 0)
        own_tiles[q].wait()
        for copy in tile_copies[q]:
            copy.wait()
        s_ref[...] = nn(onehot[...], recv[q].reshape(col_devs * CAP * feature, SPAN)).astype(BF16).reshape(
            s_ref.shape)
        lax.fori_loop(0, sq_rows, functools.partial(band, q), 0)

        def take(d, carry):
            for k in range(CAP):
                sendbuf[q, d, k] = g_ref[jnp.maximum(square(d, k), 0)]
            return carry

        lax.fori_loop(0, col_devs, take, 0)
        for a in range(sq_rows):
            part_rows = pl.ds(a * SQ + q * BAND, BAND)
            pair_out.append(local(pair_v.at[part_rows], gp_ref.at[part_rows], out_sem.at[q * sq_rows + a]))
        if q == 0:
            mirrors[1].finish_2()
            mirrors[1].start_3()
        if q == 1:
            halves[0].start_1()
        if q == 2:
            halves[0].finish()
            halves[0].start_2()
        if q == 3:
            halves[0].finish_2()
            halves[0].start_3()
            halves[1].start_1()
        back_copies.append(to_all(lambda to: sendbuf.at[q, to], lambda n: back_ref.at[q, col],
                                  lambda n: g_send.at[q, n], lambda n: g_recv.at[q, n]))
        own_back.append(local(sendbuf.at[q, col], back_ref.at[q, col], own_g.at[q]))
        if q < CHUNKS - 1:
            for copy in back_copies[q]:
                copy.start()

    for k in range(hidden // width):
        span = slice(k * width, (k + 1) * width)
        acc_ref[k * width:(k + 1) * width, :] = ag_ref[:, span]
        acc_ref[hidden + k * width:hidden + (k + 1) * width, :] = au_ref[:, span]
        acc_ref[2 * hidden + k * width:2 * hidden + (k + 1) * width, :] = ao_ref[:, span].T
    tail = 3 * hidden
    acc_ref[tail:tail + bins, :] = ad_ref[...]
    tail += bins
    acc_ref[tail:tail + feature, :] = at_ref[...]
    tail += feature
    acc_ref[tail:tail + 8, :] = an_ref[0]
    acc_ref[tail + 8:tail + 16, :] = an_ref[1]
    acc_ref[tail + 16:, :] = jnp.zeros((ROWS_SUM - tail - 16, width), F32)
    low[...] = acc_ref[...].astype(BF16)
    rows_chunk = ROWS_SUM // row_devs

    def part(r):
        return pl.ds(pl.multiple_of(r * rows_chunk, rows_chunk), rows_chunk)

    first = []
    for k in range(1, row_devs):
        to = lax.rem(row + k, row_devs)
        first.append(pltpu.make_async_remote_copy(
            src_ref=low.at[part(to)], dst_ref=rs_recv.at[k - 1], send_sem=a_send.at[k - 1],
            recv_sem=a_recv.at[k - 1], device_id=(to, col), device_id_type=MESH))
    for copy in first:
        copy.start()
    bulk = back_copies[-1]
    third = (len(bulk) + 2) // 3

    wd = wd_ref[...]

    def local_heads(j, carry):
        zj = z_ref[pl.ds(j, rows, stride=cols), :].astype(BF16)
        hl_ref[j] = nt(wd, zj).astype(BF16)
        return carry

    lax.fori_loop(0, cols, local_heads, 0)
    halves[1].finish_1()
    halves[1].start_2()
    for copy in first:
        copy.wait()
    total = acc_ref[part(row), :]
    for k in range(row_devs - 1):
        total = total + rs_recv[k].astype(F32)
    cs_send[...] = total.astype(BF16).reshape(cs_send.shape)
    second = to_all(lambda to: cs_send.at[to], lambda n: cs_recv.at[n],
                    lambda n: b_send.at[n], lambda n: b_recv.at[n])
    for copy in second:
        copy.start()
    for copy in bulk[:2 * third]:
        copy.start()
    for copy in second:
        copy.wait()
    mine = cs_send[col].astype(F32)
    for k in range(col_devs - 1):
        mine = mine + cs_recv[k].astype(F32)
    piece[...] = (mine * scale).astype(BF16)
    chunk[col] = piece[...]
    gather = to_all(lambda to: piece, lambda n: chunk.at[col], lambda n: e_send.at[n], lambda n: e_recv.at[n])
    for copy in gather:
        copy.start()
    for copy in bulk[2 * third:]:
        copy.start()
    halves[1].finish_2()
    halves[1].start_3()
    for copy in gather:
        copy.wait()
    last = []
    for k in range(1, row_devs):
        last.append(pltpu.make_async_remote_copy(
            src_ref=chunk, dst_ref=sum_ref.at[row], send_sem=f_send.at[k - 1],
            recv_sem=f_recv.at[k - 1], device_id=(lax.rem(row + k, row_devs), col), device_id_type=MESH))
    for copy in last:
        copy.start()
    local(chunk, sum_ref.at[row], own_sem.at[2]).wait()
    for copy in pair_out:
        copy.wait()
    halves[0].finish_3()
    for copy in last:
        copy.wait()
    halves[1].finish_3()
    for q in range(CHUNKS):
        own_back[q].wait()
        for copy in back_copies[q]:
            copy.wait()


def window(row_devs, col_devs, scale, code, tiles_t, cot_t, pair, *weights):
    slots, feature, cells_sq = tiles_t.shape
    cols, bins, rows = cot_t.shape
    width = pair.shape[2]
    hidden = weights[3].shape[1]
    squares = rows // SQ * (cols // SQ)
    peers, xs = col_devs - 1, row_devs // 2
    rows_chunk = ROWS_SUM // row_devs
    rows_piece = rows_chunk // col_devs
    dma = lambda *n: pltpu.SemaphoreType.DMA(n)
    deep = cols // 4 // xs
    slices = (2, 2, xs, deep, bins, rows)
    heads = (2, xs, 2, deep, bins, rows)
    return pl.pallas_call(
        functools.partial(window_kernel, row_devs, col_devs, scale),
        name="window",
        out_shape=(
            jax.ShapeDtypeStruct((CHUNKS, col_devs, CAP, feature, SPAN), BF16),
            jax.ShapeDtypeStruct(heads, BF16),
            jax.ShapeDtypeStruct((row_devs, col_devs, rows_piece, 128), BF16),
            jax.ShapeDtypeStruct(pair.shape, F32),
            jax.ShapeDtypeStruct((cols, bins, rows), BF16),
            jax.ShapeDtypeStruct((col_devs, 8, 128), jnp.int32),
        ),
        in_specs=[smem(), vmem(), vmem(), hbm()] + [vmem()] * len(weights),
        out_specs=(hbm(), hbm(), hbm(), hbm(), vmem(), hbm()),
        scratch_shapes=[
            pltpu.VMEM((col_devs, 8, 128), jnp.int32),
            pltpu.VMEM((CHUNKS, col_devs, CAP, feature, SPAN), BF16),
            pltpu.VMEM((CHUNKS, col_devs, CAP, feature, SPAN), BF16),
            pltpu.SMEM((col_devs, 8, 128), jnp.int32),
            pltpu.VMEM((squares * feature, col_devs * CAP * feature), BF16),
            pltpu.VMEM((squares, feature, SPAN), BF16),
            pltpu.VMEM((squares, feature, SPAN), BF16),
            pltpu.VMEM((rows, cols, width), F32),
            pltpu.VMEM((rows * cols, bins), F32),
            pltpu.VMEM((rows * cols, width), F32),
            pltpu.VMEM(slices, BF16),
            pltpu.VMEM(slices, BF16),
            pltpu.VMEM(heads, BF16),
            pltpu.VMEM(heads, BF16),
            pltpu.VMEM(heads, BF16),
            pltpu.VMEM(heads, BF16),
            pltpu.VMEM(heads, BF16),
            pltpu.VMEM((width, hidden), F32),
            pltpu.VMEM((width, hidden), F32),
            pltpu.VMEM((width, hidden), F32),
            pltpu.VMEM((bins, width), F32),
            pltpu.VMEM((feature, width), F32),
            pltpu.VMEM((2, 8, width), F32),
            pltpu.VMEM((ROWS_SUM, 128), F32),
            pltpu.VMEM((ROWS_SUM, 128), BF16),
            pltpu.VMEM((row_devs - 1, rows_chunk, 128), BF16),
            pltpu.VMEM((col_devs, rows_piece, 128), BF16),
            pltpu.VMEM((col_devs - 1, rows_piece, 128), BF16),
            pltpu.VMEM((rows_piece, 128), BF16),
            pltpu.VMEM((col_devs, rows_piece, 128), BF16),
            dma(1), dma(rows // BAND), dma(peers), dma(peers),
            dma(CHUNKS, peers), dma(CHUNKS, peers), dma(CHUNKS, peers), dma(CHUNKS, peers),
            dma(CHUNKS), dma(CHUNKS), dma(3),
            dma(row_devs - 1), dma(row_devs - 1), dma(peers), dma(peers),
            dma(peers), dma(peers), dma(row_devs - 1), dma(row_devs - 1),
        ] + mirror_sems(row_devs) * 4,
        compiler_params=pltpu.CompilerParams(
            collective_id=0, has_side_effects=True, vmem_limit_bytes=VMEM_LIMIT),
    )(code, tiles_t, cot_t, pair, *weights)


STEPS = 4


def finish_kernel(hidden, slot_ref, *refs):
    each = slot_ref.shape[0] // STEPS
    backs, refs = refs[:each], refs[each:]
    (count_ref, mir_ref, hl_ref, sum_ref, gp_ref,
     tile_ref, log_ref, out_ref, gt_ref, gg_ref, gu_ref, go_ref, gd_ref, gn_ref) = refs
    step = pl.program_id(0)
    out_ref[...] = gp_ref[...]
    for n, back_ref in enumerate(backs):
        inv = share(count_ref[step * each + n])
        span = back_ref.shape[3]
        for q in range(back_ref.shape[0]):
            tile_ref[n, :, q * span:(q + 1) * span] = (back_ref[q, 0].astype(F32) * inv).astype(BF16)
    per, bins, lanes = hl_ref.shape
    low = lax.broadcasted_iota(jnp.int32, (bins, lanes), 1) < lanes // 2
    for k in range(per // 2):
        half, m, t = pair_place(step * (per // 2) + k, mir_ref.shape[1])
        a, b = mir_ref[half, m, 0, t].astype(F32), mir_ref[half, m, 1, t].astype(F32)
        even = jnp.where(low, a, pltpu.roll(b, lanes // 2, 1))
        odd = jnp.where(low, pltpu.roll(a, lanes // 2, 1), b)
        log_ref[2 * k] = (hl_ref[2 * k].astype(F32) + even).astype(BF16)
        log_ref[2 * k + 1] = (hl_ref[2 * k + 1].astype(F32) + odd).astype(BF16)

    @pl.when(step == 0)
    def _():
        width = sum_ref.shape[1]
        for k in range(hidden // width):
            span = slice(k * width, (k + 1) * width)
            gg_ref[:, span] = sum_ref[k * width:(k + 1) * width, :].astype(F32)
            gu_ref[:, span] = sum_ref[hidden + k * width:hidden + (k + 1) * width, :].astype(F32)
        go_ref[...] = sum_ref[2 * hidden:3 * hidden, :].astype(F32)
        at = 3 * hidden
        gd_ref[...] = sum_ref[at:at + gd_ref.shape[0], :].astype(F32)
        at += gd_ref.shape[0]
        gt_ref[...] = sum_ref[at:at + gt_ref.shape[0], :].astype(F32)
        at += gt_ref.shape[0]
        norm = sum_ref[at:at + 16, :].astype(F32)
        gn_ref[0:1, :] = jnp.sum(norm[0:8], axis=0, keepdims=True)
        gn_ref[1:2, :] = jnp.sum(norm[8:16], axis=0, keepdims=True)


def finish(hidden, slot_of, count, back, mir, hl, sums, grad_pair):
    slots = slot_of.shape[0]
    feature, cells = back.shape[2], back.shape[0] * back.shape[3]
    cols, bins, rows = hl.shape
    width = sums.shape[1]
    per, each = cols // STEPS, slots // STEPS
    const = lambda shape: pl.BlockSpec(shape, lambda i, s: (0,) * len(shape))
    outs = [((slots, feature, cells), BF16), ((cols, bins, rows), BF16), (grad_pair.shape, F32),
            ((feature, width), F32), ((width, hidden), F32), ((width, hidden), F32), ((hidden, width), F32),
            ((bins, width), F32), ((2, width), F32)]
    held = lambda n: pl.BlockSpec(
        (back.shape[0], 1, feature, back.shape[3]), lambda i, s: (0, s[i * each + n], 0, 0))
    band = pl.BlockSpec((grad_pair.shape[0] // STEPS,) + grad_pair.shape[1:], lambda i, s: (i, 0, 0))
    return pl.pallas_call(
        functools.partial(finish_kernel, hidden),
        name="finish",
        grid_spec=pltpu.PrefetchScalarGridSpec(
            num_scalar_prefetch=1,
            grid=(STEPS,),
            in_specs=[held(n) for n in range(each)] + [
                pl.BlockSpec(memory_space=pltpu.SMEM),
                const(mir.shape),
                pl.BlockSpec((per, bins, rows), lambda i, s: (i, 0, 0)),
                const(sums.shape),
                band,
            ],
            out_specs=[
                pl.BlockSpec((each, feature, cells), lambda i, s: (i, 0, 0)),
                pl.BlockSpec((per, bins, rows), lambda i, s: (i, 0, 0)),
                band,
            ] + [const(shape) for shape, _ in outs[3:]],
        ),
        out_shape=[jax.ShapeDtypeStruct(shape, kind) for shape, kind in outs],
        compiler_params=pltpu.CompilerParams(
            dimension_semantics=("arbitrary",), vmem_limit_bytes=VMEM_LIMIT),
    )(slot_of, *([back] * each), count, mir, hl, sums, grad_pair)


def per_device(pair, logit_cotangent, tiles, tile_target, tile_square, tile_count, w_template,
               transition_norm_gain, transition_norm_bias, w_gate, w_up, w_out, w_dist):
    row_devs = lax.axis_size("row")
    col_devs = lax.axis_size("col")
    rows, cols, width = pair.shape
    length = rows * row_devs
    slots, cells_sq, feature = tiles.shape
    hidden = w_gate.shape[1]
    tiles_t = jnp.transpose(tiles, (0, 2, 1))
    cot_t = jnp.transpose(logit_cotangent, (1, 2, 0))
    target = tile_target[:, 0]
    places = jnp.arange(slots, dtype=jnp.int32)
    rank = jnp.sum((target[:, None] == target[None, :]) & (places[None, :] < places[:, None]),
                   axis=1, dtype=jnp.int32)
    slot_of = target * CAP + rank
    chosen = slot_of[None, :] == jnp.arange(col_devs * CAP, dtype=jnp.int32)[:, None]
    label = places + 256 * (tile_square + 1) + 65536 * tile_count
    code = jnp.sum(jnp.where(chosen, label[None, :], 0), axis=1).reshape(col_devs, CAP)

    back, mir_heads, sums, gp, hl, _ = window(
        row_devs, col_devs, 1.0 / length, code, tiles_t, cot_t, pair, w_template,
        transition_norm_gain[None, :], transition_norm_bias[None, :], w_gate, w_up, w_out, w_dist.T)
    grad_tiles_t, logits_t, grad_pair, g_template, g_gate, g_up, g_out, g_dist_t, g_norm = finish(
        hidden, slot_of, tile_count, back.reshape(CHUNKS, col_devs * CAP, feature, SPAN), mir_heads, hl,
        sums.reshape(ROWS_SUM, width), gp)
    return (
        jnp.transpose(logits_t, (2, 0, 1)),
        grad_pair,
        jnp.transpose(grad_tiles_t, (0, 2, 1)),
        g_template,
        g_norm[0],
        g_norm[1],
        g_gate,
        g_up,
        g_out,
        g_dist_t.T,
    )


def solution(mesh):
    return jax.shard_map(
        per_device,
        mesh=mesh,
        in_specs=(
            P("row", "col", None),
            P("row", "col", None),
            P(("row", "col"), None, None),
            P(("row", "col"), None),
            P(("row", "col")),
            P(("row", "col")),
            P(), P(), P(), P(), P(), P(), P(),
        ),
        out_specs=(
            P("row", "col", None),
            P("row", "col", None),
            P(("row", "col"), None, None),
            P(), P(), P(), P(), P(), P(), P(),
        ),
        check_vma=False,
    )
```

```python
import functools

import jax
import jax.numpy as jnp
from jax import lax
from jax.experimental import pallas as pl
from jax.experimental.pallas import tpu as pltpu
from jax.sharding import PartitionSpec as P

SQ = 32
CAP = 2
MESH = pl.DeviceIdType.MESH
F32 = jnp.float32
BF16 = jnp.bfloat16
ROWS_SUM = 2048
VMEM_LIMIT = 60 * 1024 * 1024


def vmem():
    return pl.BlockSpec(memory_space=pltpu.VMEM)


def smem():
    return pl.BlockSpec(memory_space=pltpu.SMEM)


def hbm():
    return pl.BlockSpec(memory_space=pl.ANY)


def nn(a, b):
    return lax.dot_general(a, b, (((1,), (0,)), ((), ())), preferred_element_type=F32)


def nt(a, b):
    return lax.dot_general(a, b, (((1,), (1,)), ((), ())), preferred_element_type=F32)


def tn(a, b):
    return lax.dot_general(a, b, (((0,), (0,)), ((), ())), preferred_element_type=F32)


def displacements(col_devs):
    if col_devs != 16:
        return (1, col_devs), [(0, k) for k in range(1, col_devs)]
    order = [(0, 1), (1, 0), (0, 3), (3, 0), (1, 1), (3, 3), (1, 3), (3, 1),
             (0, 2), (2, 0), (1, 2), (2, 1), (3, 2), (2, 3), (2, 2)]
    return (4, 4), order


def moved(col, shape, step, sign):
    ys, zs = shape
    y = lax.rem(col // zs + sign * step[0] + ys, ys)
    z = lax.rem(lax.rem(col, zs) + sign * step[1] + zs, zs)
    return y * zs + z


class Place:
    def __init__(self, row_devs, col_devs):
        self.row, self.col = lax.axis_index("row"), lax.axis_index("col")
        self.xs, self.zs = row_devs // 2, col_devs // (row_devs // 2)
        self.x, self.k = self.row // 2, lax.rem(self.row, 2)
        self.y, self.z = self.col // self.zs, lax.rem(self.col, self.zs)

    def turn(self, value, by):
        return lax.rem(value + by, self.xs) if self.xs > 1 else value


class Mirror:
    def __init__(self, place, src, first, second, dst, sems):
        self.p, self.src, self.first, self.second, self.dst = place, src, first, second, dst
        self.s1, self.r1, self.s2, self.r2, self.s3, self.r3, self.own = sems

    def along_x(self, source, target, send, recv):
        p = self.p
        copies = []
        for n in range(1, p.xs):
            to = p.turn(p.x, n)
            copies.append(pltpu.make_async_remote_copy(
                src_ref=source(to), dst_ref=target.at[p.x], send_sem=send.at[n - 1], recv_sem=recv.at[n - 1],
                device_id=(2 * to + p.k, p.col), device_id_type=MESH))
        return copies

    def start_1(self):
        p = self.p
        self.copies = self.along_x(lambda to: self.src.at[:, to], self.first, self.s1, self.r1)
        for copy in self.copies:
            copy.start()
        self.local = pltpu.make_async_copy(self.src.at[:, p.x], self.first.at[p.x], self.own.at[0])
        self.local.start()

    def finish(self):
        self.local.wait()
        for copy in self.copies:
            copy.wait()

    finish_1 = finish_3 = finish

    def start_2(self):
        p = self.p
        self.plan = []
        for n in range(p.xs):
            to_y = p.turn(p.y, n)
            for h in (0, 1):
                to_z, to_k = 2 * p.k + h, p.z // 2
                source, target = self.first.at[to_y, h], self.second.at[p.y, lax.rem(p.z, 2)]
                slot = 2 * n + lax.rem(p.z, 2)
                remote = pltpu.make_async_remote_copy(
                    src_ref=source, dst_ref=target, send_sem=self.s2.at[2 * n + h], recv_sem=self.r2.at[slot],
                    device_id=(2 * p.x + to_k, to_y * p.zs + to_z), device_id_type=MESH)
                if n == 0:
                    here = jnp.logical_and(to_k == p.k, to_z == p.z)
                    local = pltpu.make_async_copy(source, target, self.r2.at[slot])
                    start_one(here, remote, local)
                    self.plan.append((here, remote))
                else:
                    remote.start()
                    self.plan.append((None, remote))

    def finish_2(self):
        for i, (here, remote) in enumerate(self.plan):
            if here is None:
                remote.wait_send()
            else:
                @pl.when(jnp.logical_not(here))
                def _():
                    remote.wait_send()
            ref = self.second.at[0, 0]
            pltpu.make_async_copy(ref, ref, self.r2.at[i]).wait()

    def start_3(self):
        p = self.p
        self.copies = self.along_x(lambda to: self.second.at[to], self.dst, self.s3, self.r3)
        for copy in self.copies:
            copy.start()
        self.local = pltpu.make_async_copy(self.second.at[p.x], self.dst.at[p.x], self.own.at[1])
        self.local.start()


def start_one(here, remote, local):
    @pl.when(jnp.logical_not(here))
    def _():
        remote.start()

    @pl.when(here)
    def _():
        local.start()


def mirror_sems(row_devs):
    xs = row_devs // 2
    dma = lambda n: pltpu.SemaphoreType.DMA((n,))
    return [dma(max(xs - 1, 1)), dma(max(xs - 1, 1)), dma(2 * xs), dma(2 * xs),
            dma(max(xs - 1, 1)), dma(max(xs - 1, 1)), dma(2)]


def greet(p, row_devs, col_devs):
    barrier = pltpu.get_barrier_semaphore()
    peers = 0
    for n in range(1, col_devs):
        pl.semaphore_signal(barrier, inc=1, device_id=(p.row, lax.rem(p.col + n, col_devs)), device_id_type=MESH)
        peers += 1
    for n in range(1, row_devs):
        pl.semaphore_signal(barrier, inc=1, device_id=(lax.rem(p.row + n, row_devs), p.col), device_id_type=MESH)
        peers += 1
    for n in range(1, col_devs):
        pl.semaphore_signal(
            barrier, inc=1, device_id=(2 * p.x + 1 - p.k, lax.rem(p.col + n, col_devs)), device_id_type=MESH)
        peers += 1
    return lambda: pl.semaphore_wait(barrier, peers)


BAND = 8
CHUNKS = SQ // BAND
SPAN = BAND * SQ
PART = 256


def share(count):
    inv = jnp.where(count == 1, 1.0, jnp.where(count == 2, 0.5, jnp.where(count == 3, 1.0 / 3.0, 0.25)))
    return jnp.where(count == 0, 0.0, inv).astype(F32)


def pair_place(n, xs):
    u, q, a = lax.rem(n, BAND // 2), lax.rem(n // (BAND // 2), CHUNKS), n // (BAND // 2 * CHUNKS)
    return q // 2, lax.rem(u, xs), (lax.rem(q, 2) * 2 + a) * (BAND // 2 // xs) + u // xs


def window_kernel(row_devs, col_devs, scale, code_ref, tiles_ref, cot_ref, pair_ref, wt_ref,
                  gain_ref, bias_ref, wg_ref, wu_ref, wo_ref, wd_ref,
                  back_ref, heads_ref, sum_ref, gp_ref, hl_ref, got_ref,
                  ids_ref, sendbuf, recv, names, onehot, s_ref, g_ref, pair_v, d_ref, z_ref, hs_ref,
                  pack, c_first, c_second, c_dst, h_first, h_second,
                  ag_ref, au_ref, ao_ref, ad_ref, at_ref, an_ref, acc_ref,
                  low, rs_recv, cs_send, cs_recv, piece, chunk,
                  pair_sem, out_sem, id_send, id_recv, t_send, t_recv, g_send, g_recv, own_t, own_g, own_sem,
                  a_send, a_recv, b_send, b_recv, e_send, e_recv, f_send, f_recv, *mirror_sem):
    p = Place(row_devs, col_devs)
    row, col = p.row, p.col
    shape, order = displacements(col_devs)
    rows, cols, width = pair_v.shape
    bins, feature, hidden = wd_ref.shape[0], wt_ref.shape[0], wg_ref.shape[1]
    sq_cols, sq_rows = cols // SQ, rows // SQ
    squares = sq_cols * sq_rows
    cells = BAND * cols
    greeted = greet(p, row_devs, col_devs)
    pair_in = pltpu.make_async_copy(pair_ref, pair_v, pair_sem.at[0])
    pair_in.start()

    lanes = rows
    left = lax.broadcasted_iota(jnp.int32, (bins, lanes), 1) < lanes // 2

    def pack_pair(n, carry):
        u, v = cot_ref[2 * n].astype(F32), cot_ref[2 * n + 1].astype(F32)
        half, m, t = pair_place(n, p.xs)
        pack[half, 0, m, t] = jnp.where(left, u, pltpu.roll(v, lanes // 2, 1)).astype(BF16)
        pack[half, 1, m, t] = jnp.where(left, pltpu.roll(u, lanes // 2, 1), v).astype(BF16)
        return carry

    def fill(parts, d, carry):
        for k in range(CAP):
            code = code_ref[d, k]
            at, inv = jnp.bitwise_and(code, 255), share(code // 65536)
            for q in parts:
                sendbuf[q, d, k] = (
                    tiles_ref[at, :, q * SPAN:(q + 1) * SPAN].astype(F32) * inv).astype(BF16)
        return carry

    lax.fori_loop(0, col_devs, functools.partial(fill, (0,)), 0)
    id_lane = lax.broadcasted_iota(jnp.int32, (8, 128), 1)
    for d in range(col_devs):
        ids_ref[d] = jnp.where(id_lane == 0, code_ref[d, 0], code_ref[d, 1])
    greeted()

    def to_all(source, target, send, recv_sem):
        copies = []
        for n, step in enumerate(order):
            to = moved(col, shape, step, 1)
            copies.append(pltpu.make_async_remote_copy(
                src_ref=source(to), dst_ref=target(n), send_sem=send(n), recv_sem=recv_sem(n),
                device_id=(row, to), device_id_type=MESH))
        return copies

    def local(source, target, sem):
        copy = pltpu.make_async_copy(source, target, sem)
        copy.start()
        return copy

    id_copies = to_all(lambda to: ids_ref.at[to], lambda n: got_ref.at[col],
                       lambda n: id_send.at[n], lambda n: id_recv.at[n])
    for copy in id_copies:
        copy.start()
    own_id = local(ids_ref.at[col], got_ref.at[col], own_sem.at[0])
    tile_copies = []
    for q in range(CHUNKS):
        tile_copies.append(to_all(lambda to: sendbuf.at[q, to], lambda n: recv.at[q, col],
                                  lambda n: t_send.at[q, n], lambda n: t_recv.at[q, n]))
    for copy in tile_copies[0]:
        copy.start()
    lax.fori_loop(0, cols // 2, pack_pair, 0)
    mirrors = [Mirror(p, pack.at[n], c_first.at[n], c_second.at[n], c_dst.at[n], mirror_sem[7 * n:7 * (n + 1)])
               for n in range(2)]
    mirrors[0].start_1()
    mirrors[1].start_1()
    lax.fori_loop(0, col_devs, functools.partial(fill, tuple(range(1, CHUNKS))), 0)
    own_tiles = [local(sendbuf.at[q, col], recv.at[q, col], own_t.at[q]) for q in range(CHUNKS)]
    for ref in (ag_ref, au_ref, ao_ref, ad_ref, at_ref, an_ref):
        ref[...] = jnp.zeros(ref.shape, F32)
    mirrors[0].finish_1()
    mirrors[0].start_2()
    for copy in tile_copies[1]:
        copy.start()

    def own_cot(j, carry):
        d_ref[pl.ds(j, rows, stride=cols), :] = cot_ref[j].astype(F32).T
        return carry

    lax.fori_loop(0, cols, own_cot, 0)
    own_id.wait()
    for copy in id_copies:
        copy.wait()
    local(got_ref, names, own_sem.at[1]).wait()

    def square(d, k):
        return jnp.bitwise_and(names[d, 0, k] // 256, 255) - 1

    one_rows = lax.broadcasted_iota(jnp.int32, (squares * feature, CAP * feature), 0)
    one_cols = lax.broadcasted_iota(jnp.int32, (squares * feature, CAP * feature), 1)
    same = lax.rem(one_rows, feature) == lax.rem(one_cols, feature)
    square_of = one_rows // feature
    for d in range(col_devs):
        wanted = jnp.where(one_cols < feature, square(d, 0), square(d, 1))
        onehot[:, d * CAP * feature:(d + 1) * CAP * feature] = jnp.where(
            jnp.logical_and(same, square_of == wanted), 1.0, 0.0).astype(BF16)
    mirrors[1].finish_1()
    mirrors[1].start_2()
    for copy in tile_copies[2] + tile_copies[3]:
        copy.start()
    mirrors[0].finish_2()
    mirrors[0].start_3()

    def mirrored(half, r, carry):
        parity, r = r // (cols // 4), lax.rem(r, cols // 4)
        n = r // BAND * (2 * BAND) + half * BAND + lax.rem(r, BAND)
        _, m, t = pair_place(n, p.xs)
        at = pl.multiple_of((parity * (cols // 2) + n) * rows, rows)
        d_ref[pl.ds(at, rows), :] += c_dst[half, m, parity, t].astype(F32).T
        return carry

    mirrors[0].finish_3()
    lax.fori_loop(0, cols // 2, functools.partial(mirrored, 0), 0)
    pair_in.wait()

    def band(q, a, carry):
        row0 = a * SQ + q * BAND
        w_t = wt_ref[...]
        pieces = [s_ref[a * sq_cols + d] for d in range(sq_cols)]
        proj = jnp.concatenate(
            [tn(one, w_t).reshape(BAND, SQ, width) for one in pieces], axis=1).reshape(cells, width)
        z1 = pair_v[pl.ds(row0, BAND)].reshape(cells, width) + proj
        gain, bias = gain_ref[...], bias_ref[...]
        mean = jnp.mean(z1, axis=1, keepdims=True)
        centered = z1 - mean
        rdev = lax.rsqrt(jnp.mean(centered * centered, axis=1, keepdims=True) + 1e-5)
        xhat = centered * rdev
        normed = (xhat * gain + bias).astype(BF16)
        base = pl.multiple_of(row0 * cols, cells)
        dheads = d_ref[pl.ds(base, cells), :].astype(BF16)
        wd = wd_ref[...]
        dz2 = nn(dheads, wd)
        dzl = dz2.astype(BF16)
        normed_t = normed.T
        dzl_t = dzl.T
        z2 = z1
        dnorm = jnp.zeros((cells, width), F32)
        for k in range(hidden // PART):
            span = slice(k * PART, (k + 1) * PART)
            gate = nn(normed, wg_ref[:, span])
            up = nn(normed, wu_ref[:, span])
            dhid = nt(dzl, wo_ref[span, :])
            s = 0.5 * jnp.tanh(0.5 * gate) + 0.5
            swish = gate * s
            hid = (swish * up).astype(BF16)
            dup = (dhid * swish).astype(BF16)
            dgate = (dhid * up * (s + swish * (1.0 - s))).astype(BF16)
            z2 = z2 + nn(hid, wo_ref[span, :])
            dnorm = dnorm + nt(dgate, wg_ref[:, span]) + nt(dup, wu_ref[:, span])
            ao_ref[:, span] += nn(dzl_t, hid)
            ag_ref[:, span] += nn(normed_t, dgate)
            au_ref[:, span] += nn(normed_t, dup)
        z_ref[pl.ds(base, cells), :] = z2
        z2_low = z2.astype(BF16)
        heads_t = nt(wd, z2_low).astype(BF16)
        pairs = BAND // 2
        deep = pairs // p.xs
        for u in range(pairs):
            t = (q % 2 * 2 + lax.rem(a, 2)) * deep + u // p.xs
            hs_ref[q // 2, a // 2, u % p.xs, t] = heads_t[:, u * 128:(u + 1) * 128]
        ad_ref[...] += tn(dheads, z2_low)
        an_ref[0] += jnp.sum((dnorm * xhat).reshape(cells // 8, 8, width), axis=0)
        an_ref[1] += jnp.sum(dnorm.reshape(cells // 8, 8, width), axis=0)
        dx = dnorm * gain
        grad = dz2 + (dx - jnp.mean(dx, axis=1, keepdims=True)
                      - xhat * jnp.mean(dx * xhat, axis=1, keepdims=True)) * rdev
        grad3 = grad.reshape(BAND, cols, width)
        pair_v[pl.ds(row0, BAND)] = grad3
        total = jnp.zeros((feature, width), F32)
        for d in range(sq_cols):
            dproj = grad3[:, d * SQ:(d + 1) * SQ, :].reshape(SPAN, width).astype(BF16)
            g_ref[a * sq_cols + d] = nt(w_t, dproj).astype(BF16)
            total = total + nn(pieces[d], dproj)
        at_ref[...] += total
        return carry

    back_copies, own_back, pair_out = [], [], []
    halves = [Mirror(p, hs_ref.at[n], h_first.at[n], h_second.at[n], heads_ref.at[n],
                     mirror_sem[7 * (n + 2):7 * (n + 3)]) for n in range(2)]
    for q in range(CHUNKS):
        if q == 2:
            mirrors[1].finish_3()
            lax.fori_loop(0, cols // 2, functools.partial(mirrored, 1), 0)
        own_tiles[q].wait()
        for copy in tile_copies[q]:
            copy.wait()
        s_ref[...] = nn(onehot[...], recv[q].reshape(col_devs * CAP * feature, SPAN)).astype(BF16).reshape(
            s_ref.shape)
        lax.fori_loop(0, sq_rows, functools.partial(band, q), 0)

        def take(d, carry):
            for k in range(CAP):
                sendbuf[q, d, k] = g_ref[jnp.maximum(square(d, k), 0)]
            return carry

        lax.fori_loop(0, col_devs, take, 0)
        for a in range(sq_rows):
            part_rows = pl.ds(a * SQ + q * BAND, BAND)
            pair_out.append(local(pair_v.at[part_rows], gp_ref.at[part_rows], out_sem.at[q * sq_rows + a]))
        if q == 0:
            mirrors[1].finish_2()
            mirrors[1].start_3()
        if q == 1:
            halves[0].start_1()
        if q == 2:
            halves[0].finish()
            halves[0].start_2()
        if q == 3:
            halves[1].start_1()
        back_copies.append(to_all(lambda to: sendbuf.at[q, to], lambda n: back_ref.at[q, col],
                                  lambda n: g_send.at[q, n], lambda n: g_recv.at[q, n]))
        own_back.append(local(sendbuf.at[q, col], back_ref.at[q, col], own_g.at[q]))
        if q < CHUNKS - 2:
            for copy in back_copies[q]:
                copy.start()

    for k in range(hidden // width):
        span = slice(k * width, (k + 1) * width)
        acc_ref[k * width:(k + 1) * width, :] = ag_ref[:, span]
        acc_ref[hidden + k * width:hidden + (k + 1) * width, :] = au_ref[:, span]
        acc_ref[2 * hidden + k * width:2 * hidden + (k + 1) * width, :] = ao_ref[:, span].T
    tail = 3 * hidden
    acc_ref[tail:tail + bins, :] = ad_ref[...]
    tail += bins
    acc_ref[tail:tail + feature, :] = at_ref[...]
    tail += feature
    acc_ref[tail:tail + 8, :] = an_ref[0]
    acc_ref[tail + 8:tail + 16, :] = an_ref[1]
    acc_ref[tail + 16:, :] = jnp.zeros((ROWS_SUM - tail - 16, width), F32)
    low[...] = acc_ref[...].astype(BF16)
    rows_chunk = ROWS_SUM // row_devs

    def part(r):
        return pl.ds(pl.multiple_of(r * rows_chunk, rows_chunk), rows_chunk)

    first = []
    for k in range(1, row_devs):
        to = lax.rem(row + k, row_devs)
        first.append(pltpu.make_async_remote_copy(
            src_ref=low.at[part(to)], dst_ref=rs_recv.at[k - 1], send_sem=a_send.at[k - 1],
            recv_sem=a_recv.at[k - 1], device_id=(to, col), device_id_type=MESH))
    for copy in first:
        copy.start()
    held = back_copies[2] + back_copies[3]
    some = len(order) // 3

    wd = wd_ref[...]

    def local_heads(j, carry):
        zj = z_ref[pl.ds(j, rows, stride=cols), :].astype(BF16)
        hl_ref[j] = nt(wd, zj).astype(BF16)
        return carry

    lax.fori_loop(0, cols, local_heads, 0)
    halves[1].finish_1()
    halves[1].start_2()
    for copy in first:
        copy.wait()
    total = acc_ref[part(row), :]
    for k in range(row_devs - 1):
        total = total + rs_recv[k].astype(F32)
    cs_send[...] = total.astype(BF16).reshape(cs_send.shape)
    second = to_all(lambda to: cs_send.at[to], lambda n: cs_recv.at[n],
                    lambda n: b_send.at[n], lambda n: b_recv.at[n])
    for copy in second:
        copy.start()
    for copy in held[:some]:
        copy.start()
    halves[0].finish_2()
    halves[0].start_3()
    for copy in second:
        copy.wait()
    mine = cs_send[col].astype(F32)
    for k in range(col_devs - 1):
        mine = mine + cs_recv[k].astype(F32)
    piece[...] = (mine * scale).astype(BF16)
    chunk[col] = piece[...]
    gather = to_all(lambda to: piece, lambda n: chunk.at[col], lambda n: e_send.at[n], lambda n: e_recv.at[n])
    for copy in gather:
        copy.start()
    for copy in held[some:]:
        copy.start()
    halves[1].finish_2()
    halves[1].start_3()
    for copy in gather:
        copy.wait()
    last = []
    for k in range(1, row_devs):
        last.append(pltpu.make_async_remote_copy(
            src_ref=chunk, dst_ref=sum_ref.at[row], send_sem=f_send.at[k - 1],
            recv_sem=f_recv.at[k - 1], device_id=(lax.rem(row + k, row_devs), col), device_id_type=MESH))
    for copy in last:
        copy.start()
    local(chunk, sum_ref.at[row], own_sem.at[2]).wait()
    for copy in pair_out:
        copy.wait()
    halves[0].finish_3()
    for copy in last:
        copy.wait()
    halves[1].finish_3()
    for q in range(CHUNKS):
        own_back[q].wait()
        for copy in back_copies[q]:
            copy.wait()


def window(row_devs, col_devs, scale, code, tiles_t, cot_t, pair, *weights):
    slots, feature, cells_sq = tiles_t.shape
    cols, bins, rows = cot_t.shape
    width = pair.shape[2]
    hidden = weights[3].shape[1]
    squares = rows // SQ * (cols // SQ)
    peers, xs = col_devs - 1, row_devs // 2
    rows_chunk = ROWS_SUM // row_devs
    rows_piece = rows_chunk // col_devs
    dma = lambda *n: pltpu.SemaphoreType.DMA(n)
    deep = cols // 4 // xs
    slices = (2, 2, xs, deep, bins, rows)
    heads = (2, xs, 2, deep, bins, rows)
    return pl.pallas_call(
        functools.partial(window_kernel, row_devs, col_devs, scale),
        name="window",
        out_shape=(
            jax.ShapeDtypeStruct((CHUNKS, col_devs, CAP, feature, SPAN), BF16),
            jax.ShapeDtypeStruct(heads, BF16),
            jax.ShapeDtypeStruct((row_devs, col_devs, rows_piece, 128), BF16),
            jax.ShapeDtypeStruct(pair.shape, F32),
            jax.ShapeDtypeStruct((cols, bins, rows), BF16),
            jax.ShapeDtypeStruct((col_devs, 8, 128), jnp.int32),
        ),
        in_specs=[smem(), vmem(), vmem(), hbm()] + [vmem()] * len(weights),
        out_specs=(hbm(), hbm(), hbm(), hbm(), vmem(), hbm()),
        scratch_shapes=[
            pltpu.VMEM((col_devs, 8, 128), jnp.int32),
            pltpu.VMEM((CHUNKS, col_devs, CAP, feature, SPAN), BF16),
            pltpu.VMEM((CHUNKS, col_devs, CAP, feature, SPAN), BF16),
            pltpu.SMEM((col_devs, 8, 128), jnp.int32),
            pltpu.VMEM((squares * feature, col_devs * CAP * feature), BF16),
            pltpu.VMEM((squares, feature, SPAN), BF16),
            pltpu.VMEM((squares, feature, SPAN), BF16),
            pltpu.VMEM((rows, cols, width), F32),
            pltpu.VMEM((rows * cols, bins), F32),
            pltpu.VMEM((rows * cols, width), F32),
            pltpu.VMEM(slices, BF16),
            pltpu.VMEM(slices, BF16),
            pltpu.VMEM(heads, BF16),
            pltpu.VMEM(heads, BF16),
            pltpu.VMEM(heads, BF16),
            pltpu.VMEM(heads, BF16),
            pltpu.VMEM(heads, BF16),
            pltpu.VMEM((width, hidden), F32),
            pltpu.VMEM((width, hidden), F32),
            pltpu.VMEM((width, hidden), F32),
            pltpu.VMEM((bins, width), F32),
            pltpu.VMEM((feature, width), F32),
            pltpu.VMEM((2, 8, width), F32),
            pltpu.VMEM((ROWS_SUM, 128), F32),
            pltpu.VMEM((ROWS_SUM, 128), BF16),
            pltpu.VMEM((row_devs - 1, rows_chunk, 128), BF16),
            pltpu.VMEM((col_devs, rows_piece, 128), BF16),
            pltpu.VMEM((col_devs - 1, rows_piece, 128), BF16),
            pltpu.VMEM((rows_piece, 128), BF16),
            pltpu.VMEM((col_devs, rows_piece, 128), BF16),
            dma(1), dma(rows // BAND), dma(peers), dma(peers),
            dma(CHUNKS, peers), dma(CHUNKS, peers), dma(CHUNKS, peers), dma(CHUNKS, peers),
            dma(CHUNKS), dma(CHUNKS), dma(3),
            dma(row_devs - 1), dma(row_devs - 1), dma(peers), dma(peers),
            dma(peers), dma(peers), dma(row_devs - 1), dma(row_devs - 1),
        ] + mirror_sems(row_devs) * 4,
        compiler_params=pltpu.CompilerParams(
            collective_id=0, has_side_effects=True, vmem_limit_bytes=VMEM_LIMIT),
    )(code, tiles_t, cot_t, pair, *weights)


STEPS = 4


def finish_kernel(hidden, slot_ref, *refs):
    each = slot_ref.shape[0] // STEPS
    backs, refs = refs[:each], refs[each:]
    (count_ref, mir_ref, hl_ref, sum_ref, gp_ref,
     tile_ref, log_ref, out_ref, gt_ref, gg_ref, gu_ref, go_ref, gd_ref, gn_ref) = refs
    step = pl.program_id(0)
    out_ref[...] = gp_ref[...]
    for n, back_ref in enumerate(backs):
        inv = share(count_ref[step * each + n])
        span = back_ref.shape[3]
        for q in range(back_ref.shape[0]):
            tile_ref[n, :, q * span:(q + 1) * span] = (back_ref[q, 0].astype(F32) * inv).astype(BF16)
    per, bins, lanes = hl_ref.shape
    low = lax.broadcasted_iota(jnp.int32, (bins, lanes), 1) < lanes // 2
    for k in range(per // 2):
        half, m, t = pair_place(step * (per // 2) + k, mir_ref.shape[1])
        a, b = mir_ref[half, m, 0, t].astype(F32), mir_ref[half, m, 1, t].astype(F32)
        even = jnp.where(low, a, pltpu.roll(b, lanes // 2, 1))
        odd = jnp.where(low, pltpu.roll(a, lanes // 2, 1), b)
        log_ref[2 * k] = (hl_ref[2 * k].astype(F32) + even).astype(BF16)
        log_ref[2 * k + 1] = (hl_ref[2 * k + 1].astype(F32) + odd).astype(BF16)

    @pl.when(step == 0)
    def _():
        width = sum_ref.shape[1]
        for k in range(hidden // width):
            span = slice(k * width, (k + 1) * width)
            gg_ref[:, span] = sum_ref[k * width:(k + 1) * width, :].astype(F32)
            gu_ref[:, span] = sum_ref[hidden + k * width:hidden + (k + 1) * width, :].astype(F32)
        go_ref[...] = sum_ref[2 * hidden:3 * hidden, :].astype(F32)
        at = 3 * hidden
        gd_ref[...] = sum_ref[at:at + gd_ref.shape[0], :].astype(F32)
        at += gd_ref.shape[0]
        gt_ref[...] = sum_ref[at:at + gt_ref.shape[0], :].astype(F32)
        at += gt_ref.shape[0]
        norm = sum_ref[at:at + 16, :].astype(F32)
        gn_ref[0:1, :] = jnp.sum(norm[0:8], axis=0, keepdims=True)
        gn_ref[1:2, :] = jnp.sum(norm[8:16], axis=0, keepdims=True)


def finish(hidden, slot_of, count, back, mir, hl, sums, grad_pair):
    slots = slot_of.shape[0]
    feature, cells = back.shape[2], back.shape[0] * back.shape[3]
    cols, bins, rows = hl.shape
    width = sums.shape[1]
    per, each = cols // STEPS, slots // STEPS
    const = lambda shape: pl.BlockSpec(shape, lambda i, s: (0,) * len(shape))
    outs = [((slots, feature, cells), BF16), ((cols, bins, rows), BF16), (grad_pair.shape, F32),
            ((feature, width), F32), ((width, hidden), F32), ((width, hidden), F32), ((hidden, width), F32),
            ((bins, width), F32), ((2, width), F32)]
    held = lambda n: pl.BlockSpec(
        (back.shape[0], 1, feature, back.shape[3]), lambda i, s: (0, s[i * each + n], 0, 0))
    band = pl.BlockSpec((grad_pair.shape[0] // STEPS,) + grad_pair.shape[1:], lambda i, s: (i, 0, 0))
    return pl.pallas_call(
        functools.partial(finish_kernel, hidden),
        name="finish",
        grid_spec=pltpu.PrefetchScalarGridSpec(
            num_scalar_prefetch=1,
            grid=(STEPS,),
            in_specs=[held(n) for n in range(each)] + [
                pl.BlockSpec(memory_space=pltpu.SMEM),
                const(mir.shape),
                pl.BlockSpec((per, bins, rows), lambda i, s: (i, 0, 0)),
                const(sums.shape),
                band,
            ],
            out_specs=[
                pl.BlockSpec((each, feature, cells), lambda i, s: (i, 0, 0)),
                pl.BlockSpec((per, bins, rows), lambda i, s: (i, 0, 0)),
                band,
            ] + [const(shape) for shape, _ in outs[3:]],
        ),
        out_shape=[jax.ShapeDtypeStruct(shape, kind) for shape, kind in outs],
        compiler_params=pltpu.CompilerParams(
            dimension_semantics=("arbitrary",), vmem_limit_bytes=VMEM_LIMIT),
    )(slot_of, *([back] * each), count, mir, hl, sums, grad_pair)


def per_device(pair, logit_cotangent, tiles, tile_target, tile_square, tile_count, w_template,
               transition_norm_gain, transition_norm_bias, w_gate, w_up, w_out, w_dist):
    row_devs = lax.axis_size("row")
    col_devs = lax.axis_size("col")
    rows, cols, width = pair.shape
    length = rows * row_devs
    slots, cells_sq, feature = tiles.shape
    hidden = w_gate.shape[1]
    tiles_t = jnp.transpose(tiles, (0, 2, 1))
    cot_t = jnp.transpose(logit_cotangent, (1, 2, 0))
    target = tile_target[:, 0]
    places = jnp.arange(slots, dtype=jnp.int32)
    rank = jnp.sum((target[:, None] == target[None, :]) & (places[None, :] < places[:, None]),
                   axis=1, dtype=jnp.int32)
    slot_of = target * CAP + rank
    chosen = slot_of[None, :] == jnp.arange(col_devs * CAP, dtype=jnp.int32)[:, None]
    label = places + 256 * (tile_square + 1) + 65536 * tile_count
    code = jnp.sum(jnp.where(chosen, label[None, :], 0), axis=1).reshape(col_devs, CAP)

    back, mir_heads, sums, gp, hl, _ = window(
        row_devs, col_devs, 1.0 / length, code, tiles_t, cot_t, pair, w_template,
        transition_norm_gain[None, :], transition_norm_bias[None, :], w_gate, w_up, w_out, w_dist.T)
    grad_tiles_t, logits_t, grad_pair, g_template, g_gate, g_up, g_out, g_dist_t, g_norm = finish(
        hidden, slot_of, tile_count, back.reshape(CHUNKS, col_devs * CAP, feature, SPAN), mir_heads, hl,
        sums.reshape(ROWS_SUM, width), gp)
    return (
        jnp.transpose(logits_t, (2, 0, 1)),
        grad_pair,
        jnp.transpose(grad_tiles_t, (0, 2, 1)),
        g_template,
        g_norm[0],
        g_norm[1],
        g_gate,
        g_up,
        g_out,
        g_dist_t.T,
    )


def solution(mesh):
    return jax.shard_map(
        per_device,
        mesh=mesh,
        in_specs=(
            P("row", "col", None),
            P("row", "col", None),
            P(("row", "col"), None, None),
            P(("row", "col"), None),
            P(("row", "col")),
            P(("row", "col")),
            P(), P(), P(), P(), P(), P(), P(),
        ),
        out_specs=(
            P("row", "col", None),
            P("row", "col", None),
            P(("row", "col"), None, None),
            P(), P(), P(), P(), P(), P(), P(),
        ),
        check_vma=False,
    )
```

```python
import functools

import jax
import jax.numpy as jnp
from jax import lax
from jax.experimental import pallas as pl
from jax.experimental.pallas import tpu as pltpu
from jax.sharding import PartitionSpec as P

SQ = 32
CAP = 2
MESH = pl.DeviceIdType.MESH
F32 = jnp.float32
BF16 = jnp.bfloat16
ROWS_SUM = 2048
VMEM_LIMIT = 60 * 1024 * 1024


def vmem():
    return pl.BlockSpec(memory_space=pltpu.VMEM)


def smem():
    return pl.BlockSpec(memory_space=pltpu.SMEM)


def hbm():
    return pl.BlockSpec(memory_space=pl.ANY)


def nn(a, b):
    return lax.dot_general(a, b, (((1,), (0,)), ((), ())), preferred_element_type=F32)


def nt(a, b):
    return lax.dot_general(a, b, (((1,), (1,)), ((), ())), preferred_element_type=F32)


def tn(a, b):
    return lax.dot_general(a, b, (((0,), (0,)), ((), ())), preferred_element_type=F32)


def displacements(col_devs):
    if col_devs != 16:
        return (1, col_devs), [(0, k) for k in range(1, col_devs)]
    order = [(0, 1), (1, 0), (0, 3), (3, 0), (1, 1), (3, 3), (1, 3), (3, 1),
             (0, 2), (2, 0), (1, 2), (2, 1), (3, 2), (2, 3), (2, 2)]
    return (4, 4), order


def moved(col, shape, step, sign):
    ys, zs = shape
    y = lax.rem(col // zs + sign * step[0] + ys, ys)
    z = lax.rem(lax.rem(col, zs) + sign * step[1] + zs, zs)
    return y * zs + z


class Place:
    def __init__(self, row_devs, col_devs):
        self.row, self.col = lax.axis_index("row"), lax.axis_index("col")
        self.xs, self.zs = row_devs // 2, col_devs // (row_devs // 2)
        self.x, self.k = self.row // 2, lax.rem(self.row, 2)
        self.y, self.z = self.col // self.zs, lax.rem(self.col, self.zs)

    def turn(self, value, by):
        return lax.rem(value + by, self.xs) if self.xs > 1 else value


class Mirror:
    def __init__(self, place, src, first, second, dst, sems):
        self.p, self.src, self.first, self.second, self.dst = place, src, first, second, dst
        self.s1, self.r1, self.s2, self.r2, self.s3, self.r3, self.own = sems

    def along_x(self, source, target, send, recv):
        p = self.p
        copies = []
        for n in range(1, p.xs):
            to = p.turn(p.x, n)
            copies.append(pltpu.make_async_remote_copy(
                src_ref=source(to), dst_ref=target.at[p.x], send_sem=send.at[n - 1], recv_sem=recv.at[n - 1],
                device_id=(2 * to + p.k, p.col), device_id_type=MESH))
        return copies

    def start_1(self):
        p = self.p
        self.copies = self.along_x(lambda to: self.src.at[:, to], self.first, self.s1, self.r1)
        for copy in self.copies:
            copy.start()
        self.local = pltpu.make_async_copy(self.src.at[:, p.x], self.first.at[p.x], self.own.at[0])
        self.local.start()

    def finish(self):
        self.local.wait()
        for copy in self.copies:
            copy.wait()

    finish_1 = finish_3 = finish

    def start_2(self):
        p = self.p
        self.plan = []
        for n in range(p.xs):
            to_y = p.turn(p.y, n)
            for h in (0, 1):
                to_z, to_k = 2 * p.k + h, p.z // 2
                source, target = self.first.at[to_y, h], self.second.at[p.y, lax.rem(p.z, 2)]
                slot = 2 * n + lax.rem(p.z, 2)
                remote = pltpu.make_async_remote_copy(
                    src_ref=source, dst_ref=target, send_sem=self.s2.at[2 * n + h], recv_sem=self.r2.at[slot],
                    device_id=(2 * p.x + to_k, to_y * p.zs + to_z), device_id_type=MESH)
                if n == 0:
                    here = jnp.logical_and(to_k == p.k, to_z == p.z)
                    local = pltpu.make_async_copy(source, target, self.r2.at[slot])
                    start_one(here, remote, local)
                    self.plan.append((here, remote))
                else:
                    remote.start()
                    self.plan.append((None, remote))

    def finish_2(self):
        for i, (here, remote) in enumerate(self.plan):
            if here is None:
                remote.wait_send()
            else:
                @pl.when(jnp.logical_not(here))
                def _():
                    remote.wait_send()
            ref = self.second.at[0, 0]
            pltpu.make_async_copy(ref, ref, self.r2.at[i]).wait()

    def start_3(self):
        p = self.p
        self.copies = self.along_x(lambda to: self.second.at[to], self.dst, self.s3, self.r3)
        for copy in self.copies:
            copy.start()
        self.local = pltpu.make_async_copy(self.second.at[p.x], self.dst.at[p.x], self.own.at[1])
        self.local.start()


def start_one(here, remote, local):
    @pl.when(jnp.logical_not(here))
    def _():
        remote.start()

    @pl.when(here)
    def _():
        local.start()


def mirror_sems(row_devs):
    xs = row_devs // 2
    dma = lambda n: pltpu.SemaphoreType.DMA((n,))
    return [dma(max(xs - 1, 1)), dma(max(xs - 1, 1)), dma(2 * xs), dma(2 * xs),
            dma(max(xs - 1, 1)), dma(max(xs - 1, 1)), dma(2)]


def greet(p, row_devs, col_devs):
    barrier = pltpu.get_barrier_semaphore()
    peers = 0
    for n in range(1, col_devs):
        pl.semaphore_signal(barrier, inc=1, device_id=(p.row, lax.rem(p.col + n, col_devs)), device_id_type=MESH)
        peers += 1
    for n in range(1, row_devs):
        pl.semaphore_signal(barrier, inc=1, device_id=(lax.rem(p.row + n, row_devs), p.col), device_id_type=MESH)
        peers += 1
    for n in range(1, col_devs):
        pl.semaphore_signal(
            barrier, inc=1, device_id=(2 * p.x + 1 - p.k, lax.rem(p.col + n, col_devs)), device_id_type=MESH)
        peers += 1
    return lambda: pl.semaphore_wait(barrier, peers)


BAND = 8
CHUNKS = SQ // BAND
SPAN = BAND * SQ
PART = 256
EARLY, MIDDLE = 7, 5


def share(count):
    inv = jnp.where(count == 1, 1.0, jnp.where(count == 2, 0.5, jnp.where(count == 3, 1.0 / 3.0, 0.25)))
    return jnp.where(count == 0, 0.0, inv).astype(F32)


def pair_place(n, xs):
    u, q, a = lax.rem(n, BAND // 2), lax.rem(n // (BAND // 2), CHUNKS), n // (BAND // 2 * CHUNKS)
    return q // 2, lax.rem(u, xs), (lax.rem(q, 2) * 2 + a) * (BAND // 2 // xs) + u // xs


def window_kernel(row_devs, col_devs, scale, code_ref, tiles_ref, cot_ref, pair_ref, wt_ref,
                  gain_ref, bias_ref, wg_ref, wu_ref, wo_ref, wd_ref,
                  back_ref, heads_ref, sum_ref, gp_ref, hl_ref, got_ref,
                  ids_ref, sendbuf, recv, names, onehot, s_ref, g_ref, pair_v, d_ref, z_ref, hs_ref,
                  pack, c_first, c_second, c_dst, h_first, h_second,
                  ag_ref, au_ref, ao_ref, ad_ref, at_ref, an_ref, acc_ref,
                  low, rs_recv, cs_send, cs_recv, piece, chunk,
                  pair_sem, out_sem, id_send, id_recv, t_send, t_recv, g_send, g_recv, own_t, own_g, own_sem,
                  a_send, a_recv, b_send, b_recv, e_send, e_recv, f_send, f_recv, *mirror_sem):
    p = Place(row_devs, col_devs)
    row, col = p.row, p.col
    shape, order = displacements(col_devs)
    rows, cols, width = pair_v.shape
    bins, feature, hidden = wd_ref.shape[0], wt_ref.shape[0], wg_ref.shape[1]
    sq_cols, sq_rows = cols // SQ, rows // SQ
    squares = sq_cols * sq_rows
    cells = BAND * cols
    greeted = greet(p, row_devs, col_devs)
    pair_in = pltpu.make_async_copy(pair_ref, pair_v, pair_sem.at[0])
    pair_in.start()

    lanes = rows
    left = lax.broadcasted_iota(jnp.int32, (bins, lanes), 1) < lanes // 2

    def pack_pair(n, carry):
        u, v = cot_ref[2 * n].astype(F32), cot_ref[2 * n + 1].astype(F32)
        half, m, t = pair_place(n, p.xs)
        pack[half, 0, m, t] = jnp.where(left, u, pltpu.roll(v, lanes // 2, 1)).astype(BF16)
        pack[half, 1, m, t] = jnp.where(left, pltpu.roll(u, lanes // 2, 1), v).astype(BF16)
        return carry

    def fill(parts, d, carry):
        for k in range(CAP):
            code = code_ref[d, k]
            at, inv = jnp.bitwise_and(code, 255), share(code // 65536)
            for q in parts:
                sendbuf[q, d, k] = (
                    tiles_ref[at, :, q * SPAN:(q + 1) * SPAN].astype(F32) * inv).astype(BF16)
        return carry

    lax.fori_loop(0, col_devs, functools.partial(fill, (0,)), 0)
    id_lane = lax.broadcasted_iota(jnp.int32, (8, 128), 1)
    for d in range(col_devs):
        ids_ref[d] = jnp.where(id_lane == 0, code_ref[d, 0], code_ref[d, 1])
    greeted()

    def to_all(source, target, send, recv_sem):
        copies = []
        for n, step in enumerate(order):
            to = moved(col, shape, step, 1)
            copies.append(pltpu.make_async_remote_copy(
                src_ref=source(to), dst_ref=target(n), send_sem=send(n), recv_sem=recv_sem(n),
                device_id=(row, to), device_id_type=MESH))
        return copies

    def local(source, target, sem):
        copy = pltpu.make_async_copy(source, target, sem)
        copy.start()
        return copy

    id_copies = to_all(lambda to: ids_ref.at[to], lambda n: got_ref.at[col],
                       lambda n: id_send.at[n], lambda n: id_recv.at[n])
    for copy in id_copies:
        copy.start()
    own_id = local(ids_ref.at[col], got_ref.at[col], own_sem.at[0])
    tile_copies = []
    for q in range(CHUNKS):
        tile_copies.append(to_all(lambda to: sendbuf.at[q, to], lambda n: recv.at[q, col],
                                  lambda n: t_send.at[q, n], lambda n: t_recv.at[q, n]))
    for copy in tile_copies[0]:
        copy.start()
    lax.fori_loop(0, cols // 2, pack_pair, 0)
    mirrors = [Mirror(p, pack.at[n], c_first.at[n], c_second.at[n], c_dst.at[n], mirror_sem[7 * n:7 * (n + 1)])
               for n in range(2)]
    mirrors[0].start_1()
    mirrors[1].start_1()
    lax.fori_loop(0, col_devs, functools.partial(fill, tuple(range(1, CHUNKS))), 0)
    own_tiles = [local(sendbuf.at[q, col], recv.at[q, col], own_t.at[q]) for q in range(CHUNKS)]
    for ref in (ag_ref, au_ref, ao_ref, ad_ref, at_ref, an_ref):
        ref[...] = jnp.zeros(ref.shape, F32)
    mirrors[0].finish_1()
    mirrors[0].start_2()
    for copy in tile_copies[1]:
        copy.start()

    def own_cot(j, carry):
        d_ref[pl.ds(j, rows, stride=cols), :] = cot_ref[j].astype(F32).T
        return carry

    lax.fori_loop(0, cols, own_cot, 0)
    own_id.wait()
    for copy in id_copies:
        copy.wait()
    local(got_ref, names, own_sem.at[1]).wait()

    def square(d, k):
        return jnp.bitwise_and(names[d, 0, k] // 256, 255) - 1

    one_rows = lax.broadcasted_iota(jnp.int32, (squares * feature, CAP * feature), 0)
    one_cols = lax.broadcasted_iota(jnp.int32, (squares * feature, CAP * feature), 1)
    same = lax.rem(one_rows, feature) == lax.rem(one_cols, feature)
    square_of = one_rows // feature
    for d in range(col_devs):
        wanted = jnp.where(one_cols < feature, square(d, 0), square(d, 1))
        onehot[:, d * CAP * feature:(d + 1) * CAP * feature] = jnp.where(
            jnp.logical_and(same, square_of == wanted), 1.0, 0.0).astype(BF16)
    mirrors[1].finish_1()
    mirrors[1].start_2()
    for copy in tile_copies[2] + tile_copies[3]:
        copy.start()
    mirrors[0].finish_2()
    mirrors[0].start_3()

    def mirrored(half, r, carry):
        parity, r = r // (cols // 4), lax.rem(r, cols // 4)
        n = r // BAND * (2 * BAND) + half * BAND + lax.rem(r, BAND)
        _, m, t = pair_place(n, p.xs)
        at = pl.multiple_of((parity * (cols // 2) + n) * rows, rows)
        d_ref[pl.ds(at, rows), :] += c_dst[half, m, parity, t].astype(F32).T
        return carry

    mirrors[0].finish_3()
    lax.fori_loop(0, cols // 2, functools.partial(mirrored, 0), 0)
    pair_in.wait()

    def band(q, a, carry):
        row0 = a * SQ + q * BAND
        w_t = wt_ref[...]
        pieces = [s_ref[a * sq_cols + d] for d in range(sq_cols)]
        proj = jnp.concatenate(
            [tn(one, w_t).reshape(BAND, SQ, width) for one in pieces], axis=1).reshape(cells, width)
        z1 = pair_v[pl.ds(row0, BAND)].reshape(cells, width) + proj
        gain, bias = gain_ref[...], bias_ref[...]
        mean = jnp.mean(z1, axis=1, keepdims=True)
        centered = z1 - mean
        rdev = lax.rsqrt(jnp.mean(centered * centered, axis=1, keepdims=True) + 1e-5)
        xhat = centered * rdev
        normed = (xhat * gain + bias).astype(BF16)
        base = pl.multiple_of(row0 * cols, cells)
        dheads = d_ref[pl.ds(base, cells), :].astype(BF16)
        wd = wd_ref[...]
        dz2 = nn(dheads, wd)
        dzl = dz2.astype(BF16)
        normed_t = normed.T
        dzl_t = dzl.T
        z2 = z1
        dnorm = jnp.zeros((cells, width), F32)
        for k in range(hidden // PART):
            span = slice(k * PART, (k + 1) * PART)
            gate = nn(normed, wg_ref[:, span])
            up = nn(normed, wu_ref[:, span])
            dhid = nt(dzl, wo_ref[span, :])
            s = 0.5 * jnp.tanh(0.5 * gate) + 0.5
            swish = gate * s
            hid = (swish * up).astype(BF16)
            dup = (dhid * swish).astype(BF16)
            dgate = (dhid * up * (s + swish * (1.0 - s))).astype(BF16)
            z2 = z2 + nn(hid, wo_ref[span, :])
            dnorm = dnorm + nt(dgate, wg_ref[:, span]) + nt(dup, wu_ref[:, span])
            ao_ref[:, span] += nn(dzl_t, hid)
            ag_ref[:, span] += nn(normed_t, dgate)
            au_ref[:, span] += nn(normed_t, dup)
        z_ref[pl.ds(base, cells), :] = z2
        z2_low = z2.astype(BF16)
        heads_t = nt(wd, z2_low).astype(BF16)
        pairs = BAND // 2
        deep = pairs // p.xs
        for u in range(pairs):
            t = (q % 2 * 2 + lax.rem(a, 2)) * deep + u // p.xs
            hs_ref[q // 2, a // 2, u % p.xs, t] = heads_t[:, u * 128:(u + 1) * 128]
        ad_ref[...] += tn(dheads, z2_low)
        an_ref[0] += jnp.sum((dnorm * xhat).reshape(cells // 8, 8, width), axis=0)
        an_ref[1] += jnp.sum(dnorm.reshape(cells // 8, 8, width), axis=0)
        dx = dnorm * gain
        grad = dz2 + (dx - jnp.mean(dx, axis=1, keepdims=True)
                      - xhat * jnp.mean(dx * xhat, axis=1, keepdims=True)) * rdev
        grad3 = grad.reshape(BAND, cols, width)
        pair_v[pl.ds(row0, BAND)] = grad3
        total = jnp.zeros((feature, width), F32)
        for d in range(sq_cols):
            dproj = grad3[:, d * SQ:(d + 1) * SQ, :].reshape(SPAN, width).astype(BF16)
            g_ref[a * sq_cols + d] = nt(w_t, dproj).astype(BF16)
            total = total + nn(pieces[d], dproj)
        at_ref[...] += total
        return carry

    back_copies, own_back, pair_out = [], [], []
    halves = [Mirror(p, hs_ref.at[n], h_first.at[n], h_second.at[n], heads_ref.at[n],
                     mirror_sem[7 * (n + 2):7 * (n + 3)]) for n in range(2)]
    for q in range(CHUNKS):
        if q == 2:
            mirrors[1].finish_3()
            lax.fori_loop(0, cols // 2, functools.partial(mirrored, 1), 0)
        own_tiles[q].wait()
        for copy in tile_copies[q]:
            copy.wait()
        s_ref[...] = nn(onehot[...], recv[q].reshape(col_devs * CAP * feature, SPAN)).astype(BF16).reshape(
            s_ref.shape)
        lax.fori_loop(0, sq_rows, functools.partial(band, q), 0)

        def take(d, carry):
            for k in range(CAP):
                inv = share(names[d, 0, k] // 65536)
                sendbuf[q, d, k] = (g_ref[jnp.maximum(square(d, k), 0)].astype(F32) * inv).astype(BF16)
            return carry

        lax.fori_loop(0, col_devs, take, 0)
        for a in range(sq_rows):
            part_rows = pl.ds(a * SQ + q * BAND, BAND)
            pair_out.append(local(pair_v.at[part_rows], gp_ref.at[part_rows], out_sem.at[q * sq_rows + a]))
        if q == 0:
            mirrors[1].finish_2()
            mirrors[1].start_3()
        if q == 1:
            halves[0].start_1()
        if q == 2:
            halves[0].finish()
            halves[0].start_2()
        if q == 3:
            halves[1].start_1()
        back_copies.append(to_all(lambda to: sendbuf.at[q, to], lambda n: back_ref.at[q, col],
                                  lambda n: g_send.at[q, n], lambda n: g_recv.at[q, n]))
        own_back.append(local(sendbuf.at[q, col], back_ref.at[q, col], own_g.at[q]))
        if q < CHUNKS - 1:
            for copy in back_copies[q] if q < CHUNKS - 2 else back_copies[q][:EARLY]:
                copy.start()

    for k in range(hidden // width):
        span = slice(k * width, (k + 1) * width)
        acc_ref[k * width:(k + 1) * width, :] = ag_ref[:, span]
        acc_ref[hidden + k * width:hidden + (k + 1) * width, :] = au_ref[:, span]
        acc_ref[2 * hidden + k * width:2 * hidden + (k + 1) * width, :] = ao_ref[:, span].T
    tail = 3 * hidden
    acc_ref[tail:tail + bins, :] = ad_ref[...]
    tail += bins
    acc_ref[tail:tail + feature, :] = at_ref[...]
    tail += feature
    acc_ref[tail:tail + 8, :] = an_ref[0]
    acc_ref[tail + 8:tail + 16, :] = an_ref[1]
    acc_ref[tail + 16:, :] = jnp.zeros((ROWS_SUM - tail - 16, width), F32)
    low[...] = acc_ref[...].astype(BF16)
    rows_chunk = ROWS_SUM // row_devs

    def part(r):
        return pl.ds(pl.multiple_of(r * rows_chunk, rows_chunk), rows_chunk)

    first = []
    for k in range(1, row_devs):
        to = lax.rem(row + k, row_devs)
        first.append(pltpu.make_async_remote_copy(
            src_ref=low.at[part(to)], dst_ref=rs_recv.at[k - 1], send_sem=a_send.at[k - 1],
            recv_sem=a_recv.at[k - 1], device_id=(to, col), device_id_type=MESH))
    for copy in first:
        copy.start()
    held = back_copies[2][EARLY:] + back_copies[3]

    wd = wd_ref[...]

    def local_heads(j, carry):
        zj = z_ref[pl.ds(j, rows, stride=cols), :].astype(BF16)
        hl_ref[j] = nt(wd, zj).astype(BF16)
        return carry

    lax.fori_loop(0, cols, local_heads, 0)
    halves[1].finish_1()
    halves[1].start_2()
    for copy in first:
        copy.wait()
    total = acc_ref[part(row), :]
    for k in range(row_devs - 1):
        total = total + rs_recv[k].astype(F32)
    cs_send[...] = total.astype(BF16).reshape(cs_send.shape)
    second = to_all(lambda to: cs_send.at[to], lambda n: cs_recv.at[n],
                    lambda n: b_send.at[n], lambda n: b_recv.at[n])
    for copy in second:
        copy.start()
    for copy in held[:MIDDLE]:
        copy.start()
    halves[0].finish_2()
    halves[0].start_3()
    for copy in second:
        copy.wait()
    mine = cs_send[col].astype(F32)
    for k in range(col_devs - 1):
        mine = mine + cs_recv[k].astype(F32)
    piece[...] = (mine * scale).astype(BF16)
    chunk[col] = piece[...]
    gather = to_all(lambda to: piece, lambda n: chunk.at[col], lambda n: e_send.at[n], lambda n: e_recv.at[n])
    for copy in gather:
        copy.start()
    for copy in held[MIDDLE:]:
        copy.start()
    halves[1].finish_2()
    halves[1].start_3()
    for copy in gather:
        copy.wait()
    last = []
    for k in range(1, row_devs):
        last.append(pltpu.make_async_remote_copy(
            src_ref=chunk, dst_ref=sum_ref.at[row], send_sem=f_send.at[k - 1],
            recv_sem=f_recv.at[k - 1], device_id=(lax.rem(row + k, row_devs), col), device_id_type=MESH))
    for copy in last:
        copy.start()
    local(chunk, sum_ref.at[row], own_sem.at[2]).wait()
    for copy in pair_out:
        copy.wait()
    halves[0].finish_3()
    for copy in last:
        copy.wait()
    halves[1].finish_3()
    for q in range(CHUNKS):
        own_back[q].wait()
        for copy in back_copies[q]:
            copy.wait()


def window(row_devs, col_devs, scale, code, tiles_t, cot_t, pair, *weights):
    slots, feature, cells_sq = tiles_t.shape
    cols, bins, rows = cot_t.shape
    width = pair.shape[2]
    hidden = weights[3].shape[1]
    squares = rows // SQ * (cols // SQ)
    peers, xs = col_devs - 1, row_devs // 2
    rows_chunk = ROWS_SUM // row_devs
    rows_piece = rows_chunk // col_devs
    dma = lambda *n: pltpu.SemaphoreType.DMA(n)
    deep = cols // 4 // xs
    slices = (2, 2, xs, deep, bins, rows)
    heads = (2, xs, 2, deep, bins, rows)
    return pl.pallas_call(
        functools.partial(window_kernel, row_devs, col_devs, scale),
        name="window",
        out_shape=(
            jax.ShapeDtypeStruct((CHUNKS, col_devs, CAP, feature, SPAN), BF16),
            jax.ShapeDtypeStruct(heads, BF16),
            jax.ShapeDtypeStruct((row_devs, col_devs, rows_piece, 128), BF16),
            jax.ShapeDtypeStruct(pair.shape, F32),
            jax.ShapeDtypeStruct((cols, bins, rows), BF16),
            jax.ShapeDtypeStruct((col_devs, 8, 128), jnp.int32),
        ),
        in_specs=[smem(), vmem(), vmem(), hbm()] + [vmem()] * len(weights),
        out_specs=(hbm(), hbm(), hbm(), hbm(), vmem(), hbm()),
        scratch_shapes=[
            pltpu.VMEM((col_devs, 8, 128), jnp.int32),
            pltpu.VMEM((CHUNKS, col_devs, CAP, feature, SPAN), BF16),
            pltpu.VMEM((CHUNKS, col_devs, CAP, feature, SPAN), BF16),
            pltpu.SMEM((col_devs, 8, 128), jnp.int32),
            pltpu.VMEM((squares * feature, col_devs * CAP * feature), BF16),
            pltpu.VMEM((squares, feature, SPAN), BF16),
            pltpu.VMEM((squares, feature, SPAN), BF16),
            pltpu.VMEM((rows, cols, width), F32),
            pltpu.VMEM((rows * cols, bins), F32),
            pltpu.VMEM((rows * cols, width), F32),
            pltpu.VMEM(slices, BF16),
            pltpu.VMEM(slices, BF16),
            pltpu.VMEM(heads, BF16),
            pltpu.VMEM(heads, BF16),
            pltpu.VMEM(heads, BF16),
            pltpu.VMEM(heads, BF16),
            pltpu.VMEM(heads, BF16),
            pltpu.VMEM((width, hidden), F32),
            pltpu.VMEM((width, hidden), F32),
            pltpu.VMEM((width, hidden), F32),
            pltpu.VMEM((bins, width), F32),
            pltpu.VMEM((feature, width), F32),
            pltpu.VMEM((2, 8, width), F32),
            pltpu.VMEM((ROWS_SUM, 128), F32),
            pltpu.VMEM((ROWS_SUM, 128), BF16),
            pltpu.VMEM((row_devs - 1, rows_chunk, 128), BF16),
            pltpu.VMEM((col_devs, rows_piece, 128), BF16),
            pltpu.VMEM((col_devs - 1, rows_piece, 128), BF16),
            pltpu.VMEM((rows_piece, 128), BF16),
            pltpu.VMEM((col_devs, rows_piece, 128), BF16),
            dma(1), dma(rows // BAND), dma(peers), dma(peers),
            dma(CHUNKS, peers), dma(CHUNKS, peers), dma(CHUNKS, peers), dma(CHUNKS, peers),
            dma(CHUNKS), dma(CHUNKS), dma(3),
            dma(row_devs - 1), dma(row_devs - 1), dma(peers), dma(peers),
            dma(peers), dma(peers), dma(row_devs - 1), dma(row_devs - 1),
        ] + mirror_sems(row_devs) * 4,
        compiler_params=pltpu.CompilerParams(
            collective_id=0, has_side_effects=True, vmem_limit_bytes=42 * 1024 * 1024),
    )(code, tiles_t, cot_t, pair, *weights)


STEPS = 4


def finish_kernel(hidden, slot_ref, back_ref, mir_ref, hl_ref, sum_ref, gp_ref,
                  tile_ref, log_ref, out_ref, gt_ref, gg_ref, gu_ref, go_ref, gd_ref, gn_ref, gb_ref,
                  mir, local, total, gp, tile, back_sem, in_sem, gp_in, gp_out, tile_sem, log_sem):
    slots = tile.shape[0]
    cols, bins, lanes = local.shape
    width = total.shape[1]

    def begin(source, target, sem):
        copy = pltpu.make_async_copy(source, target, sem)
        copy.start()
        return copy

    deep = gp.shape[0] // STEPS
    bands = [pl.ds(n * deep, deep) for n in range(STEPS)]
    pair_in = [begin(gp_ref.at[bands[0]], gp.at[bands[0]], gp_in.at[0])]
    get_sum = begin(sum_ref, total, in_sem.at[0])
    span = back_ref.shape[3]
    tiles_in = [[begin(back_ref.at[q, slot_ref[n]], tile.at[n, :, pl.ds(q * span, span)], back_sem.at[n, q])
                 for q in range(CHUNKS)] for n in range(slots)]
    get_mir = begin(mir_ref, mir, in_sem.at[1])
    get_local = begin(hl_ref, local, in_sem.at[2])
    pair_in += [begin(gp_ref.at[bands[n]], gp.at[bands[n]], gp_in.at[n]) for n in range(1, STEPS)]
    leaving = []
    pair_in[0].wait()
    leaving.append(begin(gp.at[bands[0]], out_ref.at[bands[0]], gp_out.at[0]))

    get_sum.wait()
    for k in range(hidden // width):
        span = slice(k * width, (k + 1) * width)
        gg_ref[:, span] = total[k * width:(k + 1) * width, :].astype(F32)
        gu_ref[:, span] = total[hidden + k * width:hidden + (k + 1) * width, :].astype(F32)
    go_ref[...] = total[2 * hidden:3 * hidden, :].astype(F32)
    at = 3 * hidden
    gd_ref[...] = total[at:at + gd_ref.shape[0], :].astype(F32)
    at += gd_ref.shape[0]
    gt_ref[...] = total[at:at + gt_ref.shape[0], :].astype(F32)
    at += gt_ref.shape[0]
    norm = total[at:at + 16, :].astype(F32)
    gn_ref[...] = jnp.sum(norm[0:8], axis=0, keepdims=True)
    gb_ref[...] = jnp.sum(norm[8:16], axis=0, keepdims=True)

    for n in range(slots):
        for copy in tiles_in[n]:
            copy.wait()
        leaving.append(begin(tile.at[n], tile_ref.at[n], tile_sem.at[n]))

    get_mir.wait()
    get_local.wait()
    low = lax.broadcasted_iota(jnp.int32, (bins, lanes), 1) < lanes // 2
    per = cols // STEPS

    def mixed(n, carry):
        half, m, t = pair_place(n, mir.shape[1])
        a, b = mir[half, m, 0, t].astype(F32), mir[half, m, 1, t].astype(F32)
        even = jnp.where(low, a, pltpu.roll(b, lanes // 2, 1))
        odd = jnp.where(low, pltpu.roll(a, lanes // 2, 1), b)
        local[2 * n] = (local[2 * n].astype(F32) + even).astype(BF16)
        local[2 * n + 1] = (local[2 * n + 1].astype(F32) + odd).astype(BF16)
        return carry

    for i in range(STEPS):
        if i:
            pair_in[i].wait()
            leaving.append(begin(gp.at[bands[i]], out_ref.at[bands[i]], gp_out.at[i]))
        lax.fori_loop(i * per // 2, (i + 1) * per // 2, mixed, 0, unroll=2)
        part = pl.ds(i * per, per)
        leaving.append(begin(local.at[part], log_ref.at[part], log_sem.at[i]))
    for copy in leaving:
        copy.wait()


def finish(hidden, slot_of, back, mir, hl, sums, grad_pair):
    slots = slot_of.shape[0]
    chunks, _, feature, span = back.shape
    cols, bins, rows = hl.shape
    width = sums.shape[1]
    outs = [((slots, feature, chunks * span), BF16), (hl.shape, BF16), (grad_pair.shape, F32),
            ((feature, width), F32), ((width, hidden), F32), ((width, hidden), F32), ((hidden, width), F32),
            ((bins, width), F32), ((1, width), F32), ((1, width), F32)]
    dma = lambda n: pltpu.SemaphoreType.DMA((n,))
    return pl.pallas_call(
        functools.partial(finish_kernel, hidden),
        name="finish",
        in_specs=[smem()] + [hbm()] * 5,
        out_specs=[hbm()] * 3 + [vmem()] * 7,
        out_shape=[jax.ShapeDtypeStruct(shape, kind) for shape, kind in outs],
        scratch_shapes=[
            pltpu.VMEM(mir.shape, BF16),
            pltpu.VMEM(hl.shape, BF16),
            pltpu.VMEM(sums.shape, BF16),
            pltpu.VMEM(grad_pair.shape, F32),
            pltpu.VMEM((slots, feature, chunks * span), BF16),
            pltpu.SemaphoreType.DMA((slots, chunks)), dma(3), dma(STEPS), dma(STEPS), dma(slots), dma(STEPS),
        ],
        compiler_params=pltpu.CompilerParams(vmem_limit_bytes=14 * 1024 * 1024),
    )(slot_of, back, mir, hl, sums, grad_pair)


def per_device(pair, logit_cotangent, tiles, tile_target, tile_square, tile_count, w_template,
               transition_norm_gain, transition_norm_bias, w_gate, w_up, w_out, w_dist):
    row_devs = lax.axis_size("row")
    col_devs = lax.axis_size("col")
    rows, cols, width = pair.shape
    length = rows * row_devs
    slots, cells_sq, feature = tiles.shape
    hidden = w_gate.shape[1]
    tiles_t = jnp.transpose(tiles, (0, 2, 1))
    cot_t = jnp.transpose(logit_cotangent, (1, 2, 0))
    target = tile_target[:, 0]
    places = jnp.arange(slots, dtype=jnp.int32)
    rank = jnp.sum((target[:, None] == target[None, :]) & (places[None, :] < places[:, None]),
                   axis=1, dtype=jnp.int32)
    slot_of = target * CAP + rank
    chosen = slot_of[None, :] == jnp.arange(col_devs * CAP, dtype=jnp.int32)[:, None]
    label = places + 256 * (tile_square + 1) + 65536 * tile_count
    code = jnp.sum(jnp.where(chosen, label[None, :], 0), axis=1).reshape(col_devs, CAP)

    back, mir_heads, sums, gp, hl, _ = window(
        row_devs, col_devs, 1.0 / length, code, tiles_t, cot_t, pair, w_template,
        transition_norm_gain[None, :], transition_norm_bias[None, :], w_gate, w_up, w_out, w_dist.T)
    grad_tiles_t, logits_t, grad_pair, g_template, g_gate, g_up, g_out, g_dist_t, g_gain, g_bias = finish(
        hidden, slot_of, back.reshape(CHUNKS, col_devs * CAP, feature, SPAN), mir_heads, hl,
        sums.reshape(ROWS_SUM, width), gp)
    return (
        jnp.transpose(logits_t, (2, 0, 1)),
        grad_pair,
        jnp.transpose(grad_tiles_t, (0, 2, 1)),
        g_template,
        g_gain.reshape(width),
        g_bias.reshape(width),
        g_gate,
        g_up,
        g_out,
        g_dist_t.T,
    )


def solution(mesh):
    return jax.shard_map(
        per_device,
        mesh=mesh,
        in_specs=(
            P("row", "col", None),
            P("row", "col", None),
            P(("row", "col"), None, None),
            P(("row", "col"), None),
            P(("row", "col")),
            P(("row", "col")),
            P(), P(), P(), P(), P(), P(), P(),
        ),
        out_specs=(
            P("row", "col", None),
            P("row", "col", None),
            P(("row", "col"), None, None),
            P(), P(), P(), P(), P(), P(), P(),
        ),
        check_vma=False,
    )
```

```python
import functools

import jax
import jax.numpy as jnp
from jax import lax
from jax.experimental import pallas as pl
from jax.experimental.pallas import tpu as pltpu
from jax.sharding import PartitionSpec as P

SQ = 32
CAP = 2
MESH = pl.DeviceIdType.MESH
F32 = jnp.float32
BF16 = jnp.bfloat16
ROWS_SUM = 2048
VMEM_LIMIT = 60 * 1024 * 1024


def vmem():
    return pl.BlockSpec(memory_space=pltpu.VMEM)


def smem():
    return pl.BlockSpec(memory_space=pltpu.SMEM)


def hbm():
    return pl.BlockSpec(memory_space=pl.ANY)


def nn(a, b):
    return lax.dot_general(a, b, (((1,), (0,)), ((), ())), preferred_element_type=F32)


def nt(a, b):
    return lax.dot_general(a, b, (((1,), (1,)), ((), ())), preferred_element_type=F32)


def tn(a, b):
    return lax.dot_general(a, b, (((0,), (0,)), ((), ())), preferred_element_type=F32)


def displacements(col_devs):
    if col_devs != 16:
        return (1, col_devs), [(0, k) for k in range(1, col_devs)]
    order = [(0, 1), (1, 0), (0, 3), (3, 0), (1, 1), (3, 3), (1, 3), (3, 1),
             (0, 2), (2, 0), (1, 2), (2, 1), (3, 2), (2, 3), (2, 2)]
    return (4, 4), order


def moved(col, shape, step, sign):
    ys, zs = shape
    y = lax.rem(col // zs + sign * step[0] + ys, ys)
    z = lax.rem(lax.rem(col, zs) + sign * step[1] + zs, zs)
    return y * zs + z


class Place:
    def __init__(self, row_devs, col_devs):
        self.row, self.col = lax.axis_index("row"), lax.axis_index("col")
        self.xs, self.zs = row_devs // 2, col_devs // (row_devs // 2)
        self.x, self.k = self.row // 2, lax.rem(self.row, 2)
        self.y, self.z = self.col // self.zs, lax.rem(self.col, self.zs)

    def turn(self, value, by):
        return lax.rem(value + by, self.xs) if self.xs > 1 else value


class Mirror:
    def __init__(self, place, src, first, second, dst, sems):
        self.p, self.src, self.first, self.second, self.dst = place, src, first, second, dst
        self.s1, self.r1, self.s2, self.r2, self.s3, self.r3, self.own = sems

    def along_x(self, source, target, send, recv):
        p = self.p
        copies = []
        for n in range(1, p.xs):
            to = p.turn(p.x, n)
            copies.append(pltpu.make_async_remote_copy(
                src_ref=source(to), dst_ref=target.at[p.x], send_sem=send.at[n - 1], recv_sem=recv.at[n - 1],
                device_id=(2 * to + p.k, p.col), device_id_type=MESH))
        return copies

    def start_1(self):
        p = self.p
        self.copies = self.along_x(lambda to: self.src.at[:, to], self.first, self.s1, self.r1)
        for copy in self.copies:
            copy.start()
        self.local = pltpu.make_async_copy(self.src.at[:, p.x], self.first.at[p.x], self.own.at[0])
        self.local.start()

    def finish(self):
        self.local.wait()
        for copy in self.copies:
            copy.wait()

    finish_1 = finish_3 = finish

    def start_2(self):
        p = self.p
        self.plan = []
        for n in range(p.xs):
            to_y = p.turn(p.y, n)
            for h in (0, 1):
                to_z, to_k = 2 * p.k + h, p.z // 2
                source, target = self.first.at[to_y, h], self.second.at[p.y, lax.rem(p.z, 2)]
                slot = 2 * n + lax.rem(p.z, 2)
                remote = pltpu.make_async_remote_copy(
                    src_ref=source, dst_ref=target, send_sem=self.s2.at[2 * n + h], recv_sem=self.r2.at[slot],
                    device_id=(2 * p.x + to_k, to_y * p.zs + to_z), device_id_type=MESH)
                if n == 0:
                    here = jnp.logical_and(to_k == p.k, to_z == p.z)
                    local = pltpu.make_async_copy(source, target, self.r2.at[slot])
                    start_one(here, remote, local)
                    self.plan.append((here, remote))
                else:
                    remote.start()
                    self.plan.append((None, remote))

    def finish_2(self):
        for i, (here, remote) in enumerate(self.plan):
            if here is None:
                remote.wait_send()
            else:
                @pl.when(jnp.logical_not(here))
                def _():
                    remote.wait_send()
            ref = self.second.at[0, 0]
            pltpu.make_async_copy(ref, ref, self.r2.at[i]).wait()

    def start_3(self):
        p = self.p
        self.copies = self.along_x(lambda to: self.second.at[to], self.dst, self.s3, self.r3)
        for copy in self.copies:
            copy.start()
        self.local = pltpu.make_async_copy(self.second.at[p.x], self.dst.at[p.x], self.own.at[1])
        self.local.start()


def start_one(here, remote, local):
    @pl.when(jnp.logical_not(here))
    def _():
        remote.start()

    @pl.when(here)
    def _():
        local.start()


def mirror_sems(row_devs):
    xs = row_devs // 2
    dma = lambda n: pltpu.SemaphoreType.DMA((n,))
    return [dma(max(xs - 1, 1)), dma(max(xs - 1, 1)), dma(2 * xs), dma(2 * xs),
            dma(max(xs - 1, 1)), dma(max(xs - 1, 1)), dma(2)]


def greet(p, row_devs, col_devs):
    barrier = pltpu.get_barrier_semaphore()
    peers = 0
    for n in range(1, col_devs):
        pl.semaphore_signal(barrier, inc=1, device_id=(p.row, lax.rem(p.col + n, col_devs)), device_id_type=MESH)
        peers += 1
    for n in range(1, row_devs):
        pl.semaphore_signal(barrier, inc=1, device_id=(lax.rem(p.row + n, row_devs), p.col), device_id_type=MESH)
        peers += 1
    for n in range(1, col_devs):
        pl.semaphore_signal(
            barrier, inc=1, device_id=(2 * p.x + 1 - p.k, lax.rem(p.col + n, col_devs)), device_id_type=MESH)
        peers += 1
    return lambda: pl.semaphore_wait(barrier, peers)


BAND = 8
CHUNKS = SQ // BAND
SPAN = BAND * SQ
PART = 256
EARLY, MIDDLE = 7, 5


def share(count):
    inv = jnp.where(count == 1, 1.0, jnp.where(count == 2, 0.5, jnp.where(count == 3, 1.0 / 3.0, 0.25)))
    return jnp.where(count == 0, 0.0, inv).astype(F32)


def pair_place(n, xs):
    u, q, a = lax.rem(n, BAND // 2), lax.rem(n // (BAND // 2), CHUNKS), n // (BAND // 2 * CHUNKS)
    return q // 2, lax.rem(u, xs), (lax.rem(q, 2) * 2 + a) * (BAND // 2 // xs) + u // xs


def window_kernel(row_devs, col_devs, scale, code_ref, tiles_ref, cot_ref, pair_ref, wt_ref,
                  gain_ref, bias_ref, wg_ref, wu_ref, wo_ref, wd_ref,
                  back_ref, heads_ref, sum_ref, gp_ref, hl_ref, got_ref,
                  ids_ref, sendbuf, recv, names, onehot, s_ref, g_ref, pair_v, d_ref, z_ref, hs_ref,
                  pack, c_first, c_second, c_dst, h_first, h_second,
                  ag_ref, au_ref, ao_ref, ad_ref, at_ref, an_ref, acc_ref,
                  low, rs_recv, cs_send, cs_recv, piece, chunk,
                  pair_sem, out_sem, id_send, id_recv, t_send, t_recv, g_send, g_recv, own_t, own_g, own_sem,
                  a_send, a_recv, b_send, b_recv, e_send, e_recv, f_send, f_recv, *mirror_sem):
    p = Place(row_devs, col_devs)
    row, col = p.row, p.col
    shape, order = displacements(col_devs)
    rows, cols, width = pair_v.shape
    bins, feature, hidden = wd_ref.shape[0], wt_ref.shape[0], wg_ref.shape[1]
    sq_cols, sq_rows = cols // SQ, rows // SQ
    squares = sq_cols * sq_rows
    cells = BAND * cols
    greeted = greet(p, row_devs, col_devs)
    pair_in = pltpu.make_async_copy(pair_ref, pair_v, pair_sem.at[0])
    pair_in.start()

    lanes = rows
    left = lax.broadcasted_iota(jnp.int32, (bins, lanes), 1) < lanes // 2

    def pack_pair(n, carry):
        u, v = cot_ref[2 * n].astype(F32), cot_ref[2 * n + 1].astype(F32)
        half, m, t = pair_place(n, p.xs)
        pack[half, 0, m, t] = jnp.where(left, u, pltpu.roll(v, lanes // 2, 1)).astype(BF16)
        pack[half, 1, m, t] = jnp.where(left, pltpu.roll(u, lanes // 2, 1), v).astype(BF16)
        return carry

    def fill(parts, d, carry):
        for k in range(CAP):
            code = code_ref[d, k]
            at, inv = jnp.bitwise_and(code, 255), share(code // 65536)
            for q in parts:
                sendbuf[q, d, k] = (
                    tiles_ref[at, :, q * SPAN:(q + 1) * SPAN].astype(F32) * inv).astype(BF16)
        return carry

    lax.fori_loop(0, col_devs, functools.partial(fill, (0,)), 0)
    id_lane = lax.broadcasted_iota(jnp.int32, (8, 128), 1)
    for d in range(col_devs):
        ids_ref[d] = jnp.where(id_lane == 0, code_ref[d, 0], code_ref[d, 1])
    greeted()

    def to_all(source, target, send, recv_sem):
        copies = []
        for n, step in enumerate(order):
            to = moved(col, shape, step, 1)
            copies.append(pltpu.make_async_remote_copy(
                src_ref=source(to), dst_ref=target(n), send_sem=send(n), recv_sem=recv_sem(n),
                device_id=(row, to), device_id_type=MESH))
        return copies

    def local(source, target, sem):
        copy = pltpu.make_async_copy(source, target, sem)
        copy.start()
        return copy

    id_copies = to_all(lambda to: ids_ref.at[to], lambda n: got_ref.at[col],
                       lambda n: id_send.at[n], lambda n: id_recv.at[n])
    for copy in id_copies:
        copy.start()
    own_id = local(ids_ref.at[col], got_ref.at[col], own_sem.at[0])
    tile_copies = []
    for q in range(CHUNKS):
        tile_copies.append(to_all(lambda to: sendbuf.at[q, to], lambda n: recv.at[q, col],
                                  lambda n: t_send.at[q, n], lambda n: t_recv.at[q, n]))
    for copy in tile_copies[0]:
        copy.start()
    lax.fori_loop(0, cols // 2, pack_pair, 0)
    mirrors = [Mirror(p, pack.at[n], c_first.at[n], c_second.at[n], c_dst.at[n], mirror_sem[7 * n:7 * (n + 1)])
               for n in range(2)]
    mirrors[0].start_1()
    mirrors[1].start_1()
    lax.fori_loop(0, col_devs, functools.partial(fill, tuple(range(1, CHUNKS))), 0)
    own_tiles = [local(sendbuf.at[q, col], recv.at[q, col], own_t.at[q]) for q in range(CHUNKS)]
    for ref in (ag_ref, au_ref, ao_ref, ad_ref, at_ref, an_ref):
        ref[...] = jnp.zeros(ref.shape, F32)
    mirrors[0].finish_1()
    mirrors[0].start_2()
    for copy in tile_copies[1]:
        copy.start()

    def own_cot(j, carry):
        d_ref[pl.ds(j, rows, stride=cols), :] = cot_ref[j].astype(F32).T
        return carry

    lax.fori_loop(0, cols, own_cot, 0)
    own_id.wait()
    for copy in id_copies:
        copy.wait()
    local(got_ref, names, own_sem.at[1]).wait()

    def square(d, k):
        return jnp.bitwise_and(names[d, 0, k] // 256, 255) - 1

    one_rows = lax.broadcasted_iota(jnp.int32, (squares * feature, CAP * feature), 0)
    one_cols = lax.broadcasted_iota(jnp.int32, (squares * feature, CAP * feature), 1)
    same = lax.rem(one_rows, feature) == lax.rem(one_cols, feature)
    square_of = one_rows // feature
    for d in range(col_devs):
        wanted = jnp.where(one_cols < feature, square(d, 0), square(d, 1))
        onehot[:, d * CAP * feature:(d + 1) * CAP * feature] = jnp.where(
            jnp.logical_and(same, square_of == wanted), 1.0, 0.0).astype(BF16)
    mirrors[1].finish_1()
    mirrors[1].start_2()
    for copy in tile_copies[2] + tile_copies[3]:
        copy.start()
    mirrors[0].finish_2()
    mirrors[0].start_3()

    def mirrored(half, r, carry):
        parity, r = r // (cols // 4), lax.rem(r, cols // 4)
        n = r // BAND * (2 * BAND) + half * BAND + lax.rem(r, BAND)
        _, m, t = pair_place(n, p.xs)
        at = pl.multiple_of((parity * (cols // 2) + n) * rows, rows)
        d_ref[pl.ds(at, rows), :] += c_dst[half, m, parity, t].astype(F32).T
        return carry

    mirrors[0].finish_3()
    lax.fori_loop(0, cols // 2, functools.partial(mirrored, 0), 0)
    pair_in.wait()

    def band(q, a, carry):
        row0 = a * SQ + q * BAND
        w_t = wt_ref[...]
        pieces = [s_ref[a * sq_cols + d] for d in range(sq_cols)]
        proj = jnp.concatenate(
            [tn(one, w_t).reshape(BAND, SQ, width) for one in pieces], axis=1).reshape(cells, width)
        z1 = pair_v[pl.ds(row0, BAND)].reshape(cells, width) + proj
        gain, bias = gain_ref[...], bias_ref[...]
        mean = jnp.mean(z1, axis=1, keepdims=True)
        centered = z1 - mean
        rdev = lax.rsqrt(jnp.mean(centered * centered, axis=1, keepdims=True) + 1e-5)
        xhat = centered * rdev
        normed = (xhat * gain + bias).astype(BF16)
        base = pl.multiple_of(row0 * cols, cells)
        dheads = d_ref[pl.ds(base, cells), :].astype(BF16)
        wd = wd_ref[...]
        dz2 = nn(dheads, wd)
        dzl = dz2.astype(BF16)
        normed_t = normed.T
        dzl_t = dzl.T
        z2 = z1
        dnorm = jnp.zeros((cells, width), F32)
        for k in range(hidden // PART):
            span = slice(k * PART, (k + 1) * PART)
            gate = nn(normed, wg_ref[:, span])
            up = nn(normed, wu_ref[:, span])
            dhid = nt(dzl, wo_ref[span, :])
            s = 0.5 * jnp.tanh(0.5 * gate) + 0.5
            swish = gate * s
            hid = (swish * up).astype(BF16)
            dup = (dhid * swish).astype(BF16)
            dgate = (dhid * up * (s + swish * (1.0 - s))).astype(BF16)
            z2 = z2 + nn(hid, wo_ref[span, :])
            dnorm = dnorm + nt(dgate, wg_ref[:, span]) + nt(dup, wu_ref[:, span])
            ao_ref[:, span] += nn(dzl_t, hid)
            ag_ref[:, span] += nn(normed_t, dgate)
            au_ref[:, span] += nn(normed_t, dup)
        z_ref[pl.ds(base, cells), :] = z2
        z2_low = z2.astype(BF16)
        heads_t = nt(wd, z2_low).astype(BF16)
        pairs = BAND // 2
        deep = pairs // p.xs
        for u in range(pairs):
            t = (q % 2 * 2 + lax.rem(a, 2)) * deep + u // p.xs
            hs_ref[q // 2, a // 2, u % p.xs, t] = heads_t[:, u * 128:(u + 1) * 128]
        ad_ref[...] += tn(dheads, z2_low)
        an_ref[0] += jnp.sum((dnorm * xhat).reshape(cells // 8, 8, width), axis=0)
        an_ref[1] += jnp.sum(dnorm.reshape(cells // 8, 8, width), axis=0)
        dx = dnorm * gain
        grad = dz2 + (dx - jnp.mean(dx, axis=1, keepdims=True)
                      - xhat * jnp.mean(dx * xhat, axis=1, keepdims=True)) * rdev
        grad3 = grad.reshape(BAND, cols, width)
        pair_v[pl.ds(row0, BAND)] = grad3
        total = jnp.zeros((feature, width), F32)
        for d in range(sq_cols):
            dproj = grad3[:, d * SQ:(d + 1) * SQ, :].reshape(SPAN, width).astype(BF16)
            g_ref[a * sq_cols + d] = nt(w_t, dproj).astype(BF16)
            total = total + nn(pieces[d], dproj)
        at_ref[...] += total
        return carry

    back_copies, own_back, pair_out = [], [], []
    halves = [Mirror(p, hs_ref.at[n], h_first.at[n], h_second.at[n], heads_ref.at[n],
                     mirror_sem[7 * (n + 2):7 * (n + 3)]) for n in range(2)]
    for q in range(CHUNKS):
        if q == 2:
            mirrors[1].finish_3()
            lax.fori_loop(0, cols // 2, functools.partial(mirrored, 1), 0)
        own_tiles[q].wait()
        for copy in tile_copies[q]:
            copy.wait()
        s_ref[...] = nn(onehot[...], recv[q].reshape(col_devs * CAP * feature, SPAN)).astype(BF16).reshape(
            s_ref.shape)
        lax.fori_loop(0, sq_rows, functools.partial(band, q), 0)

        def take(d, carry):
            for k in range(CAP):
                sendbuf[q, d, k] = g_ref[jnp.maximum(square(d, k), 0)]
            return carry

        lax.fori_loop(0, col_devs, take, 0)
        for a in range(sq_rows):
            part_rows = pl.ds(a * SQ + q * BAND, BAND)
            pair_out.append(local(pair_v.at[part_rows], gp_ref.at[part_rows], out_sem.at[q * sq_rows + a]))
        if q == 0:
            mirrors[1].finish_2()
            mirrors[1].start_3()
        if q == 1:
            halves[0].start_1()
        if q == 2:
            halves[0].finish()
            halves[0].start_2()
        if q == 3:
            halves[1].start_1()
        back_copies.append(to_all(lambda to: sendbuf.at[q, to], lambda n: back_ref.at[q, col],
                                  lambda n: g_send.at[q, n], lambda n: g_recv.at[q, n]))
        own_back.append(local(sendbuf.at[q, col], back_ref.at[q, col], own_g.at[q]))
        if q < CHUNKS - 1:
            for copy in back_copies[q] if q < CHUNKS - 2 else back_copies[q][:EARLY]:
                copy.start()

    for k in range(hidden // width):
        span = slice(k * width, (k + 1) * width)
        acc_ref[k * width:(k + 1) * width, :] = ag_ref[:, span]
        acc_ref[hidden + k * width:hidden + (k + 1) * width, :] = au_ref[:, span]
        acc_ref[2 * hidden + k * width:2 * hidden + (k + 1) * width, :] = ao_ref[:, span].T
    tail = 3 * hidden
    acc_ref[tail:tail + bins, :] = ad_ref[...]
    tail += bins
    acc_ref[tail:tail + feature, :] = at_ref[...]
    tail += feature
    acc_ref[tail:tail + 8, :] = an_ref[0]
    acc_ref[tail + 8:tail + 16, :] = an_ref[1]
    acc_ref[tail + 16:, :] = jnp.zeros((ROWS_SUM - tail - 16, width), F32)
    low[...] = acc_ref[...].astype(BF16)
    rows_chunk = ROWS_SUM // row_devs

    def part(r):
        return pl.ds(pl.multiple_of(r * rows_chunk, rows_chunk), rows_chunk)

    first = []
    for k in range(1, row_devs):
        to = lax.rem(row + k, row_devs)
        first.append(pltpu.make_async_remote_copy(
            src_ref=low.at[part(to)], dst_ref=rs_recv.at[k - 1], send_sem=a_send.at[k - 1],
            recv_sem=a_recv.at[k - 1], device_id=(to, col), device_id_type=MESH))
    for copy in first:
        copy.start()
    held = back_copies[2][EARLY:] + back_copies[3]

    wd = wd_ref[...]

    def local_heads(j, carry):
        zj = z_ref[pl.ds(j, rows, stride=cols), :].astype(BF16)
        hl_ref[j] = nt(wd, zj).astype(BF16)
        return carry

    lax.fori_loop(0, cols, local_heads, 0)
    halves[1].finish_1()
    halves[1].start_2()
    for copy in first:
        copy.wait()
    total = acc_ref[part(row), :]
    for k in range(row_devs - 1):
        total = total + rs_recv[k].astype(F32)
    cs_send[...] = total.astype(BF16).reshape(cs_send.shape)
    second = to_all(lambda to: cs_send.at[to], lambda n: cs_recv.at[n],
                    lambda n: b_send.at[n], lambda n: b_recv.at[n])
    for copy in second:
        copy.start()
    for copy in held[:MIDDLE]:
        copy.start()
    halves[0].finish_2()
    halves[0].start_3()
    for copy in second:
        copy.wait()
    mine = cs_send[col].astype(F32)
    for k in range(col_devs - 1):
        mine = mine + cs_recv[k].astype(F32)
    piece[...] = (mine * scale).astype(BF16)
    chunk[col] = piece[...]
    gather = to_all(lambda to: piece, lambda n: chunk.at[col], lambda n: e_send.at[n], lambda n: e_recv.at[n])
    for copy in gather:
        copy.start()
    for copy in held[MIDDLE:]:
        copy.start()
    halves[1].finish_2()
    halves[1].start_3()
    for copy in gather:
        copy.wait()
    last = []
    for k in range(1, row_devs):
        last.append(pltpu.make_async_remote_copy(
            src_ref=chunk, dst_ref=sum_ref.at[row], send_sem=f_send.at[k - 1],
            recv_sem=f_recv.at[k - 1], device_id=(lax.rem(row + k, row_devs), col), device_id_type=MESH))
    for copy in last:
        copy.start()
    local(chunk, sum_ref.at[row], own_sem.at[2]).wait()
    for copy in pair_out:
        copy.wait()
    halves[0].finish_3()
    for copy in last:
        copy.wait()
    halves[1].finish_3()
    for q in range(CHUNKS):
        own_back[q].wait()
        for copy in back_copies[q]:
            copy.wait()


def window(row_devs, col_devs, scale, code, tiles_t, cot_t, pair, *weights):
    slots, feature, cells_sq = tiles_t.shape
    cols, bins, rows = cot_t.shape
    width = pair.shape[2]
    hidden = weights[3].shape[1]
    squares = rows // SQ * (cols // SQ)
    peers, xs = col_devs - 1, row_devs // 2
    rows_chunk = ROWS_SUM // row_devs
    rows_piece = rows_chunk // col_devs
    dma = lambda *n: pltpu.SemaphoreType.DMA(n)
    deep = cols // 4 // xs
    slices = (2, 2, xs, deep, bins, rows)
    heads = (2, xs, 2, deep, bins, rows)
    return pl.pallas_call(
        functools.partial(window_kernel, row_devs, col_devs, scale),
        name="window",
        out_shape=(
            jax.ShapeDtypeStruct((CHUNKS, col_devs, CAP, feature, SPAN), BF16),
            jax.ShapeDtypeStruct(heads, BF16),
            jax.ShapeDtypeStruct((row_devs, col_devs, rows_piece, 128), BF16),
            jax.ShapeDtypeStruct(pair.shape, F32),
            jax.ShapeDtypeStruct((cols, bins, rows), BF16),
            jax.ShapeDtypeStruct((col_devs, 8, 128), jnp.int32),
        ),
        in_specs=[smem(), vmem(), vmem(), hbm()] + [vmem()] * len(weights),
        out_specs=(hbm(), hbm(), hbm(), hbm(), vmem(), hbm()),
        scratch_shapes=[
            pltpu.VMEM((col_devs, 8, 128), jnp.int32),
            pltpu.VMEM((CHUNKS, col_devs, CAP, feature, SPAN), BF16),
            pltpu.VMEM((CHUNKS, col_devs, CAP, feature, SPAN), BF16),
            pltpu.SMEM((col_devs, 8, 128), jnp.int32),
            pltpu.VMEM((squares * feature, col_devs * CAP * feature), BF16),
            pltpu.VMEM((squares, feature, SPAN), BF16),
            pltpu.VMEM((squares, feature, SPAN), BF16),
            pltpu.VMEM((rows, cols, width), F32),
            pltpu.VMEM((rows * cols, bins), F32),
            pltpu.VMEM((rows * cols, width), F32),
            pltpu.VMEM(slices, BF16),
            pltpu.VMEM(slices, BF16),
            pltpu.VMEM(heads, BF16),
            pltpu.VMEM(heads, BF16),
            pltpu.VMEM(heads, BF16),
            pltpu.VMEM(heads, BF16),
            pltpu.VMEM(heads, BF16),
            pltpu.VMEM((width, hidden), F32),
            pltpu.VMEM((width, hidden), F32),
            pltpu.VMEM((width, hidden), F32),
            pltpu.VMEM((bins, width), F32),
            pltpu.VMEM((feature, width), F32),
            pltpu.VMEM((2, 8, width), F32),
            pltpu.VMEM((ROWS_SUM, 128), F32),
            pltpu.VMEM((ROWS_SUM, 128), BF16),
            pltpu.VMEM((row_devs - 1, rows_chunk, 128), BF16),
            pltpu.VMEM((col_devs, rows_piece, 128), BF16),
            pltpu.VMEM((col_devs - 1, rows_piece, 128), BF16),
            pltpu.VMEM((rows_piece, 128), BF16),
            pltpu.VMEM((col_devs, rows_piece, 128), BF16),
            dma(1), dma(rows // BAND), dma(peers), dma(peers),
            dma(CHUNKS, peers), dma(CHUNKS, peers), dma(CHUNKS, peers), dma(CHUNKS, peers),
            dma(CHUNKS), dma(CHUNKS), dma(3),
            dma(row_devs - 1), dma(row_devs - 1), dma(peers), dma(peers),
            dma(peers), dma(peers), dma(row_devs - 1), dma(row_devs - 1),
        ] + mirror_sems(row_devs) * 4,
        compiler_params=pltpu.CompilerParams(
            collective_id=0, has_side_effects=True, vmem_limit_bytes=VMEM_LIMIT),
    )(code, tiles_t, cot_t, pair, *weights)


STEPS = 2


def finish_kernel(hidden, slot_ref, *refs):
    each = slot_ref.shape[0] // STEPS
    backs, refs = refs[:each], refs[each:]
    (count_ref, mir_ref, hl_ref, sum_ref, gp_ref,
     tile_ref, log_ref, out_ref, gt_ref, gg_ref, gu_ref, go_ref, gd_ref, gn_ref, gb_ref) = refs
    step = pl.program_id(0)
    out_ref[...] = gp_ref[...]
    for n, back_ref in enumerate(backs):
        inv = share(count_ref[step * each + n])
        span = back_ref.shape[3]
        for q in range(back_ref.shape[0]):
            tile_ref[n, :, q * span:(q + 1) * span] = (back_ref[q, 0].astype(F32) * inv).astype(BF16)
    per, bins, lanes = hl_ref.shape
    low = lax.broadcasted_iota(jnp.int32, (bins, lanes), 1) < lanes // 2
    for k in range(per // 2):
        half, m, t = pair_place(step * (per // 2) + k, mir_ref.shape[1])
        a, b = mir_ref[half, m, 0, t].astype(F32), mir_ref[half, m, 1, t].astype(F32)
        even = jnp.where(low, a, pltpu.roll(b, lanes // 2, 1))
        odd = jnp.where(low, pltpu.roll(a, lanes // 2, 1), b)
        log_ref[2 * k] = (hl_ref[2 * k].astype(F32) + even).astype(BF16)
        log_ref[2 * k + 1] = (hl_ref[2 * k + 1].astype(F32) + odd).astype(BF16)

    @pl.when(step == 0)
    def _():
        width = sum_ref.shape[1]
        for k in range(hidden // width):
            span = slice(k * width, (k + 1) * width)
            gg_ref[:, span] = sum_ref[k * width:(k + 1) * width, :].astype(F32)
            gu_ref[:, span] = sum_ref[hidden + k * width:hidden + (k + 1) * width, :].astype(F32)
        go_ref[...] = sum_ref[2 * hidden:3 * hidden, :].astype(F32)
        at = 3 * hidden
        gd_ref[...] = sum_ref[at:at + gd_ref.shape[0], :].astype(F32)
        at += gd_ref.shape[0]
        gt_ref[...] = sum_ref[at:at + gt_ref.shape[0], :].astype(F32)
        at += gt_ref.shape[0]
        norm = sum_ref[at:at + 16, :].astype(F32)
        gn_ref[...] = jnp.sum(norm[0:8], axis=0, keepdims=True)
        gb_ref[...] = jnp.sum(norm[8:16], axis=0, keepdims=True)


def finish(hidden, slot_of, count, back, mir, hl, sums, grad_pair):
    slots = slot_of.shape[0]
    feature, cells = back.shape[2], back.shape[0] * back.shape[3]
    cols, bins, rows = hl.shape
    width = sums.shape[1]
    per, each = cols // STEPS, slots // STEPS
    const = lambda shape: pl.BlockSpec(shape, lambda i, s: (0,) * len(shape))
    outs = [((slots, feature, cells), BF16), ((cols, bins, rows), BF16), (grad_pair.shape, F32),
            ((feature, width), F32), ((width, hidden), F32), ((width, hidden), F32), ((hidden, width), F32),
            ((bins, width), F32), ((1, width), F32), ((1, width), F32)]
    held = lambda n: pl.BlockSpec(
        (back.shape[0], 1, feature, back.shape[3]), lambda i, s: (0, s[i * each + n], 0, 0))
    band = pl.BlockSpec((grad_pair.shape[0] // STEPS,) + grad_pair.shape[1:], lambda i, s: (i, 0, 0))
    return pl.pallas_call(
        functools.partial(finish_kernel, hidden),
        name="finish",
        grid_spec=pltpu.PrefetchScalarGridSpec(
            num_scalar_prefetch=1,
            grid=(STEPS,),
            in_specs=[held(n) for n in range(each)] + [
                pl.BlockSpec(memory_space=pltpu.SMEM),
                const(mir.shape),
                pl.BlockSpec((per, bins, rows), lambda i, s: (i, 0, 0)),
                const(sums.shape),
                band,
            ],
            out_specs=[
                pl.BlockSpec((each, feature, cells), lambda i, s: (i, 0, 0)),
                pl.BlockSpec((per, bins, rows), lambda i, s: (i, 0, 0)),
                band,
            ] + [const(shape) for shape, _ in outs[3:]],
        ),
        out_shape=[jax.ShapeDtypeStruct(shape, kind) for shape, kind in outs],
        compiler_params=pltpu.CompilerParams(
            dimension_semantics=("arbitrary",), vmem_limit_bytes=VMEM_LIMIT),
    )(slot_of, *([back] * each), count, mir, hl, sums, grad_pair)


def per_device(pair, logit_cotangent, tiles, tile_target, tile_square, tile_count, w_template,
               transition_norm_gain, transition_norm_bias, w_gate, w_up, w_out, w_dist):
    row_devs = lax.axis_size("row")
    col_devs = lax.axis_size("col")
    rows, cols, width = pair.shape
    length = rows * row_devs
    slots, cells_sq, feature = tiles.shape
    hidden = w_gate.shape[1]
    tiles_t = jnp.transpose(tiles, (0, 2, 1))
    cot_t = jnp.transpose(logit_cotangent, (1, 2, 0))
    target = tile_target[:, 0]
    places = jnp.arange(slots, dtype=jnp.int32)
    rank = jnp.sum((target[:, None] == target[None, :]) & (places[None, :] < places[:, None]),
                   axis=1, dtype=jnp.int32)
    slot_of = target * CAP + rank
    chosen = slot_of[None, :] == jnp.arange(col_devs * CAP, dtype=jnp.int32)[:, None]
    label = places + 256 * (tile_square + 1) + 65536 * tile_count
    code = jnp.sum(jnp.where(chosen, label[None, :], 0), axis=1).reshape(col_devs, CAP)

    back, mir_heads, sums, gp, hl, _ = window(
        row_devs, col_devs, 1.0 / length, code, tiles_t, cot_t, pair, w_template,
        transition_norm_gain[None, :], transition_norm_bias[None, :], w_gate, w_up, w_out, w_dist.T)
    grad_tiles_t, logits_t, grad_pair, g_template, g_gate, g_up, g_out, g_dist_t, g_gain, g_bias = finish(
        hidden, slot_of, tile_count, back.reshape(CHUNKS, col_devs * CAP, feature, SPAN), mir_heads, hl,
        sums.reshape(ROWS_SUM, width), gp)
    return (
        jnp.transpose(logits_t, (2, 0, 1)),
        grad_pair,
        jnp.transpose(grad_tiles_t, (0, 2, 1)),
        g_template,
        g_gain.reshape(width),
        g_bias.reshape(width),
        g_gate,
        g_up,
        g_out,
        g_dist_t.T,
    )


def solution(mesh):
    return jax.shard_map(
        per_device,
        mesh=mesh,
        in_specs=(
            P("row", "col", None),
            P("row", "col", None),
            P(("row", "col"), None, None),
            P(("row", "col"), None),
            P(("row", "col")),
            P(("row", "col")),
            P(), P(), P(), P(), P(), P(), P(),
        ),
        out_specs=(
            P("row", "col", None),
            P("row", "col", None),
            P(("row", "col"), None, None),
            P(), P(), P(), P(), P(), P(), P(),
        ),
        check_vma=False,
    )
```
